32 devices in a mesh: row: 8 (over z, x), col: 4 (over y, core).
Axes of the slice: x: 2, y: 2, z: 4, core: 2. Of those that a mesh axis runs over, the one named last changes fastest.
Arguments:
- patches: bfloat16 [16384, 1024], P('row', 'col'), may hold values from -16 to 16
- w_query: bfloat16 [1024, 1024], P('row', 'col'), may hold values from -0.1875 to 0.1875
- w_key: bfloat16 [1024, 1024], P('row', 'col'), may hold values from -0.1875 to 0.1875
- w_value: bfloat16 [1024, 1024], P('row', 'col'), may hold values from -0.1875 to 0.1875
- w_out: bfloat16 [1024, 1024], P('col', 'row'), may hold values from -2 to 2
- w_gate: bfloat16 [1024, 2816], P('row', 'col'), may hold values from -0.1875 to 0.1875
- w_up: bfloat16 [1024, 2816], P('row', 'col'), may hold values from -0.1875 to 0.1875
- w_down: bfloat16 [2816, 1024], P('col', 'row'), may hold values from -0.109375 to 0.109375
- gain_attn: bfloat16 [1024], P('row'), may hold values from 0.5 to 1.5
- gain_mlp: bfloat16 [1024], P('row'), may hold values from 0.5 to 1.5
- lengths: int32 [16], P('row'), may hold values from 256 to 1024, as said below
- cotangent: bfloat16 [16384, 1024], P('row', 'col'), may hold values from -6 to 6
Outputs:
- output: bfloat16 [16384, 1024], P('row', 'col')
- grad_patches: float32 [16384, 1024], P('row', 'col')
- grad_query: float32 [1024, 1024], P('row', 'col')
- grad_key: float32 [1024, 1024], P('row', 'col')
- grad_value: float32 [1024, 1024], P('row', 'col')
- grad_out: float32 [1024, 1024], P('col', 'row')
- grad_gate: float32 [1024, 2816], P('row', 'col')
- grad_up: float32 [1024, 2816], P('row', 'col')
- grad_down: float32 [2816, 1024], P('col', 'row')
- grad_gain_attn: float32 [1024], P('row')
- grad_gain_mlp: float32 [1024], P('row')
The draws below stay inside these ranges and needn't reach their ends.
Inputs may be any that keep to these rules, and one draw needn't show every extreme that they name: Each sequence's valid slots are its first lengths[s]; every draw has a sequence with all 1024 slots valid and one with 256.
All inputs are finite; a program needn't handle non-finite values.
Results may differ from the reference program's by a relative error of at most 0.012.
The reference program's roundings to bfloat16 on the way count: a program that leaves them out, or rounds other values in their place, can miss the bound.
Values may be sent and summed in bfloat16 or wider, within the bound.
No kernel may reach another device: no remote copies, remote signals or barrier semaphores. Data moves between devices by JAX's collectives and lax.ppermute only.
A program may use at most 192 MiB of HBM per device.

```python
import math
import jax
import jax.numpy as jnp
from jax import lax

D = 1024
HEADS = 16
HEAD_DIM = 64
FF = 2816
SEQ = 1024
SEQS = 16
TOKENS = 16384


def draw_lengths(key, part):
    first, second = jax.random.split(key)
    base = jax.random.randint(first, (SEQS,), SEQ // 4, SEQ + 1, dtype=jnp.int32)
    order = jax.random.permutation(second, SEQS)
    base = base.at[order[0]].set(SEQ)
    return base.at[order[1]].set(SEQ // 4)


def draw_patches(key, part):
    values_key = jax.random.fold_in(key, 11)
    scales_key = jax.random.fold_in(key, 12)
    normal_part = jax.random.truncated_normal(values_key, -6.0, 6.0, (TOKENS, D), jnp.float32)
    column_scale = jnp.exp(jax.random.uniform(scales_key, (D,), jnp.float32) * math.log(16.0)) / 6.0
    return (normal_part * column_scale[None, :]).astype(jnp.bfloat16)


def level_of(stream_key, dims, pieces, smallest, largest):
    factor_of, own = 1.0, jax.random.fold_in(stream_key, 6)
    for axis_at, parts in pieces:
        draws = jnp.exp(jax.random.uniform(jax.random.fold_in(own, axis_at), (parts,), jnp.float32, smallest / len(pieces), largest / len(pieces)))
        factor_of = factor_of * jnp.repeat(draws, dims[axis_at] // parts).reshape([-1 if axis == axis_at else 1 for axis in range(len(dims))])
    return factor_of


def centred(rng, extent, scale, bound, cuts=(), kind=jnp.bfloat16):
    values = scale * jax.random.normal(rng, extent, jnp.float32)
    if cuts:
        values = values * level_of(rng, extent, cuts, -0.22, 0.18)
    return jnp.clip(values, -bound, bound).astype(kind)


def setup_inputs(seed: int = 0) -> dict:
    streams_of = jax.random.split(jax.random.key(seed), 13)
    patches = draw_patches(jax.random.fold_in(streams_of[12], 71), 0)
    w_query = centred(streams_of[1], (D, D), D ** -0.5, 0.1875, ((0, 8), (1, 4)))
    w_key = centred(streams_of[2], (D, D), D ** -0.5, 0.1875, ((0, 8), (1, 4)))
    w_value = centred(streams_of[3], (D, D), D ** -0.5, 0.1875, ((0, 8), (1, 4)))
    w_out = centred(streams_of[4], (D, D), (D * 8 // SEQ) ** -0.5, 2.0, ((0, 4), (1, 8)))
    w_gate = centred(streams_of[5], (D, FF), D ** -0.5, 0.1875, ((0, 8), (1, 4)))
    w_up = centred(streams_of[6], (D, FF), D ** -0.5, 0.1875, ((0, 8), (1, 4)))
    w_down = centred(streams_of[7], (FF, D), FF ** -0.5, 0.109375, ((0, 4), (1, 8)))
    gain_attn = jnp.clip(1.0 + 0.1 * jax.random.normal(streams_of[8], (D,), jnp.float32), 0.5, 1.5).astype(jnp.bfloat16)
    gain_mlp = jnp.clip(1.0 + 0.1 * jax.random.normal(streams_of[9], (D,), jnp.float32), 0.5, 1.5).astype(jnp.bfloat16)
    lengths = draw_lengths(jax.random.fold_in(streams_of[12], 71), 0)
    cotangent = centred(streams_of[11], (TOKENS, D), 1.0, 6.0, ((0, 8), (1, 4)))
    return {"patches": patches, "w_query": w_query, "w_key": w_key, "w_value": w_value, "w_out": w_out, "w_gate": w_gate, "w_up": w_up, "w_down": w_down, "gain_attn": gain_attn, "gain_mlp": gain_mlp, "lengths": lengths, "cotangent": cotangent}


EPSILON = 1e-06
MASKED = -1000000000.0

@jax.custom_vjp
def low(v):
    return lax.optimization_barrier(v.astype(jnp.bfloat16)).astype(jnp.float32)

@jax.custom_vjp
def low_back(v):
    return v

def low_keep(v):
    return (low(v), None)

def low_pass(kept, grad):
    return (grad,)

def back_keep(v):
    return (v, None)

def back_low(kept, grad):
    return (low(grad),)
low.defvjp(low_keep, low_pass)
low_back.defvjp(back_keep, back_low)

def project(left, right):
    return jnp.einsum('gsd,de->gse', left, right, precision=lax.Precision.HIGHEST)

def layer(group_rows, group_lengths, w_query, w_key, w_value, w_out, w_gate, w_up, w_down, gain_attn, gain_mlp):
    groups = group_rows.shape[0]
    positions = jnp.arange(SEQ, dtype=jnp.int32)
    rstd_one = lax.rsqrt(lax.optimization_barrier(jnp.mean(group_rows * group_rows, axis=-1, keepdims=True)) + EPSILON)
    normed_one = low(group_rows * rstd_one * gain_attn)
    queries = low(low_back(project(normed_one, w_query)))
    keys_all = low(low_back(project(normed_one, w_key)))
    values_all = low(low_back(project(normed_one, w_value)))

    def heads_first(tensor):
        return jnp.transpose(tensor.reshape(groups, SEQ, HEADS, HEAD_DIM), (2, 0, 1, 3))
    causal = positions[None, :] <= positions[:, None]
    visible = causal[None, :, :] & (positions[None, None, :] < group_lengths[:, None, None])

    def per_head(operands):
        query_h, key_h, value_h = operands
        raw = jnp.einsum('gie,gje->gij', query_h, key_h, precision=lax.Precision.HIGHEST) * HEAD_DIM ** (-0.5)
        scores = low_back(jnp.where(visible, raw, MASKED))
        probs = jax.nn.softmax(scores, axis=-1)
        return jnp.einsum('gij,gje->gie', low(probs), value_h, precision=lax.Precision.HIGHEST)
    attended = lax.map(jax.checkpoint(per_head), (heads_first(queries), heads_first(keys_all), heads_first(values_all)))
    attended = jnp.transpose(attended, (1, 2, 0, 3)).reshape(groups, SEQ, D)
    attended = low(low_back(attended))
    hstate = group_rows + low_back(project(attended, w_out))
    rstd_two = lax.rsqrt(lax.optimization_barrier(jnp.mean(hstate * hstate, axis=-1, keepdims=True)) + EPSILON)
    normed_two = low(hstate * rstd_two * gain_mlp)
    gate = low_back(project(normed_two, w_gate))
    upward = low_back(project(normed_two, w_up))
    hidden = low(jax.nn.silu(gate) * upward)
    mixed = project(hidden, w_down)
    valid = (positions[None, :] < group_lengths[:, None])[:, :, None]
    return jnp.where(valid, hstate + low_back(mixed), 0.0)

def reference(patches, w_query, w_key, w_value, w_out, w_gate, w_up, w_down, gain_attn, gain_mlp, lengths, cotangent):
    group = math.gcd(SEQS, max(1, 4096 // SEQ))
    count = SEQS // group
    lengths_grouped = lengths.reshape(count, group)

    def forward(inputs, wq_f, wk_f, wv_f, wo_f, wg_f, wu_f, wd_f, ga_f, gm_f):
        stacked = inputs.reshape(count, group, SEQ, D)

        def scan_step(carry, item):
            rows_now, lengths_now = item
            result = jax.checkpoint(layer)(rows_now, lengths_now, wq_f, wk_f, wv_f, wo_f, wg_f, wu_f, wd_f, ga_f, gm_f)
            return (carry, result)
        unused, outputs = lax.scan(scan_step, jnp.zeros((), jnp.float32), (stacked, lengths_grouped))
        return outputs.reshape(TOKENS, D)
    floats = [a.astype(jnp.float32) for a in (patches, w_query, w_key, w_value, w_out, w_gate, w_up, w_down, gain_attn, gain_mlp)]
    result, pullback = jax.vjp(forward, floats[0], floats[1], floats[2], floats[3], floats[4], floats[5], floats[6], floats[7], floats[8], floats[9])
    grads = pullback(cotangent.astype(jnp.float32))
    return (result.astype(jnp.bfloat16), grads[0], grads[1], grads[2], grads[3], grads[4], grads[5], grads[6], grads[7], grads[8], grads[9])
```

```python
import functools

import jax
import jax.numpy as jnp
from jax import lax
from jax.experimental import pallas as pl
from jax.experimental.pallas import tpu as pltpu
from jax.sharding import PartitionSpec as P

HEAD_DIM = 64
PAIR = 2 * HEAD_DIM
EPSILON = 1e-06
MASKED = -1000000000.0
BF16 = jnp.bfloat16
F32 = jnp.float32
MIB = 1 << 20

NN = (((1,), (0,)), ((), ()))
NT = (((1,), (1,)), ((), ()))
TN = (((0,), (0,)), ((), ()))

ANY = pl.BlockSpec(memory_space=pl.ANY)
SCALARS = pl.BlockSpec(memory_space=pltpu.SMEM)


def mm(left, right, dims):
    return lax.dot_general(left, right, dims, preferred_element_type=F32)


def params(mib):
    return pltpu.CompilerParams(
        dimension_semantics=("arbitrary",), vmem_limit_bytes=mib * MIB
    )


def fetch_copies(me, buffers, first, scratch, sems):
    zs, rows, _ = buffers[0].shape
    out = []
    for at, buffer in enumerate(buffers):
        half, px = at // 2, at % 2
        for pz in range(zs):
            owner = ((me[0] ^ pz) * 2) + (me[1] ^ px)
            out.append(
                pltpu.make_async_copy(
                    buffer.at[pz, :, pl.ds(*first)],
                    scratch.at[half, pl.ds(owner * rows, rows), :],
                    sems.at[at, pz],
                )
            )
    return out


def emit_copies(me, staged, buffers, sems):
    zs, rows, _ = buffers[0].shape
    out = []
    for px, buffer in enumerate(buffers):
        for pz in range(zs):
            owner = ((me[0] ^ pz) * 2) + (me[1] ^ px)
            out.append(
                pltpu.make_async_copy(
                    staged.at[pl.ds(owner * rows, rows), :], buffer.at[pz], sems.at[px, pz]
                )
            )
    return out


def run(copies):
    for copy in copies:
        copy.start()
    for copy in copies:
        copy.wait()


def norm_in(x_ref, gain_ref, n_ref):
    x = x_ref[...].astype(F32)
    rstd = lax.rsqrt(jnp.mean(x * x, axis=1, keepdims=True) + EPSILON)
    n_ref[...] = (x * rstd * gain_ref[...].astype(F32)).astype(BF16)


def norm_first(x, gain):
    tokens, width = x.shape
    block = tokens // 4
    row = pl.BlockSpec((block, width), lambda i: (i, 0))
    return pl.pallas_call(
        norm_in,
        out_shape=jax.ShapeDtypeStruct((tokens, width), BF16),
        grid=(4,),
        in_specs=[row, pl.BlockSpec((1, width), lambda i: (0, 0))],
        out_specs=row,
        compiler_params=params(32),
        name="norm_first",
    )(x, gain)


def project_in(me_ref, n_ref, wa, wb, wc, wd, out_ref, w_scr, sems):
    @pl.when(pl.program_id(0) == 0)
    def _():
        run(fetch_copies(me_ref, (wa, wb, wc, wd), (0, w_scr.shape[2]), w_scr, sems))

    n = w_scr.shape[2]
    for half in range(2):
        out_ref[:, half * n : (half + 1) * n] = mm(n_ref[...], w_scr[half], NN).astype(BF16)


def project_qkv(me, normed, weights, columns):
    tokens, width = normed.shape
    block = tokens // 4
    zs = weights[0].shape[0]
    return pl.pallas_call(
        project_in,
        out_shape=jax.ShapeDtypeStruct((tokens, 2 * columns), BF16),
        grid=(4,),
        in_specs=[SCALARS, pl.BlockSpec((block, width), lambda i: (i, 0)), ANY, ANY, ANY, ANY],
        out_specs=pl.BlockSpec((block, 2 * columns), lambda i: (i, 0)),
        scratch_shapes=[
            pltpu.VMEM((2, width, columns), BF16),
            pltpu.SemaphoreType.DMA((4, zs)),
        ],
        compiler_params=params(32),
        name="project_qkv",
    )(me, normed, *weights)


def stack_heads(pair):
    lane = lax.broadcasted_iota(jnp.int32, pair.shape, 1)
    zero = jnp.zeros_like(pair)
    return jnp.concatenate(
        [jnp.where(lane < HEAD_DIM, pair, zero), jnp.where(lane < HEAD_DIM, zero, pair)], axis=0
    )


def masked_scores(length, key_rows, queries, first):
    raw = mm(key_rows, queries, NT)
    key_at = lax.broadcasted_iota(jnp.int32, raw.shape, 0)
    rows = raw.shape[1] // 2
    query_at = lax.broadcasted_iota(jnp.int32, raw.shape, 1)
    query_at = first + jnp.where(query_at >= rows, query_at - rows, query_at)
    return jnp.where((key_at <= query_at) & (key_at < length), raw, MASKED)


def attend_in(len_ref, q_ref, k_ref, v_ref, o_ref, lse_ref):
    tokens = q_ref.shape[0]
    rows = tokens // 4
    scale = HEAD_DIM ** (-0.5)
    length = len_ref[0]
    values_t = v_ref[...].T
    for at in range(4):
        first, last = at * rows, (at + 1) * rows
        queries = stack_heads(q_ref[first:last] * jnp.asarray(scale, BF16))
        scores = masked_scores(length, k_ref[:last], queries, first)
        peak = jnp.max(scores, axis=0, keepdims=True)
        expo = jnp.exp(scores - peak)
        denom = jnp.sum(expo, axis=0, keepdims=True)
        probs = (expo * (1.0 / denom)).astype(BF16)
        both = mm(values_t[:, :last], probs, NN)
        joined = jnp.concatenate([both[:HEAD_DIM, :rows], both[HEAD_DIM:, rows:]], axis=0)
        o_ref[first:last] = joined.T.astype(BF16)
        lse_ref[0, at : at + 1] = peak + jnp.log(denom)


def attend(length, qkv, heads):
    tokens = qkv.shape[0]
    pairs = heads // 2
    per = qkv.shape[1] // (6 * PAIR)

    def spec(which):
        return pl.BlockSpec(
            (tokens, PAIR), lambda i: (0, (i // per) * 3 * per + which * per + i % per)
        )

    return pl.pallas_call(
        attend_in,
        out_shape=(
            jax.ShapeDtypeStruct((tokens, pairs * PAIR), BF16),
            jax.ShapeDtypeStruct((pairs, 4, tokens // 2), F32),
        ),
        grid=(pairs,),
        in_specs=[SCALARS, spec(0), spec(1), spec(2)],
        out_specs=(
            pl.BlockSpec((tokens, PAIR), lambda i: (0, i)),
            pl.BlockSpec((1, 4, tokens // 2), lambda i: (i, 0, 0)),
        ),
        compiler_params=params(48),
        name="attend",
    )(length, qkv, qkv, qkv)


def project_out_in(me_ref, a_ref, wa, wb, wc, wd, out_ref, w_scr, sems):
    n = w_scr.shape[2]
    first = wa.shape[2] - n

    @pl.when(pl.program_id(0) == 0)
    def _():
        run(fetch_copies(me_ref, (wa, wb, wc, wd), (first, n), w_scr, sems))

    total = mm(a_ref[:, :n], w_scr[0], NT) + mm(a_ref[:, n:], w_scr[1], NT)
    out_ref[...] = total.astype(BF16)


def project_out(me, attended, weights):
    tokens, heads_wide = attended.shape
    zs, rows, _ = weights[0].shape
    width = zs * 2 * rows
    n = heads_wide // 2
    block = tokens // 4
    return pl.pallas_call(
        project_out_in,
        out_shape=jax.ShapeDtypeStruct((tokens, width), BF16),
        grid=(4,),
        in_specs=[SCALARS, pl.BlockSpec((block, 2 * n), lambda i: (i, 0)), ANY, ANY, ANY, ANY],
        out_specs=pl.BlockSpec((block, width), lambda i: (i, 0)),
        scratch_shapes=[pltpu.VMEM((2, width, n), BF16), pltpu.SemaphoreType.DMA((4, zs))],
        compiler_params=params(32),
        name="project_out",
    )(me, attended, *weights)


def norm_second_in(x_ref, own_ref, recv_ref, gain_ref, h_ref, n_ref):
    hidden = x_ref[...].astype(F32) + (own_ref[...].astype(F32) + recv_ref[...].astype(F32))
    h_ref[...] = hidden
    rstd = lax.rsqrt(jnp.mean(hidden * hidden, axis=1, keepdims=True) + EPSILON)
    n_ref[...] = (hidden * rstd * gain_ref[...].astype(F32)).astype(BF16)


def norm_second(x, own, recv, gain):
    tokens, width = x.shape
    row = pl.BlockSpec((tokens // 4, width), lambda i: (i, 0))
    return pl.pallas_call(
        norm_second_in,
        out_shape=(
            jax.ShapeDtypeStruct((tokens, width), F32),
            jax.ShapeDtypeStruct((tokens, width), BF16),
        ),
        grid=(4,),
        in_specs=[row, row, row, pl.BlockSpec((1, width), lambda i: (0, 0))],
        out_specs=(row, row),
        compiler_params=params(40),
        name="norm_second",
    )(x, own, recv, gain)


def mlp_in(first, me_ref, n_ref, m_ref, wa, wb, *refs):
    if first:
        mixed_ref, back_ref, g0, g1 = refs[:4]
        w_scr, grads, staged, sems, out_sems = refs[4:]
    else:
        mixed_acc, back_acc, mixed_ref, back_ref, g0, g1 = refs[:6]
        w_scr, grads, staged, sems, out_sems = refs[6:]
    step = pl.program_id(0)
    n = w_scr.shape[2] // 3

    @pl.when(step == 0)
    def _():
        run(fetch_copies(me_ref, (wa, wb), (0, 3 * n), w_scr, sems))

    normed, grad_mixed = n_ref[...], m_ref[...]
    parts = []
    for lo in range(0, n, 256):
        cut = slice(lo, lo + 256)
        gate = mm(normed, w_scr[0, :, lo : lo + 256], NN)
        up = mm(normed, w_scr[0, :, n + lo : n + lo + 256], NN)
        grad_hidden = mm(grad_mixed, w_scr[0, :, 2 * n + lo : 2 * n + lo + 256], NN)
        sig = 0.5 * jnp.tanh(0.5 * gate) + 0.5
        act = gate * sig
        hidden = (act * up).astype(BF16)
        grad_gate = (grad_hidden * up * (sig * (1.0 + gate * (1.0 - sig)))).astype(BF16)
        grad_up = (grad_hidden * act).astype(BF16)
        parts.append((grad_gate, grad_up, hidden))
    gate_all = jnp.concatenate([p[0] for p in parts], axis=1)
    up_all = jnp.concatenate([p[1] for p in parts], axis=1)
    hidden_all = jnp.concatenate([p[2] for p in parts], axis=1)
    mixed = mm(hidden_all, w_scr[0, :, 2 * n :], NT)
    back = mm(gate_all, w_scr[0, :, :n], NT) + mm(up_all, w_scr[0, :, n : 2 * n], NT)
    if not first:
        mixed = mixed + mixed_acc[...]
        back = back + back_acc[...]
    mixed_ref[...] = mixed.astype(mixed_ref.dtype)
    back_ref[...] = back.astype(back_ref.dtype)
    new = (
        mm(normed, gate_all, TN),
        mm(normed, up_all, TN),
        mm(grad_mixed, hidden_all, TN),
    )

    @pl.when(step == 0)
    def _():
        for at in range(3):
            grads[:, at * n : (at + 1) * n] = new[at]

    @pl.when(step == pl.num_programs(0) - 1)
    def _():
        for at in range(3):
            cut = slice(at * n, (at + 1) * n)
            staged[:, cut] = (grads[:, cut] + new[at]).astype(BF16)
        run(emit_copies(me_ref, staged, (g0, g1), out_sems))


def mlp(me, normed, grad_mixed, wa, wb, accs):
    tokens, width = normed.shape
    zs, rows, n3 = wa.shape
    block = tokens // 2
    row = pl.BlockSpec((block, width), lambda i: (i, 0))
    first = accs is None
    kind = F32 if first else BF16
    extra = [] if first else [row, row]
    return pl.pallas_call(
        functools.partial(mlp_in, first),
        out_shape=(
            jax.ShapeDtypeStruct((tokens, width), kind),
            jax.ShapeDtypeStruct((tokens, width), kind),
            jax.ShapeDtypeStruct((zs, rows, n3), BF16),
            jax.ShapeDtypeStruct((zs, rows, n3), BF16),
        ),
        grid=(2,),
        in_specs=[SCALARS, row, row, ANY, ANY] + extra,
        out_specs=(row, row, ANY, ANY),
        scratch_shapes=[
            pltpu.VMEM((1, width, n3), BF16),
            pltpu.VMEM((width, n3), F32),
            pltpu.VMEM((width, n3), BF16),
            pltpu.SemaphoreType.DMA((2, zs)),
            pltpu.SemaphoreType.DMA((2, zs)),
        ],
        compiler_params=params(60),
        name="mlp",
    )(me, normed, grad_mixed, wa, wb, *(() if first else accs))


def norm_second_back_in(
    h_ref, own_ref, recv_ref, gm_ref, gain_ref, gh_ref, gb_ref, gg_ref
):
    hidden = h_ref[...]
    width = hidden.shape[1]
    rstd = lax.rsqrt(jnp.mean(hidden * hidden, axis=1, keepdims=True) + EPSILON)
    grad = own_ref[...].astype(F32) + recv_ref[...].astype(F32)
    weighted = grad * gain_ref[...].astype(F32)
    stat = jnp.sum(weighted * hidden, axis=1, keepdims=True)
    grad_h = (
        gm_ref[...].astype(F32)
        + rstd * weighted
        - hidden * (rstd * rstd * rstd * stat / width)
    )
    gh_ref[...] = grad_h
    gb_ref[...] = grad_h.astype(BF16)
    piece = jnp.sum(grad * hidden * rstd, axis=0, keepdims=True)

    @pl.when(pl.program_id(0) == 0)
    def _():
        gg_ref[...] = jnp.zeros_like(gg_ref)

    gg_ref[...] += piece


def norm_second_back(hidden, own, recv, grad_mixed, gain):
    tokens, width = hidden.shape
    row = pl.BlockSpec((tokens // 4, width), lambda i: (i, 0))
    one = pl.BlockSpec((1, width), lambda i: (0, 0))
    return pl.pallas_call(
        norm_second_back_in,
        out_shape=(
            jax.ShapeDtypeStruct((tokens, width), F32),
            jax.ShapeDtypeStruct((tokens, width), BF16),
            jax.ShapeDtypeStruct((1, width), F32),
        ),
        grid=(4,),
        in_specs=[row, row, row, row, one],
        out_specs=(row, row, one),
        compiler_params=params(40),
        name="norm_second_back",
    )(hidden, own, recv, grad_mixed, gain)


def out_back_in(me_ref, gb_ref, a_ref, wa, wb, wc, wd, ga_ref, g0, g1, g2, g3, *scratch):
    w_scr, grads, staged, sems, out_sems = scratch
    n = w_scr.shape[2]
    first = wa.shape[2] - n
    step = pl.program_id(0)

    @pl.when(step == 0)
    def _():
        run(fetch_copies(me_ref, (wa, wb, wc, wd), (first, n), w_scr, sems))

    for half in range(2):
        ga_ref[:, half * n : (half + 1) * n] = mm(gb_ref[...], w_scr[half], NN).astype(BF16)
    new = mm(gb_ref[...], a_ref[...], TN)

    @pl.when(step == 0)
    def _():
        grads[...] = new

    @pl.when(step == pl.num_programs(0) - 1)
    def _():
        total = (grads[...] + new).astype(BF16)
        staged[0] = total[:, :n]
        staged[1] = total[:, n:]
        run(
            emit_copies(me_ref, staged.at[0], (g0, g1), out_sems.at[0])
            + emit_copies(me_ref, staged.at[1], (g2, g3), out_sems.at[1])
        )


def out_back(me, grad_branch, attended, weights):
    tokens, width = grad_branch.shape
    heads_wide = attended.shape[1]
    zs, rows, _ = weights[0].shape
    n = heads_wide // 2
    block = tokens // 2
    piece = jax.ShapeDtypeStruct((zs, rows, n), BF16)
    return pl.pallas_call(
        out_back_in,
        out_shape=(jax.ShapeDtypeStruct((tokens, heads_wide), BF16),) + (piece,) * 4,
        grid=(2,),
        in_specs=[
            SCALARS,
            pl.BlockSpec((block, width), lambda i: (i, 0)),
            pl.BlockSpec((block, heads_wide), lambda i: (i, 0)),
            ANY,
            ANY,
            ANY,
            ANY,
        ],
        out_specs=(pl.BlockSpec((block, heads_wide), lambda i: (i, 0)),) + (ANY,) * 4,
        scratch_shapes=[
            pltpu.VMEM((2, width, n), BF16),
            pltpu.VMEM((width, heads_wide), F32),
            pltpu.VMEM((2, width, n), BF16),
            pltpu.SemaphoreType.DMA((4, zs)),
            pltpu.SemaphoreType.DMA((2, 2, zs)),
        ],
        compiler_params=params(40),
        name="out_back",
    )(me, grad_branch, attended, *weights)


def attend_back_in(len_ref, q_ref, k_ref, v_ref, g_ref, lse_ref, gq_ref, gk_ref, gv_ref, *scratch):
    gk_acc, gv_acc = scratch
    tokens = q_ref.shape[0]
    rows = tokens // 4
    scale = HEAD_DIM ** (-0.5)
    length = len_ref[0]
    keys_t = k_ref[...].T
    gk_acc[...] = jnp.zeros_like(gk_acc)
    gv_acc[...] = jnp.zeros_like(gv_acc)
    for at in range(4):
        first, last = at * rows, (at + 1) * rows
        queries = stack_heads(q_ref[first:last] * jnp.asarray(scale, BF16))
        grads = stack_heads(g_ref[first:last])
        scores = masked_scores(length, k_ref[:last], queries, first)
        probs = jnp.exp(scores - lse_ref[0, at : at + 1])
        grad_probs = mm(v_ref[:last], grads, NT)
        inner = jnp.sum(probs * grad_probs, axis=0, keepdims=True)
        grad_scores = (probs * (grad_probs - inner)).astype(BF16)
        both = mm(keys_t[:, :last], grad_scores, NN)
        joined = jnp.concatenate([both[:HEAD_DIM, :rows], both[HEAD_DIM:, rows:]], axis=0)
        gq_ref[first:last] = (joined.T * scale).astype(BF16)
        gk_acc[:last] += mm(grad_scores, queries, NN)
        gv_acc[:last] += mm(probs.astype(BF16), grads, NN)
    gk_ref[...] = gk_acc[...].astype(BF16)
    gv_ref[...] = gv_acc[...].astype(BF16)


def attend_back(length, qkv, grad_attended, lse):
    tokens = qkv.shape[0]
    pairs = lse.shape[0]
    per = qkv.shape[1] // (6 * PAIR)

    def spec(which):
        return pl.BlockSpec(
            (tokens, PAIR), lambda i: (0, (i // per) * 3 * per + which * per + i % per)
        )

    own = pl.BlockSpec((tokens, PAIR), lambda i: (0, i))
    shape = jax.ShapeDtypeStruct((tokens, pairs * PAIR), BF16)
    return pl.pallas_call(
        attend_back_in,
        out_shape=(shape, shape, shape),
        grid=(pairs,),
        in_specs=[
            SCALARS,
            spec(0),
            spec(1),
            spec(2),
            own,
            pl.BlockSpec((1, 4, tokens // 2), lambda i: (i, 0, 0)),
        ],
        out_specs=(own, own, own),
        scratch_shapes=[pltpu.VMEM((tokens, PAIR), F32), pltpu.VMEM((tokens, PAIR), F32)],
        compiler_params=params(56),
        name="attend_back",
    )(length, qkv, qkv, qkv, grad_attended, lse)


def qkv_back_in(
    me_ref, gq_ref, gk_ref, gv_ref, n_ref, wa, wb, wc, wd, back_ref, g0, g1, g2, g3, *scratch
):
    w_scr, grads, staged, sems, out_sems = scratch
    columns = w_scr.shape[2]
    n = columns // 3
    step = pl.program_id(0)

    @pl.when(step == 0)
    def _():
        run(fetch_copies(me_ref, (wa, wb, wc, wd), (0, columns), w_scr, sems))

    total = None
    for half in range(2):
        cut = slice(half * n, (half + 1) * n)
        grad = jnp.concatenate([gq_ref[:, cut], gk_ref[:, cut], gv_ref[:, cut]], axis=1)
        piece = mm(grad, w_scr[half], NT)
        total = piece if total is None else total + piece
        new = mm(n_ref[...], grad, TN)

        @pl.when(step == 0)
        def _():
            grads[half] = new

        @pl.when(step == pl.num_programs(0) - 1)
        def _():
            staged[half] = (grads[half] + new).astype(BF16)

    back_ref[...] = total.astype(BF16)

    @pl.when(step == pl.num_programs(0) - 1)
    def _():
        run(
            emit_copies(me_ref, staged.at[0], (g0, g1), out_sems.at[0])
            + emit_copies(me_ref, staged.at[1], (g2, g3), out_sems.at[1])
        )


def qkv_back(me, grads, normed, weights, columns):
    tokens, width = normed.shape
    zs, rows, _ = weights[0].shape
    block = tokens // 2
    heads_wide = grads[0].shape[1]
    piece = jax.ShapeDtypeStruct((zs, rows, columns), BF16)
    grad_spec = pl.BlockSpec((block, heads_wide), lambda i: (i, 0))
    return pl.pallas_call(
        qkv_back_in,
        out_shape=(jax.ShapeDtypeStruct((tokens, width), BF16),) + (piece,) * 4,
        grid=(2,),
        in_specs=[
            SCALARS,
            grad_spec,
            grad_spec,
            grad_spec,
            pl.BlockSpec((block, width), lambda i: (i, 0)),
            ANY,
            ANY,
            ANY,
            ANY,
        ],
        out_specs=(pl.BlockSpec((block, width), lambda i: (i, 0)),) + (ANY,) * 4,
        scratch_shapes=[
            pltpu.VMEM((2, width, columns), BF16),
            pltpu.VMEM((2, width, columns), F32),
            pltpu.VMEM((2, width, columns), BF16),
            pltpu.SemaphoreType.DMA((4, zs)),
            pltpu.SemaphoreType.DMA((2, 2, zs)),
        ],
        compiler_params=params(48),
        name="qkv_back",
    )(me, *grads, normed, *weights)


def norm_first_back_in(x_ref, own_ref, recv_ref, gh_ref, gain_ref, gx_ref, gg_ref):
    x = x_ref[...].astype(F32)
    width = x.shape[1]
    rstd = lax.rsqrt(jnp.mean(x * x, axis=1, keepdims=True) + EPSILON)
    grad = own_ref[...].astype(F32) + recv_ref[...].astype(F32)
    weighted = grad * gain_ref[...].astype(F32)
    stat = jnp.sum(weighted * x, axis=1, keepdims=True)
    gx = gh_ref[...] + rstd * weighted - x * (rstd * rstd * rstd * stat / width)
    gx_ref[...] = gx.astype(BF16)

    @pl.when(pl.program_id(0) == 0)
    def _():
        gg_ref[...] = jnp.zeros_like(gg_ref)

    gg_ref[...] += jnp.sum(grad * x * rstd, axis=0, keepdims=True)


def norm_first_back(x, own, recv, grad_h, gain):
    tokens, width = x.shape
    row = pl.BlockSpec((tokens // 2, width), lambda i: (i, 0))
    one = pl.BlockSpec((1, width), lambda i: (0, 0))
    return pl.pallas_call(
        norm_first_back_in,
        out_shape=(
            jax.ShapeDtypeStruct((tokens, width), BF16),
            jax.ShapeDtypeStruct((1, width), F32),
        ),
        grid=(2,),
        in_specs=[row, row, row, row, one],
        out_specs=(row, one),
        compiler_params=params(40),
        name="norm_first_back",
    )(x, own, recv, grad_h, gain)


def shards(
    patches,
    w_query,
    w_key,
    w_value,
    w_out,
    w_gate,
    w_up,
    w_down,
    gain_attn,
    gain_mlp,
    lengths,
    cotangent,
):
    slab = patches.shape[1]
    rows_axis, cols_axis = lax.axis_size("row"), lax.axis_size("col")
    width = slab * cols_axis
    micro = lengths.shape[0]
    seq = patches.shape[0] // micro
    zs = rows_axis // 2
    row, col = lax.axis_index("row"), lax.axis_index("col")
    z, x, y, c = row // 2, row % 2, col // 2, col % 2
    me = jnp.stack([z, x, y, c]).astype(jnp.int32)
    heads_here = w_query.shape[1]
    columns = 3 * heads_here

    def swap(value, axis, bit):
        size = lax.axis_size(axis)
        return lax.ppermute(value, axis, [(i, i ^ bit) for i in range(size)])

    def gather(shard):
        near = jnp.stack([shard] + [swap(shard, "row", 2 * k) for k in range(1, zs)])
        beside = swap(near, "row", 1)
        across = swap(near, "col", 2)
        return near, beside, across, swap(across, "row", 1)

    def reduce_back(g00, g01, g10, g11):
        far = swap(g11, "row", 1)
        side = swap(g01, "row", 1)
        over = swap((g10.astype(F32) + far.astype(F32)).astype(BF16), "col", 2)

        def part(k):
            return g00[k].astype(F32) + (side[k].astype(F32) + over[k].astype(F32))

        total = part(0)
        for k in range(1, zs):
            total = total + swap(part(k).astype(BF16), "row", 2 * k).astype(F32)
        return total

    def pick(flag, one, other):
        return jnp.where(flag == 0, one, other)

    def spread(value):
        both = value.reshape(micro, seq, slab)
        mine = lax.dynamic_index_in_dim(both, y, 0, keepdims=False)
        theirs = lax.dynamic_index_in_dim(both, 1 - y, 0, keepdims=False)
        theirs = swap(theirs, "col", 2)
        pair = jnp.stack([mine, theirs])
        other = swap(pair, "col", 1)
        blocks = [
            pick(
                y ^ yy,
                pick(c ^ cc, pair[0], other[0]),
                pick(c ^ cc, pair[1], other[1]),
            )
            for yy in range(2)
            for cc in range(2)
        ]
        return jnp.concatenate(blocks, axis=1)

    def unspread(value):
        half = seq // 2
        quad = value.reshape(half, 2, 2, slab)
        stay = pick(c, quad[:, :, 0], quad[:, :, 1])
        leave = pick(c, quad[:, :, 1], quad[:, :, 0])
        come = swap(leave, "col", 1)
        whole = jnp.concatenate([pick(c, stay, come), pick(c, come, stay)], axis=0)
        keep = pick(y, whole[:, 0], whole[:, 1])
        send = pick(y, whole[:, 1], whole[:, 0])
        got = swap(send, "col", 2)
        return jnp.concatenate([pick(y, keep, got), pick(y, got, keep)], axis=0)

    inner = w_gate.shape[1]
    padded = -(-inner // 256) * 256
    pad = ((0, 0), (0, padded - inner))
    attn_shard = jnp.concatenate([w_query, w_key, w_value, w_out.T], axis=1)
    mlp_shard = jnp.concatenate(
        [jnp.pad(w_gate, pad), jnp.pad(w_up, pad), jnp.pad(w_down.T, pad)], axis=1
    )
    gains = lax.all_gather(jnp.stack([gain_attn, gain_mlp]), "row", axis=1, tiled=True)
    attn_gain, mlp_gain = gains[0:1], gains[1:2]

    x_all = spread(patches)
    attn_w = gather(attn_shard)
    mlp_w = gather(mlp_shard)

    length = lax.dynamic_slice_in_dim(lengths, y, 1)
    grad_mixed = spread(cotangent)
    grad_mixed = jnp.where(
        lax.iota(jnp.int32, seq)[:, None] < length, grad_mixed, jnp.zeros((), BF16)
    )

    normed_one = norm_first(x_all, attn_gain)
    qkv = project_qkv(me, normed_one, attn_w, columns)
    attended, lse = attend(length, qkv, 2 * heads_here // HEAD_DIM)
    branch = project_out(me, attended, attn_w)
    hidden, normed_two = norm_second(x_all, branch, swap(branch, "col", 1), mlp_gain)

    first = mlp(me, normed_two, grad_mixed, mlp_w[0], mlp_w[1], None)
    second = mlp(me, normed_two, grad_mixed, mlp_w[2], mlp_w[3], first[:2])
    mixed, back_two = second[:2]
    grad_h, grad_branch, mlp_gain_grad = norm_second_back(
        hidden, back_two, swap(back_two, "col", 1), grad_mixed, mlp_gain
    )
    mlp_grad = reduce_back(first[2], first[3], second[2], second[3])

    half = seq // 2

    def own_half(value):
        return lax.dynamic_slice_in_dim(value, c * half, half)

    def other_half(value):
        return lax.dynamic_slice_in_dim(value, (1 - c) * half, half)

    total = own_half(hidden) + (
        own_half(mixed).astype(F32) + swap(other_half(mixed), "col", 1).astype(F32)
    )
    valid = (lax.iota(jnp.int32, half) + c * half)[:, None] < length
    output = unspread(jnp.where(valid, total, 0.0).astype(BF16))

    back = out_back(me, grad_branch, attended, attn_w)
    out_grad = reduce_back(*back[1:])
    grads = attend_back(length, qkv, back[0], lse)
    back_one, *pieces = qkv_back(me, grads, normed_one, attn_w, columns)
    qkv_grad = reduce_back(*pieces)
    grad_x, attn_gain_grad = norm_first_back(
        own_half(x_all), own_half(back_one), swap(other_half(back_one), "col", 1),
        own_half(grad_h), attn_gain,
    )
    grad_patches = unspread(grad_x).astype(F32)

    gain_grads = lax.psum(
        jnp.concatenate([attn_gain_grad, 0.5 * mlp_gain_grad], axis=0), ("row", "col")
    )
    own_rows = width // rows_axis
    gain_grads = lax.dynamic_slice_in_dim(gain_grads, row * own_rows, own_rows, axis=1)

    return (
        output,
        grad_patches,
        qkv_grad[:, :heads_here],
        qkv_grad[:, heads_here : 2 * heads_here],
        qkv_grad[:, 2 * heads_here :],
        out_grad.T,
        mlp_grad[:, :inner],
        mlp_grad[:, padded : padded + inner],
        mlp_grad[:, 2 * padded : 2 * padded + inner].T,
        gain_grads[0],
        gain_grads[1],
    )


def solution(mesh):
    placed = (
        P("row", "col"),
        P("row", "col"),
        P("row", "col"),
        P("row", "col"),
        P("col", "row"),
        P("row", "col"),
        P("row", "col"),
        P("col", "row"),
        P("row"),
        P("row"),
        P("row"),
        P("row", "col"),
    )
    return jax.shard_map(
        shards,
        mesh=mesh,
        in_specs=placed,
        out_specs=(
            P("row", "col"),
            P("row", "col"),
            P("row", "col"),
            P("row", "col"),
            P("row", "col"),
            P("col", "row"),
            P("row", "col"),
            P("row", "col"),
            P("col", "row"),
            P("row"),
            P("row"),
        ),
        check_vma=False,
    )
```

```python
import functools

import jax
import jax.numpy as jnp
from jax import lax
from jax.experimental import pallas as pl
from jax.experimental.pallas import tpu as pltpu
from jax.sharding import PartitionSpec as P

HEAD_DIM = 64
PAIR = 2 * HEAD_DIM
EPSILON = 1e-06
MASKED = -1000000000.0
BF16 = jnp.bfloat16
F32 = jnp.float32
MIB = 1 << 20

NN = (((1,), (0,)), ((), ()))
NT = (((1,), (1,)), ((), ()))
TN = (((0,), (0,)), ((), ()))

ANY = pl.BlockSpec(memory_space=pltpu.HBM)
SCALARS = pl.BlockSpec(memory_space=pltpu.SMEM)


def mm(left, right, dims):
    return lax.dot_general(left, right, dims, preferred_element_type=F32)


def work(micros, values=0):
    return pl.CostEstimate(
        flops=int(micros * 1.15e9), transcendentals=0, bytes_accessed=int(micros * 1e6) + values
    )


def params(mib):
    return pltpu.CompilerParams(
        dimension_semantics=("arbitrary",), vmem_limit_bytes=mib * MIB
    )


def z_order(zs):
    order, bit = [0], zs // 2
    while bit:
        order += [at ^ bit for at in order]
        bit //= 2
    return order


def plan_planes(zs):
    order, half = z_order(zs), zs // 2
    return [
        [(py, px, pz) for pz in order[lo : lo + half]]
        for py in range(2)
        for px in range(2)
        for lo in (0, half)
    ]


def plan_lines(zs):
    order, half = z_order(zs), zs // 2
    return [
        [(py, px, pz) for pz in order[lo : lo + half] for py in range(2)]
        for px in range(2)
        for lo in (0, half)
    ]


def plan_back_planes(zs):
    return [[(py, px, pz) for pz in z_order(zs)] for py in range(2) for px in range(2)]


def plan_back_lines(zs):
    order, half = z_order(zs), zs // 2
    return [
        [(py, px, pz) for pz in order[lo : lo + half] for px in range(2) for py in range(2)]
        for lo in (0, half)
    ]


def block_copies(me, plan, buffers, parts, scratch_of, sems, out):
    rows = buffers[0].shape[1]
    copies = []
    for blocks, buffer in zip(plan, buffers, strict=True):
        for at_block, (py, px, pz) in enumerate(blocks):
            owner = ((me[0] ^ pz) * 2) + (me[1] ^ px)
            for at, (first, n) in enumerate(parts):
                remote = buffer.at[at_block, :, pl.ds(first, n)]
                local = scratch_of(at, py, pl.ds(owner * rows, rows))
                ends = (local, remote) if out else (remote, local)
                copies.append(pltpu.make_async_copy(*ends, sems.at[py, px, pz, at]))
    return copies


def fetch_copies(me, plan, buffers, parts, scratch_of, sems):
    return block_copies(me, plan, buffers, parts, scratch_of, sems, False)


def emit_copies(me, plan, buffers, parts, scratch_of, sems):
    return block_copies(me, plan, buffers, parts, scratch_of, sems, True)


def copy_sems(zs, parts):
    return pltpu.SemaphoreType.DMA((2, 2, zs, parts))


def run(copies):
    for copy in copies:
        copy.start()
    for copy in copies:
        copy.wait()


def norm_in(x_ref, gain_ref, n_ref):
    x = x_ref[...].astype(F32)
    rstd = lax.rsqrt(jnp.mean(x * x, axis=1, keepdims=True) + EPSILON)
    n_ref[...] = (x * rstd * gain_ref[...].astype(F32)).astype(BF16)


def norm_first(x, gain):
    tokens, width = x.shape
    block = tokens // 4
    row = pl.BlockSpec((block, width), lambda i: (i, 0))
    return pl.pallas_call(
        norm_in,
        out_shape=jax.ShapeDtypeStruct((tokens, width), BF16),
        grid=(4,),
        in_specs=[row, pl.BlockSpec((1, width), lambda i: (0, 0))],
        out_specs=row,
        compiler_params=params(32),
        cost_estimate=work(1),
        name="norm_first",
    )(x, gain)


def by_half(scratch):
    return lambda at, half, rows: scratch.at[half, rows, :]


def by_part(scratch):
    n = scratch.shape[2] // 2
    return lambda at, half, rows: scratch.at[at, rows, pl.ds(half * n, n)]


def project_in(plan, me_ref, n_ref, *refs):
    weights, (out_ref, w_scr, sems) = refs[:8], refs[8:]
    n = w_scr.shape[2]

    @pl.when(pl.program_id(0) == 0)
    def _():
        run(fetch_copies(me_ref, plan, weights, [(0, n)], by_half(w_scr), sems))

    for half in range(2):
        out_ref[:, half * n : (half + 1) * n] = mm(n_ref[...], w_scr[half], NN).astype(BF16)


def project_qkv(me, normed, weights, columns):
    tokens, width = normed.shape
    block = tokens // 4
    zs = 2 * weights[0].shape[0]
    return pl.pallas_call(
        functools.partial(project_in, plan_planes(zs)),
        out_shape=jax.ShapeDtypeStruct((tokens, 2 * columns), BF16),
        grid=(4,),
        in_specs=[SCALARS, pl.BlockSpec((block, width), lambda i: (i, 0))] + [ANY] * 8,
        out_specs=pl.BlockSpec((block, 2 * columns), lambda i: (i, 0)),
        scratch_shapes=[pltpu.VMEM((2, width, columns), BF16), copy_sems(zs, 1)],
        compiler_params=params(32),
        cost_estimate=work(6),
        name="project_qkv",
    )(me, normed, *weights)


def stack_heads(pair):
    lane = lax.broadcasted_iota(jnp.int32, pair.shape, 1)
    zero = jnp.zeros_like(pair)
    return jnp.concatenate(
        [jnp.where(lane < HEAD_DIM, pair, zero), jnp.where(lane < HEAD_DIM, zero, pair)], axis=0
    )


def masked_scores(length, key_rows, queries, first):
    raw = mm(key_rows, queries, NT)
    key_at = lax.broadcasted_iota(jnp.int32, raw.shape, 0)
    rows = raw.shape[1] // 2
    query_at = lax.broadcasted_iota(jnp.int32, raw.shape, 1)
    query_at = first + jnp.where(query_at >= rows, query_at - rows, query_at)
    return jnp.where((key_at <= query_at) & (key_at < length), raw, MASKED)


def attend_in(len_ref, q_ref, k_ref, v_ref, o_ref, lse_ref):
    tokens = q_ref.shape[0]
    rows = tokens // 4
    scale = HEAD_DIM ** (-0.5)
    length = len_ref[0]
    values_t = v_ref[...].T
    for at in range(4):
        first, last = at * rows, (at + 1) * rows
        queries = stack_heads(q_ref[first:last] * jnp.asarray(scale, BF16))
        scores = masked_scores(length, k_ref[:last], queries, first)
        peak = jnp.max(scores, axis=0, keepdims=True)
        expo = jnp.exp(scores - peak)
        denom = jnp.sum(expo, axis=0, keepdims=True)
        probs = (expo * (1.0 / denom)).astype(BF16)
        both = mm(values_t[:, :last], probs, NN)
        joined = jnp.concatenate([both[:HEAD_DIM, :rows], both[HEAD_DIM:, rows:]], axis=0)
        o_ref[first:last] = joined.T.astype(BF16)
        lse_ref[0, at : at + 1] = peak + jnp.log(denom)


def attend(length, qkv, heads):
    tokens = qkv.shape[0]
    pairs = heads // 2
    per = qkv.shape[1] // (6 * PAIR)

    def spec(which):
        return pl.BlockSpec(
            (tokens, PAIR), lambda i: (0, (i // per) * 3 * per + which * per + i % per)
        )

    return pl.pallas_call(
        attend_in,
        out_shape=(
            jax.ShapeDtypeStruct((tokens, pairs * PAIR), BF16),
            jax.ShapeDtypeStruct((pairs, 4, tokens // 2), F32),
        ),
        grid=(pairs,),
        in_specs=[SCALARS, spec(0), spec(1), spec(2)],
        out_specs=(
            pl.BlockSpec((tokens, PAIR), lambda i: (0, i)),
            pl.BlockSpec((1, 4, tokens // 2), lambda i: (i, 0, 0)),
        ),
        compiler_params=params(48),
        cost_estimate=work(13),
        name="attend",
    )(length, qkv, qkv, qkv)


def halves(block, width):
    return (
        pl.BlockSpec((block, width), lambda i: (jnp.minimum(i, 1), 0)),
        pl.BlockSpec((block, width), lambda i: (jnp.maximum(i - 2, 0), 0)),
    )


def to_halves(first, second, value):
    @pl.when(pl.program_id(0) < 2)
    def _():
        first[...] = value

    @pl.when(pl.program_id(0) >= 2)
    def _():
        second[...] = value


def of_halves(first, second):
    return jnp.where(pl.program_id(0) < 2, first[...].astype(F32), second[...].astype(F32))


def project_out_in(plan, me_ref, a_ref, *refs):
    weights, (out0, out1, w_scr, sems) = refs[:8], refs[8:]
    n = w_scr.shape[2]
    first = weights[0].shape[2] - n

    @pl.when(pl.program_id(0) == 0)
    def _():
        run(fetch_copies(me_ref, plan, weights, [(first, n)], by_half(w_scr), sems))

    total = mm(a_ref[:, :n], w_scr[0], NT) + mm(a_ref[:, n:], w_scr[1], NT)
    to_halves(out0, out1, total.astype(BF16))


def project_out(me, attended, weights):
    tokens, heads_wide = attended.shape
    half_zs, rows, _ = weights[0].shape
    zs = 2 * half_zs
    width = zs * 2 * rows
    n = heads_wide // 2
    block = tokens // 4
    return pl.pallas_call(
        functools.partial(project_out_in, plan_planes(zs)),
        out_shape=(jax.ShapeDtypeStruct((tokens // 2, width), BF16),) * 2,
        grid=(4,),
        in_specs=[SCALARS, pl.BlockSpec((block, 2 * n), lambda i: (i, 0))] + [ANY] * 8,
        out_specs=halves(block, width),
        scratch_shapes=[pltpu.VMEM((2, width, n), BF16), copy_sems(2 * half_zs, 1)],
        compiler_params=params(32),
        cost_estimate=work(5),
        name="project_out",
    )(me, attended, *weights)


def norm_second_in(x_ref, own0, own1, recv0, recv1, gain_ref, h_ref, n_ref):
    hidden = x_ref[...].astype(F32) + (of_halves(own0, own1) + of_halves(recv0, recv1))
    h_ref[...] = hidden
    rstd = lax.rsqrt(jnp.mean(hidden * hidden, axis=1, keepdims=True) + EPSILON)
    n_ref[...] = (hidden * rstd * gain_ref[...].astype(F32)).astype(BF16)


def norm_second(x, own, recv, gain):
    tokens, width = x.shape
    row = pl.BlockSpec((tokens // 4, width), lambda i: (i, 0))
    pair = halves(tokens // 4, width)
    return pl.pallas_call(
        norm_second_in,
        out_shape=(
            jax.ShapeDtypeStruct((tokens, width), F32),
            jax.ShapeDtypeStruct((tokens, width), BF16),
        ),
        grid=(4,),
        in_specs=[row, *pair, *pair, pl.BlockSpec((1, width), lambda i: (0, 0))],
        out_specs=(row, row),
        compiler_params=params(40),
        cost_estimate=work(4),
        name="norm_second",
    )(x, *own, *recv, gain)


def mlp_in(plan, back_plan, me_ref, n_ref, m_ref, *refs):
    count, back_count = len(plan), len(back_plan)
    weights, act_ref = refs[:count], refs[count]
    outs = refs[count + 1 : count + 1 + back_count]
    w_scr, grads, staged, sems, out_sems = refs[count + 1 + back_count :]
    step = pl.program_id(0)
    n = w_scr.shape[2]
    parts = [(at * n // 2, n // 2) for at in range(3)]

    @pl.when(step == 0)
    def _():
        run(fetch_copies(me_ref, plan, weights, parts, by_part(w_scr), sems))

    normed, grad_mixed = n_ref[...], m_ref[...]
    for lo in range(0, n, 256):
        cut = slice(lo, lo + 256)
        gate = mm(normed, w_scr[0, :, cut], NN)
        up = mm(normed, w_scr[1, :, cut], NN)
        grad_hidden = mm(grad_mixed, w_scr[2, :, cut], NN)
        sig = 0.5 * jnp.tanh(0.5 * gate) + 0.5
        act = gate * sig
        act_ref[2, :, cut] = (act * up).astype(BF16)
        act_ref[0, :, cut] = (grad_hidden * up * (sig * (1.0 + gate * (1.0 - sig)))).astype(BF16)
        act_ref[1, :, cut] = (grad_hidden * act).astype(BF16)
    for part in range(3):
        new = mm(normed if part < 2 else grad_mixed, act_ref[part], TN)

        @pl.when(step == 0)
        def _():
            grads[part] = new

        @pl.when(step == pl.num_programs(0) - 1)
        def _():
            staged[part] = (grads[part] + new).astype(BF16)

    @pl.when(step == pl.num_programs(0) - 1)
    def _():
        run(emit_copies(me_ref, back_plan, outs, parts, by_part(staged), out_sems))


def mlp(me, normed, grad_mixed, weights, zs, plan, back_plan):
    tokens, width = normed.shape
    _, rows, n3 = weights[0].shape
    n = 2 * n3 // 3
    block = tokens // 2
    row = pl.BlockSpec((block, width), lambda i: (i, 0))
    pieces = tuple(jax.ShapeDtypeStruct((len(p), rows, n3), BF16) for p in back_plan)
    return pl.pallas_call(
        functools.partial(mlp_in, plan, back_plan),
        out_shape=(jax.ShapeDtypeStruct((3, tokens, n), BF16),) + pieces,
        grid=(2,),
        in_specs=[SCALARS, row, row] + [ANY] * len(plan),
        out_specs=(pl.BlockSpec((3, block, n), lambda i: (0, i, 0)),) + (ANY,) * len(pieces),
        scratch_shapes=[
            pltpu.VMEM((3, width, n), BF16),
            pltpu.VMEM((3, width, n), F32),
            pltpu.VMEM((3, width, n), BF16),
            copy_sems(zs, 3),
            copy_sems(zs, 3),
        ],
        compiler_params=params(60),
        cost_estimate=work(26),
        name="mlp",
    )(me, normed, grad_mixed, *weights)


def mlp_back_in(plans, me_ref, a0, a1, *refs):
    first = len(plans[0])
    count = first + len(plans[1])
    out0, out1, scr0, scr1, sems0, sems1 = refs[count:]
    n = scr0.shape[2]
    parts = [(at * n // 2, n // 2) for at in range(2)]

    @pl.when(pl.program_id(0) == 0)
    def _():
        run(
            fetch_copies(me_ref, plans[0], refs[:first], parts, by_part(scr0), sems0)
            + fetch_copies(me_ref, plans[1], refs[first:count], parts, by_part(scr1), sems1)
        )

    total = mm(a0[0], scr0[0], NT) + mm(a0[1], scr0[1], NT)
    total = total + mm(a1[0], scr1[0], NT) + mm(a1[1], scr1[1], NT)
    to_halves(out0, out1, total.astype(BF16))


def mlp_back(me, acts, weights, zs, plans):
    _, tokens, n = acts[0].shape
    _, rows, n3 = weights[0][0].shape
    width = zs * 2 * rows
    count = len(plans[0]) + len(plans[1])
    block = tokens // 4
    act = pl.BlockSpec((2, block, n), lambda i: (0, i, 0))
    return pl.pallas_call(
        functools.partial(mlp_back_in, plans),
        out_shape=(jax.ShapeDtypeStruct((tokens // 2, width), BF16),) * 2,
        grid=(4,),
        in_specs=[SCALARS, act, act] + [ANY] * count,
        out_specs=halves(block, width),
        scratch_shapes=[
            pltpu.VMEM((2, width, n), BF16),
            pltpu.VMEM((2, width, n), BF16),
            copy_sems(zs, 2),
            copy_sems(zs, 2),
        ],
        compiler_params=params(48),
        cost_estimate=work(12),
        name="mlp_back",
    )(me, *acts, *weights[0], *weights[1])


def mlp_out_in(plans, me_ref, a0, a1, *refs):
    first = len(plans[0])
    count = first + len(plans[1])
    own_ref, other_ref, scr0, scr1, sems0, sems1 = refs[count:]
    n = scr0.shape[2]
    parts = [(n, n // 2)]
    step = pl.program_id(0)

    @pl.when(step == 0)
    def _():
        run(
            fetch_copies(me_ref, plans[0], refs[:first], parts, by_part(scr0), sems0)
            + fetch_copies(me_ref, plans[1], refs[first:count], parts, by_part(scr1), sems1)
        )

    total = (mm(a0[0], scr0[0], NT) + mm(a1[0], scr1[0], NT)).astype(BF16)

    @pl.when(step == 0)
    def _():
        other_ref[...] = total

    @pl.when(step == 1)
    def _():
        own_ref[...] = total


def mlp_out(me, acts, weights, zs, plans):
    _, tokens, n = acts[0].shape
    _, rows, n3 = weights[0][0].shape
    width = zs * 2 * rows
    count = len(plans[0]) + len(plans[1])
    half = tokens // 2
    act = pl.BlockSpec((1, half, n), lambda i, m: (2, m[3] ^ 1 ^ i, 0))
    out = pl.BlockSpec((half, width), lambda i, m: (0, 0))
    shape = jax.ShapeDtypeStruct((half, width), BF16)
    return pl.pallas_call(
        functools.partial(mlp_out_in, plans),
        out_shape=(shape, shape),
        grid_spec=pltpu.PrefetchScalarGridSpec(
            num_scalar_prefetch=1,
            grid=(2,),
            in_specs=[act, act] + [ANY] * count,
            out_specs=(out, out),
            scratch_shapes=[
                pltpu.VMEM((1, width, n), BF16),
                pltpu.VMEM((1, width, n), BF16),
                copy_sems(zs, 1),
                copy_sems(zs, 1),
            ],
        ),
        compiler_params=params(48),
        cost_estimate=work(8),
        name="mlp_out",
    )(me, *acts, *weights[0], *weights[1])


def scatter_lanes(me, value, full, stay_ref, leave_ref):
    slab = stay_ref.shape[2]
    full[...] = value
    for py in range(2):
        for ref, pc in ((stay_ref, 0), (leave_ref, 1)):
            at = (me[2] ^ py) * 2 + (me[3] ^ pc)
            ref[py] = full[:, pl.ds(pl.multiple_of(at * slab, slab), slab)]


def finish_in(me_ref, len_ref, h_ref, own_ref, recv_ref, stay_ref, leave_ref, full):
    total = h_ref[...] + (own_ref[...].astype(F32) + recv_ref[...].astype(F32))
    tokens = total.shape[0]
    at = lax.broadcasted_iota(jnp.int32, total.shape, 0) + me_ref[3] * tokens
    total = jnp.where(at < len_ref[0], total, 0.0)
    scatter_lanes(me_ref, total.astype(BF16), full, stay_ref, leave_ref)


def finish(me, length, hidden, own, recv, slab):
    half, width = own.shape
    part = pl.BlockSpec((2, half, slab), lambda i, m, n: (0, 0, 0))
    mine = pl.BlockSpec((half, width), lambda i, m, n: (m[3], 0))
    row = pl.BlockSpec((half, width), lambda i, m, n: (0, 0))
    shape = jax.ShapeDtypeStruct((2, half, slab), BF16)
    return pl.pallas_call(
        finish_in,
        out_shape=(shape, shape),
        grid_spec=pltpu.PrefetchScalarGridSpec(
            num_scalar_prefetch=2,
            grid=(1,),
            in_specs=[mine, row, row],
            out_specs=(part, part),
            scratch_shapes=[pltpu.VMEM((half, width), BF16)],
        ),
        compiler_params=params(40),
        cost_estimate=work(3),
        name="finish",
    )(me, length, hidden, own, recv)


def norm_second_back_in(
    h_ref, own0, own1, recv0, recv1, gm_ref, gain_ref, gh_ref, gb_ref, gg_ref
):
    hidden = h_ref[...]
    width = hidden.shape[1]
    rstd = lax.rsqrt(jnp.mean(hidden * hidden, axis=1, keepdims=True) + EPSILON)
    grad = of_halves(own0, own1) + of_halves(recv0, recv1)
    weighted = grad * gain_ref[...].astype(F32)
    stat = jnp.sum(weighted * hidden, axis=1, keepdims=True)
    grad_h = (
        gm_ref[...].astype(F32)
        + rstd * weighted
        - hidden * (rstd * rstd * rstd * stat / width)
    )
    gh_ref[...] = grad_h
    gb_ref[...] = grad_h.astype(BF16)
    piece = jnp.sum(grad * hidden * rstd, axis=0, keepdims=True)

    @pl.when(pl.program_id(0) == 0)
    def _():
        gg_ref[...] = jnp.zeros_like(gg_ref)

    gg_ref[...] += piece


def norm_second_back(hidden, own, recv, grad_mixed, gain):
    tokens, width = hidden.shape
    row = pl.BlockSpec((tokens // 4, width), lambda i: (i, 0))
    one = pl.BlockSpec((1, width), lambda i: (0, 0))
    pair = halves(tokens // 4, width)
    return pl.pallas_call(
        norm_second_back_in,
        out_shape=(
            jax.ShapeDtypeStruct((tokens, width), F32),
            jax.ShapeDtypeStruct((tokens, width), BF16),
            jax.ShapeDtypeStruct((1, width), F32),
        ),
        grid=(4,),
        in_specs=[row, *pair, *pair, row, one],
        out_specs=(row, row, one),
        compiler_params=params(40),
        cost_estimate=work(5),
        name="norm_second_back",
    )(hidden, *own, *recv, grad_mixed, gain)


def out_back_in(plan, back_plan, me_ref, gb_ref, a_ref, *refs):
    weights, ga_ref, outs = refs[:8], refs[8], refs[9:11]
    w_scr, grads, staged, sems, out_sems = refs[11:]
    n = w_scr.shape[2]
    first = weights[0].shape[2] - n
    step = pl.program_id(0)

    @pl.when(step == 0)
    def _():
        run(fetch_copies(me_ref, plan, weights, [(first, n)], by_half(w_scr), sems))

    for half in range(2):
        ga_ref[:, half * n : (half + 1) * n] = mm(gb_ref[...], w_scr[half], NN).astype(BF16)
    new = mm(gb_ref[...], a_ref[...], TN)

    @pl.when(step == 0)
    def _():
        grads[...] = new

    @pl.when(step == pl.num_programs(0) - 1)
    def _():
        total = (grads[...] + new).astype(BF16)
        staged[0] = total[:, :n]
        staged[1] = total[:, n:]
        run(emit_copies(me_ref, back_plan, outs, [(0, n)], by_half(staged), out_sems))


def out_back(me, grad_branch, attended, weights):
    tokens, width = grad_branch.shape
    heads_wide = attended.shape[1]
    half_zs, rows, _ = weights[0].shape
    zs = 2 * half_zs
    n = heads_wide // 2
    block = tokens // 2
    piece = jax.ShapeDtypeStruct((2 * zs, rows, n), BF16)
    return pl.pallas_call(
        functools.partial(out_back_in, plan_planes(zs), plan_back_lines(zs)),
        out_shape=(jax.ShapeDtypeStruct((tokens, heads_wide), BF16),) + (piece,) * 2,
        grid=(2,),
        in_specs=[
            SCALARS,
            pl.BlockSpec((block, width), lambda i: (i, 0)),
            pl.BlockSpec((block, heads_wide), lambda i: (i, 0)),
        ]
        + [ANY] * 8,
        out_specs=(pl.BlockSpec((block, heads_wide), lambda i: (i, 0)),) + (ANY,) * 2,
        scratch_shapes=[
            pltpu.VMEM((2, width, n), BF16),
            pltpu.VMEM((width, heads_wide), F32),
            pltpu.VMEM((2, width, n), BF16),
            copy_sems(zs, 1),
            copy_sems(zs, 1),
        ],
        compiler_params=params(40),
        cost_estimate=work(7),
        name="out_back",
    )(me, grad_branch, attended, *weights)


def attend_back_in(len_ref, q_ref, k_ref, v_ref, g_ref, lse_ref, gq_ref, gk_ref, gv_ref, *scratch):
    gk_acc, gv_acc = scratch
    tokens = q_ref.shape[0]
    rows = tokens // 4
    scale = HEAD_DIM ** (-0.5)
    length = len_ref[0]
    keys_t = k_ref[...].T
    gk_acc[...] = jnp.zeros_like(gk_acc)
    gv_acc[...] = jnp.zeros_like(gv_acc)
    for at in range(4):
        first, last = at * rows, (at + 1) * rows
        queries = stack_heads(q_ref[first:last] * jnp.asarray(scale, BF16))
        grads = stack_heads(g_ref[first:last])
        scores = masked_scores(length, k_ref[:last], queries, first)
        probs = jnp.exp(scores - lse_ref[0, at : at + 1])
        grad_probs = mm(v_ref[:last], grads, NT)
        inner = jnp.sum(probs * grad_probs, axis=0, keepdims=True)
        grad_scores = (probs * (grad_probs - inner)).astype(BF16)
        both = mm(keys_t[:, :last], grad_scores, NN)
        joined = jnp.concatenate([both[:HEAD_DIM, :rows], both[HEAD_DIM:, rows:]], axis=0)
        gq_ref[first:last] = (joined.T * scale).astype(BF16)
        gk_acc[:last] += mm(grad_scores, queries, NN)
        gv_acc[:last] += mm(probs.astype(BF16), grads, NN)
    gk_ref[...] = gk_acc[...].astype(BF16)
    gv_ref[...] = gv_acc[...].astype(BF16)


def attend_back(length, qkv, grad_attended, lse, half):
    tokens = qkv.shape[0]
    per = lse.shape[0] // 2

    def spec(which):
        return pl.BlockSpec((tokens, PAIR), lambda i: (0, half * 3 * per + which * per + i))

    out = pl.BlockSpec((tokens, PAIR), lambda i: (0, i))
    shape = jax.ShapeDtypeStruct((tokens, per * PAIR), BF16)
    return pl.pallas_call(
        attend_back_in,
        out_shape=(shape, shape, shape),
        grid=(per,),
        in_specs=[
            SCALARS,
            spec(0),
            spec(1),
            spec(2),
            pl.BlockSpec((tokens, PAIR), lambda i: (0, half * per + i)),
            pl.BlockSpec((1, 4, tokens // 2), lambda i: (half * per + i, 0, 0)),
        ],
        out_specs=(out, out, out),
        scratch_shapes=[pltpu.VMEM((tokens, PAIR), F32), pltpu.VMEM((tokens, PAIR), F32)],
        compiler_params=params(56),
        cost_estimate=work(11),
        name="attend_back",
    )(length, qkv, qkv, qkv, grad_attended, lse)


def qkv_back_in(plan, back_plan, me_ref, gq_ref, gk_ref, gv_ref, n_ref, *refs):
    weights, refs = refs[: len(plan)], refs[len(plan) :]
    if len(refs) == 8:
        acc_ref, (back_ref, *outs), scratch = None, refs[:3], refs[3:]
    else:
        acc_ref, (own_ref, other_ref, *outs), scratch = refs[0], refs[1:5], refs[5:]
    w_scr, grads, staged, sems, out_sems = scratch
    columns = w_scr.shape[1]
    step = pl.program_id(0)

    def place(at, half, rows):
        return w_scr.at[rows, :]

    @pl.when(step == 0)
    def _():
        run(fetch_copies(me_ref, plan, weights, [(0, columns)], place, sems))

    grad = jnp.concatenate([gq_ref[...], gk_ref[...], gv_ref[...]], axis=1)
    total = mm(grad, w_scr[...], NT)
    new = mm(n_ref[...], grad, TN)

    @pl.when(step == 0)
    def _():
        grads[...] = new

    if acc_ref is None:
        back_ref[...] = total
    else:
        total = (total + acc_ref[...]).astype(BF16)

        @pl.when(step == 0)
        def _():
            other_ref[...] = total

        @pl.when(step == 1)
        def _():
            own_ref[...] = total

    @pl.when(step == 1)
    def _():
        staged[...] = (grads[...] + new).astype(BF16)
        run(
            emit_copies(
                me_ref, back_plan, outs, [(0, columns)],
                lambda at, half, rows: staged.at[rows, :], out_sems,
            )
        )


def qkv_back(me, grads, normed, weights, columns, acc, half):
    tokens, width = normed.shape
    half_zs, rows, _ = weights[0].shape
    zs = 2 * half_zs
    block = tokens // 2
    n = grads[0].shape[1]
    plan = [p for p in plan_planes(zs) if p[0][0] == half]
    back_plan = [p for p in plan_back_planes(zs) if p[0][0] == half]
    weights = weights[len(plan) * half : len(plan) * (half + 1)]
    piece = jax.ShapeDtypeStruct((zs, rows, columns), BF16)
    grad_spec = pl.BlockSpec((block, n), lambda i, m: (m[3] ^ 1 ^ i, 0))
    row = pl.BlockSpec((block, width), lambda i, m: (m[3] ^ 1 ^ i, 0))
    if acc is None:
        extra, backs = [], ((jax.ShapeDtypeStruct((tokens, width), F32), row),)
    else:
        out = pl.BlockSpec((block, width), lambda i, m: (0, 0))
        extra, backs = [row], ((jax.ShapeDtypeStruct((block, width), BF16), out),) * 2
    return pl.pallas_call(
        functools.partial(qkv_back_in, plan, back_plan),
        out_shape=tuple(b[0] for b in backs) + (piece,) * 2,
        grid_spec=pltpu.PrefetchScalarGridSpec(
            num_scalar_prefetch=1,
            grid=(2,),
            in_specs=[grad_spec, grad_spec, grad_spec, row] + [ANY] * len(plan) + extra,
            out_specs=tuple(b[1] for b in backs) + (ANY,) * 2,
            scratch_shapes=[
                pltpu.VMEM((width, columns), BF16),
                pltpu.VMEM((width, columns), F32),
                pltpu.VMEM((width, columns), BF16),
                copy_sems(zs, 1),
                copy_sems(zs, 1),
            ],
        ),
        compiler_params=params(48),
        cost_estimate=work(9),
        name="qkv_back",
    )(me, *grads, normed, *weights, *(() if acc is None else (acc,)))


def norm_first_back_in(
    me_ref, x_ref, own_ref, recv_ref, gh_ref, gain_ref, stay_ref, leave_ref, gg_ref, full
):
    x = x_ref[...].astype(F32)
    width = x.shape[1]
    rstd = lax.rsqrt(jnp.mean(x * x, axis=1, keepdims=True) + EPSILON)
    grad = own_ref[...].astype(F32) + recv_ref[...].astype(F32)
    weighted = grad * gain_ref[...].astype(F32)
    stat = jnp.sum(weighted * x, axis=1, keepdims=True)
    gx = gh_ref[...] + rstd * weighted - x * (rstd * rstd * rstd * stat / width)
    gg_ref[...] = jnp.sum(grad * x * rstd, axis=0, keepdims=True)
    scatter_lanes(me_ref, gx.astype(BF16), full, stay_ref, leave_ref)


def norm_first_back(me, x, own, recv, grad_h, gain, slab):
    half, width = own.shape
    part = pl.BlockSpec((2, half, slab), lambda i, m: (0, 0, 0))
    mine = pl.BlockSpec((half, width), lambda i, m: (m[3], 0))
    row = pl.BlockSpec((half, width), lambda i, m: (0, 0))
    one = pl.BlockSpec((1, width), lambda i, m: (0, 0))
    shape = jax.ShapeDtypeStruct((2, half, slab), BF16)
    return pl.pallas_call(
        norm_first_back_in,
        out_shape=(shape, shape, jax.ShapeDtypeStruct((1, width), F32)),
        grid_spec=pltpu.PrefetchScalarGridSpec(
            num_scalar_prefetch=1,
            grid=(1,),
            in_specs=[mine, row, row, mine, one],
            out_specs=(part, part, one),
            scratch_shapes=[pltpu.VMEM((half, width), BF16)],
        ),
        compiler_params=params(40),
        cost_estimate=work(4),
        name="norm_first_back",
    )(me, x, own, recv, grad_h, gain)


def shards(
    patches,
    w_query,
    w_key,
    w_value,
    w_out,
    w_gate,
    w_up,
    w_down,
    gain_attn,
    gain_mlp,
    lengths,
    cotangent,
):
    slab = patches.shape[1]
    rows_axis, cols_axis = lax.axis_size("row"), lax.axis_size("col")
    width = slab * cols_axis
    micro = lengths.shape[0]
    seq = patches.shape[0] // micro
    zs = rows_axis // 2
    row, col = lax.axis_index("row"), lax.axis_index("col")
    z, x, y, c = row // 2, row % 2, col // 2, col % 2
    me = jnp.stack([z, x, y, c]).astype(jnp.int32)
    heads_here = w_query.shape[1]
    columns = 3 * heads_here

    def swap(value, axis, bit):
        size = lax.axis_size(axis)
        return lax.ppermute(value, axis, [(i, i ^ bit) for i in range(size)])

    sent = {"x": [], "y": [], "z": [], "c": []}
    depth = {"x": 2, "y": 2, "z": 2, "c": 2}
    bits = {"x": ("row", 1), "y": ("col", 2), "c": ("col", 1)}

    def send(value, link, bit=None):
        axis, one = bits.get(link, ("row", bit))
        queue = sent[link]
        if len(queue) >= depth[link]:
            value = lax.optimization_barrier((value, queue[-depth[link]]))[0]
        out = swap(value, axis, one)
        queue.append(out)
        return out

    def gather_z(shard, *done):
        near, bit = shard[None], zs // 2
        while bit > 1:
            near = jnp.concatenate([near, tie(send(near, "z", 2 * bit), *done)])
            bit //= 2
        return near, send(near, "z", 2)

    def gather_lines(both, come):
        near, bit = jnp.concatenate([both, come]), zs // 4
        while bit > 1:
            near = jnp.concatenate([near, send(near, "z", 2 * bit)])
            bit //= 2
        return near, send(near, "z", 2)

    def tie(value, *done):
        return lax.optimization_barrier((value, *done))[0]

    def order_rows(both):
        owned = [0]
        for bit in [1] + [2 * (zs >> k) for k in range(1, zs.bit_length())]:
            owned += [at ^ bit for at in owned]
        ordered = [jnp.zeros_like(both[0])] * rows_axis
        for at, rel in enumerate(owned):
            ordered = [jnp.where((row ^ rel) == k, both[at], o) for k, o in enumerate(ordered)]
        return jnp.concatenate(ordered, axis=1)

    def add(*values):
        total = values[0].astype(F32)
        for value in values[1:]:
            total = total + value.astype(F32)
        return total

    def leave_z(pieces):
        return add(*(p[zs // 2 :] for p in pieces)).astype(BF16)

    def keep_z(pieces, come):
        return add(*(p[: zs // 2] for p in pieces), come)

    def last_z(total):
        count, bit = zs // 4, 4
        while count:
            come = send(total[count:].astype(BF16), "z", bit)
            total = add(total[:count], come)
            count, bit = count // 2, bit * 2
        return total[0]

    def out_last(total):
        count, bit = zs // 4, 8
        while count > 1:
            count //= 2
            come = send(total[4 * count :].astype(BF16), "z", bit)
            total, bit = add(total[: 4 * count], come), bit * 2
        total = add(total[:2], send(total[2:].astype(BF16), "x"))
        return add(total[0], send(total[1].astype(BF16), "y"))

    def tie_all(values, *done):
        return lax.optimization_barrier((tuple(values), done))[0]

    def pick(flag, one, other):
        return jnp.where(flag == 0, one, other)

    def split_micro(value):
        both = value.reshape(micro, seq, slab)
        mine = lax.dynamic_index_in_dim(both, y, 0, keepdims=False)
        return mine, lax.dynamic_index_in_dim(both, 1 - y, 0, keepdims=False)

    def spread(mine, theirs):
        theirs = send(theirs, "y")
        pair = jnp.stack([mine, theirs])
        other = send(pair, "c")
        blocks = [
            pick(
                y ^ yy,
                pick(c ^ cc, pair[0], other[0]),
                pick(c ^ cc, pair[1], other[1]),
            )
            for yy in range(2)
            for cc in range(2)
        ]
        return jnp.concatenate(blocks, axis=1), theirs

    def unspread(stay, leave):
        come = send(leave, "c")
        got = send(jnp.stack([stay[1], come[1]]), "y")
        return jnp.concatenate(
            [
                pick(
                    y ^ at,
                    pick(c ^ side, stay[0], come[0]),
                    pick(c ^ side, got[0], got[1]),
                )
                for at in range(2)
                for side in range(2)
            ],
            axis=0,
        )

    inner = w_gate.shape[1]
    padded = -(-inner // 256) * 256
    chunk = padded // 2
    pad = ((0, 0), (0, padded - inner))
    attn_shard = jnp.concatenate([w_query, w_key, w_value, w_out.T], axis=1)
    gate_up_down = [jnp.pad(w_gate, pad), jnp.pad(w_up, pad), jnp.pad(w_down.T, pad)]
    mlp_shards = [
        jnp.concatenate([w[:, at * chunk : (at + 1) * chunk] for w in gate_up_down], axis=1)
        for at in range(2)
    ]
    gain_parts = jnp.stack([gain_attn, gain_mlp])[None]
    gain_parts = jnp.concatenate([gain_parts, swap(gain_parts, "row", 1)])
    patches_mine, patches_other = split_micro(patches)
    near, bit = tie(attn_shard, patches_other)[None], zs // 2
    while bit > 1:
        come = send(near, "z", 2 * bit)
        gain_parts = jnp.concatenate([gain_parts, swap(gain_parts, "row", 2 * bit)])
        near = jnp.concatenate([near, tie(come, gain_parts)])
        bit //= 2
    gain_parts = jnp.concatenate([gain_parts, swap(gain_parts, "row", 2)])
    gains = order_rows(gain_parts)
    attn_gain, mlp_gain = gains[0:1], gains[1:2]
    x_all, x_half = spread(patches_mine, patches_other)
    cotangent_all, cotangent_half = spread(*split_micro(cotangent))
    a0, a1 = near, send(near, "z", 2)
    b0, c0 = send(a0, "x"), send(a0, "y")
    b1, c1 = send(tie(a1, b0), "x"), send(tie(a1, c0), "y")
    d0, d1 = send(tie(c0, b1), "x"), send(tie(b1, c1), "y")
    two_other = send(tie(mlp_shards[1], c1), "y")
    attn_w = (a0, a1, b0, b1, c0, c1, d0, d1)
    e0, e1 = gather_z(tie(mlp_shards[0], a1), b1, c1)
    one_near = jnp.concatenate([e0, e1])
    f = send(tie(one_near, d0), "x")
    two_pair = jnp.stack([mlp_shards[1], two_other])
    g = send(tie(one_near, d1), "y")
    one_w = (one_near, f, g, send(f, "y"))
    two_pair = tie(two_pair, e1)
    two_come = send(two_pair, "z", zs)

    length = lax.dynamic_slice_in_dim(lengths, y, 1)
    grad_mixed = jnp.where(
        lax.iota(jnp.int32, seq)[:, None] < length, cotangent_all, jnp.zeros((), BF16)
    )

    back_plan = plan_back_planes(zs)
    plans = (back_plan, plan_lines(zs))
    normed_one = norm_first(x_all, attn_gain)
    qkv = project_qkv(me, tie(normed_one, e0), attn_w, columns)
    attended, lse = attend(length, tie(qkv, one_near, two_pair), 2 * heads_here // HEAD_DIM)
    branch = project_out(me, tie(attended, g, two_come), attn_w)
    q0, q1 = gather_lines(two_pair, tie(two_come, branch[0]))
    two_w = (q0, q1, send(q0, "x"), send(q1, "x"))
    hidden, normed_two = norm_second(
        x_all, branch, [send(v, "c") for v in branch], mlp_gain
    )

    act_one, *grad_one = mlp(
        me, tie(normed_two, q1), tie(grad_mixed, branch[0]), one_w, zs, plans[0], back_plan
    )
    g00, g01, g10, g11 = grad_one
    far_one = send(g11, "x")
    side_one = send(g01, "x")
    act_two, *grad_two = mlp(
        me, tie(normed_two, act_one), grad_mixed, two_w, zs, plans[1], back_plan
    )
    h00, h01, h10, h11 = grad_two
    far_two = send(h11, "y")
    weights = (one_w, two_w)
    back_two = mlp_back(me, (act_one, act_two), weights, zs, plans)
    back_recv = [send(v, "c") for v in back_two]
    over_one = add(*tie_all((g10, far_one), back_two[0])).astype(BF16)
    mixed_own, mixed_other = mlp_out(me, (act_one, tie(act_two, over_one)), weights, zs, plans)
    over_one = send(over_one, "y")
    grad_h, grad_branch, mlp_gain_grad = norm_second_back(
        tie(hidden, mixed_own), back_two, back_recv, grad_mixed, mlp_gain
    )
    mixed_recv = send(tie(mixed_other, grad_branch), "c")
    side_two = send(h10, "y")
    over_two = add(*tie_all((h01, far_two), grad_branch)).astype(BF16)

    grad_attended, o0, o1 = out_back(me, tie(grad_branch, over_two), attended, attn_w)
    over_two = send(over_two, "x")
    finished = finish(me, length, tie(hidden, grad_attended), mixed_own, mixed_recv, slab)
    leave_out = send(o1, "z", 2)
    grads = attend_back(length, qkv, tie(grad_attended, finished[0]), lse, 1)
    first_one = leave_z(tie_all((g00, side_one, over_one), grads[0]))
    finished = tie_all(finished, grads[0])
    back_part, p10, p11 = qkv_back(
        me, (tie(grads[0], first_one, leave_out), *grads[1:]), normed_one, attn_w, columns, None, 1
    )
    far_qkv = send(p11, "x")
    first_one = send(first_one, "z", 2)
    out_sum = add(*tie_all((o0, leave_out), back_part))
    keep_out, leave_out = out_sum[:zs], out_sum[zs:].astype(BF16)
    sum_one = keep_z((g00, side_one, over_one), tie(first_one, back_part))
    grads = attend_back(
        length, qkv, tie(grad_attended, back_part, leave_out, sum_one), lse, 0
    )
    out_come = send(leave_out, "z", 4)
    sum_one = last_z(sum_one)
    over_qkv = add(*tie_all((p10, far_qkv), grads[0])).astype(BF16)
    out_sum = add(keep_out, tie(out_come, grads[0]))
    pieces = tie_all((h00, side_two, over_two), grads[0])
    leave_two = leave_z(pieces)
    back_own, back_other, p00, p01 = qkv_back(
        me, (tie(grads[0], over_qkv, leave_two, out_sum), *grads[1:]),
        normed_one, attn_w, columns, back_part, 0,
    )
    over_qkv = send(over_qkv, "y")
    side_qkv = send(p01, "x")
    two_left = send(leave_two, "z", 2)
    out_grad = out_last(out_sum)
    output = unspread(*finished)
    sum_two = last_z(keep_z(pieces, tie(two_left, back_own)))
    *grad_x, attn_gain_grad = norm_first_back(
        me, x_all, back_own, send(back_other, "c"), grad_h, attn_gain, slab
    )
    gain_grads = jnp.concatenate([attn_gain_grad, 0.5 * mlp_gain_grad], axis=0)
    for axis, bit in (("col", 1), ("col", 2)):
        gain_grads = gain_grads + swap(gain_grads, axis, bit)
    grad_patches = unspread(*tie_all(grad_x, gain_grads)).astype(F32)
    gain_grads = gain_grads + swap(gain_grads, "row", 1)
    pieces = (p00, side_qkv, over_qkv)
    qkv_grad = last_z(keep_z(pieces, send(leave_z(pieces), "z", 2)))
    bit = 2
    while bit < rows_axis:
        gain_grads = gain_grads + swap(gain_grads, "row", bit)
        bit *= 2
    mlp_sums = [
        jnp.concatenate([v[:, at * chunk : (at + 1) * chunk] for v in (sum_one, sum_two)], axis=1)[
            :, :inner
        ]
        for at in range(3)
    ]

    own_rows = width // rows_axis
    gain_grads = lax.dynamic_slice_in_dim(gain_grads, row * own_rows, own_rows, axis=1)

    return (
        output,
        grad_patches,
        qkv_grad[:, :heads_here],
        qkv_grad[:, heads_here : 2 * heads_here],
        qkv_grad[:, 2 * heads_here :],
        out_grad.T,
        mlp_sums[0],
        mlp_sums[1],
        mlp_sums[2].T,
        gain_grads[0],
        gain_grads[1],
    )


def solution(mesh):
    placed = (
        P("row", "col"),
        P("row", "col"),
        P("row", "col"),
        P("row", "col"),
        P("col", "row"),
        P("row", "col"),
        P("row", "col"),
        P("col", "row"),
        P("row"),
        P("row"),
        P("row"),
        P("row", "col"),
    )
    return jax.shard_map(
        shards,
        mesh=mesh,
        in_specs=placed,
        out_specs=(
            P("row", "col"),
            P("row", "col"),
            P("row", "col"),
            P("row", "col"),
            P("row", "col"),
            P("col", "row"),
            P("row", "col"),
            P("row", "col"),
            P("col", "row"),
            P("row"),
            P("row"),
        ),
        check_vma=False,
    )
```

```python
import functools

import jax
import jax.numpy as jnp
from jax import lax
from jax.experimental import pallas as pl
from jax.experimental.pallas import tpu as pltpu
from jax.sharding import PartitionSpec as P

HEAD_DIM = 64
PAIR = 2 * HEAD_DIM
EPSILON = 1e-06
MASKED = -1000000000.0
BF16 = jnp.bfloat16
F32 = jnp.float32
MIB = 1 << 20

NN = (((1,), (0,)), ((), ()))
NT = (((1,), (1,)), ((), ()))
TN = (((0,), (0,)), ((), ()))

ANY = pl.BlockSpec(memory_space=pltpu.HBM)
SCALARS = pl.BlockSpec(memory_space=pltpu.SMEM)


def mm(left, right, dims):
    return lax.dot_general(left, right, dims, preferred_element_type=F32)


def work(micros, values=0):
    return pl.CostEstimate(
        flops=int(micros * 1.15e9), transcendentals=0, bytes_accessed=int(micros * 1e6) + values
    )


def params(mib):
    return pltpu.CompilerParams(
        dimension_semantics=("arbitrary",), vmem_limit_bytes=mib * MIB
    )


def z_order(zs):
    order, bit = [0], zs // 2
    while bit:
        order += [at ^ bit for at in order]
        bit //= 2
    return order


def plan_planes(zs):
    order, half = z_order(zs), zs // 2
    return [
        [(py, px, pz) for pz in order[lo : lo + half]]
        for py in range(2)
        for px in range(2)
        for lo in (0, half)
    ]


def plan_wholes(zs):
    order, half = z_order(zs), zs // 2
    out = [[(py, px, pz) for pz in order] for py, px in ((0, 0), (0, 1), (1, 0))]
    return out + [[(1, 1, pz) for pz in order[lo : lo + half]] for lo in (0, half)]


def plan_back_planes(zs):
    return [[(py, px, pz) for pz in z_order(zs)] for py in range(2) for px in range(2)]


def plan_back_lines(zs):
    order, half = z_order(zs), zs // 2
    return [
        [(py, px, pz) for pz in order[lo : lo + half] for px in range(2) for py in range(2)]
        for lo in (0, half)
    ]


def block_copies(me, plan, buffers, parts, scratch_of, sems, out):
    rows = buffers[0].shape[1]
    copies = [[] for _ in parts]
    for blocks, buffer in zip(plan, buffers, strict=True):
        for at_block, (py, px, pz) in enumerate(blocks):
            owner = ((me[0] ^ pz) * 2) + (me[1] ^ px)
            for at, (first, n) in enumerate(parts):
                remote = buffer.at[at_block, :, pl.ds(first, n)]
                local = scratch_of(at, py, pl.ds(owner * rows, rows))
                ends = (local, remote) if out else (remote, local)
                copies[at].append(pltpu.make_async_copy(*ends, sems.at[at, py, px, pz]))
    return copies


def fetch_copies(me, plan, buffers, parts, scratch_of, sems):
    return block_copies(me, plan, buffers, parts, scratch_of, sems, False)


def emit_copies(me, plan, buffers, parts, scratch_of, sems):
    return block_copies(me, plan, buffers, parts, scratch_of, sems, True)


def copy_sems(zs, parts):
    return pltpu.SemaphoreType.DMA((parts, 2, 2, zs))


def start(copies):
    for copy in copies:
        copy.start()


def wait(copies):
    for copy in copies:
        copy.wait()


def run(parts):
    for copies in parts:
        start(copies)
    for copies in parts:
        wait(copies)


def vmem(mib):
    return pltpu.CompilerParams(vmem_limit_bytes=mib * MIB)


def norm_in(x_ref, gain_ref, n_ref):
    x = x_ref[...].astype(F32)
    rstd = lax.rsqrt(jnp.mean(x * x, axis=1, keepdims=True) + EPSILON)
    n_ref[...] = (x * rstd * gain_ref[...].astype(F32)).astype(BF16)


def norm_first(x, gain):
    tokens, width = x.shape
    block = tokens // 4
    row = pl.BlockSpec((block, width), lambda i: (i, 0))
    return pl.pallas_call(
        norm_in,
        out_shape=jax.ShapeDtypeStruct((tokens, width), BF16),
        grid=(4,),
        in_specs=[row, pl.BlockSpec((1, width), lambda i: (0, 0))],
        out_specs=row,
        compiler_params=params(32),
        cost_estimate=work(1),
        name="norm_first",
    )(x, gain)


def by_half(scratch):
    return lambda at, half, rows: scratch.at[half, rows, :]


def by_part(scratch):
    n = scratch.shape[2] // 2
    return lambda at, half, rows: scratch.at[at, rows, pl.ds(half * n, n)]


def project_in(plan, me_ref, n_ref, *refs):
    weights, (out_ref, w_scr, sems) = refs[:8], refs[8:]
    n = w_scr.shape[2]

    @pl.when(pl.program_id(0) == 0)
    def _():
        run(fetch_copies(me_ref, plan, weights, [(0, n)], by_half(w_scr), sems))

    for half in range(2):
        out_ref[:, half * n : (half + 1) * n] = mm(n_ref[...], w_scr[half], NN).astype(BF16)


def project_qkv(me, normed, weights, columns):
    tokens, width = normed.shape
    block = tokens // 4
    zs = 2 * weights[0].shape[0]
    return pl.pallas_call(
        functools.partial(project_in, plan_planes(zs)),
        out_shape=jax.ShapeDtypeStruct((tokens, 2 * columns), BF16),
        grid=(4,),
        in_specs=[SCALARS, pl.BlockSpec((block, width), lambda i: (i, 0))] + [ANY] * 8,
        out_specs=pl.BlockSpec((block, 2 * columns), lambda i: (i, 0)),
        scratch_shapes=[pltpu.VMEM((2, width, columns), BF16), copy_sems(zs, 1)],
        compiler_params=params(32),
        cost_estimate=work(6),
        name="project_qkv",
    )(me, normed, *weights)


def stack_heads(pair):
    lane = lax.broadcasted_iota(jnp.int32, pair.shape, 1)
    zero = jnp.zeros_like(pair)
    return jnp.concatenate(
        [jnp.where(lane < HEAD_DIM, pair, zero), jnp.where(lane < HEAD_DIM, zero, pair)], axis=0
    )


def masked_scores(length, key_rows, queries, first):
    raw = mm(key_rows, queries, NT)
    key_at = lax.broadcasted_iota(jnp.int32, raw.shape, 0)
    rows = raw.shape[1] // 2
    query_at = lax.broadcasted_iota(jnp.int32, raw.shape, 1)
    query_at = first + jnp.where(query_at >= rows, query_at - rows, query_at)
    return jnp.where((key_at <= query_at) & (key_at < length), raw, MASKED)


def attend_in(len_ref, q_ref, k_ref, v_ref, o_ref, lse_ref):
    tokens = q_ref.shape[0]
    rows = tokens // 4
    scale = HEAD_DIM ** (-0.5)
    length = len_ref[0]
    values_t = v_ref[...].T
    for at in range(4):
        first, last = at * rows, (at + 1) * rows
        queries = stack_heads(q_ref[first:last] * jnp.asarray(scale, BF16))
        scores = masked_scores(length, k_ref[:last], queries, first)
        peak = jnp.max(scores, axis=0, keepdims=True)
        expo = jnp.exp(scores - peak)
        denom = jnp.sum(expo, axis=0, keepdims=True)
        probs = (expo * (1.0 / denom)).astype(BF16)
        both = mm(values_t[:, :last], probs, NN)
        joined = jnp.concatenate([both[:HEAD_DIM, :rows], both[HEAD_DIM:, rows:]], axis=0)
        o_ref[first:last] = joined.T.astype(BF16)
        lse_ref[0, at : at + 1] = peak + jnp.log(denom)


def attend(length, qkv, heads):
    tokens = qkv.shape[0]
    pairs = heads // 2
    per = qkv.shape[1] // (6 * PAIR)

    def spec(which):
        return pl.BlockSpec(
            (tokens, PAIR), lambda i: (0, (i // per) * 3 * per + which * per + i % per)
        )

    return pl.pallas_call(
        attend_in,
        out_shape=(
            jax.ShapeDtypeStruct((tokens, pairs * PAIR), BF16),
            jax.ShapeDtypeStruct((pairs, 4, tokens // 2), F32),
        ),
        grid=(pairs,),
        in_specs=[SCALARS, spec(0), spec(1), spec(2)],
        out_specs=(
            pl.BlockSpec((tokens, PAIR), lambda i: (0, i)),
            pl.BlockSpec((1, 4, tokens // 2), lambda i: (i, 0, 0)),
        ),
        compiler_params=params(48),
        cost_estimate=work(13),
        name="attend",
    )(length, qkv, qkv, qkv)


def halves(block, width):
    return (
        pl.BlockSpec((block, width), lambda i: (jnp.minimum(i, 1), 0)),
        pl.BlockSpec((block, width), lambda i: (jnp.maximum(i - 2, 0), 0)),
    )


def to_halves(first, second, value):
    @pl.when(pl.program_id(0) < 2)
    def _():
        first[...] = value

    @pl.when(pl.program_id(0) >= 2)
    def _():
        second[...] = value


def of_halves(first, second):
    return jnp.where(pl.program_id(0) < 2, first[...].astype(F32), second[...].astype(F32))


def project_out_in(plan, me_ref, a_ref, *refs):
    weights, (out0, out1, w_scr, sems) = refs[:8], refs[8:]
    n = w_scr.shape[2]
    first = weights[0].shape[2] - n

    @pl.when(pl.program_id(0) == 0)
    def _():
        run(fetch_copies(me_ref, plan, weights, [(first, n)], by_half(w_scr), sems))

    total = mm(a_ref[:, :n], w_scr[0], NT) + mm(a_ref[:, n:], w_scr[1], NT)
    to_halves(out0, out1, total.astype(BF16))


def project_out(me, attended, weights):
    tokens, heads_wide = attended.shape
    half_zs, rows, _ = weights[0].shape
    zs = 2 * half_zs
    width = zs * 2 * rows
    n = heads_wide // 2
    block = tokens // 4
    return pl.pallas_call(
        functools.partial(project_out_in, plan_planes(zs)),
        out_shape=(jax.ShapeDtypeStruct((tokens // 2, width), BF16),) * 2,
        grid=(4,),
        in_specs=[SCALARS, pl.BlockSpec((block, 2 * n), lambda i: (i, 0))] + [ANY] * 8,
        out_specs=halves(block, width),
        scratch_shapes=[pltpu.VMEM((2, width, n), BF16), copy_sems(2 * half_zs, 1)],
        compiler_params=params(32),
        cost_estimate=work(5),
        name="project_out",
    )(me, attended, *weights)


def norm_second_in(x_ref, own0, own1, recv0, recv1, gain_ref, h_ref, n_ref):
    hidden = x_ref[...].astype(F32) + (of_halves(own0, own1) + of_halves(recv0, recv1))
    h_ref[...] = hidden
    rstd = lax.rsqrt(jnp.mean(hidden * hidden, axis=1, keepdims=True) + EPSILON)
    n_ref[...] = (hidden * rstd * gain_ref[...].astype(F32)).astype(BF16)


def norm_second(x, own, recv, gain):
    tokens, width = x.shape
    row = pl.BlockSpec((tokens // 4, width), lambda i: (i, 0))
    pair = halves(tokens // 4, width)
    return pl.pallas_call(
        norm_second_in,
        out_shape=(
            jax.ShapeDtypeStruct((tokens, width), F32),
            jax.ShapeDtypeStruct((tokens, width), BF16),
        ),
        grid=(4,),
        in_specs=[row, *pair, *pair, pl.BlockSpec((1, width), lambda i: (0, 0))],
        out_specs=(row, row),
        compiler_params=params(40),
        cost_estimate=work(4),
        name="norm_second",
    )(x, *own, *recv, gain)


def mlp_in(plan, back_plan, me_ref, n_hbm, m_hbm, *refs):
    count, back_count = len(plan), len(back_plan)
    weights, act_hbm = refs[:count], refs[count]
    outs = refs[count + 1 : count + 1 + back_count]
    n_ref, m_ref, w_scr, acts, staged, load_sems, sems, act_sems, out_sems = refs[
        count + 1 + back_count :
    ]
    n = w_scr.shape[2]
    parts = [(at * n // 2, n // 2) for at in range(3)]
    load_n = [pltpu.make_async_copy(n_hbm, n_ref, load_sems.at[0])]
    load_m = [pltpu.make_async_copy(m_hbm, m_ref, load_sems.at[1])]
    fetch = fetch_copies(me_ref, plan, weights, parts, by_part(w_scr), sems)
    emit = emit_copies(me_ref, back_plan, outs, parts, by_part(staged), out_sems)
    keep = [
        [pltpu.make_async_copy(acts.at[at], act_hbm.at[at], act_sems.at[at])] for at in range(3)
    ]
    for copies in (load_n, fetch[0], fetch[1], load_m, fetch[2]):
        start(copies)
    for lo in range(0, n, 256):
        cut = slice(lo, lo + 256)
        if lo == 0:
            wait(load_n + fetch[0])
        gate = mm(n_ref[...], w_scr[0, :, cut], NN)
        if lo == 0:
            wait(fetch[1])
        up = mm(n_ref[...], w_scr[1, :, cut], NN)
        if lo == 0:
            wait(load_m + fetch[2])
        grad_hidden = mm(m_ref[...], w_scr[2, :, cut], NN)
        sig = 0.5 * jnp.tanh(0.5 * gate) + 0.5
        act = gate * sig
        acts[2, :, cut] = (act * up).astype(BF16)
        acts[0, :, cut] = (grad_hidden * up * (sig * (1.0 + gate * (1.0 - sig)))).astype(BF16)
        acts[1, :, cut] = (grad_hidden * act).astype(BF16)
    for at in range(3):
        start(keep[at])
        staged[at] = mm((n_ref if at < 2 else m_ref)[...], acts[at], TN).astype(BF16)
        start(emit[at])
    for at in range(3):
        wait(keep[at] + emit[at])


def mlp(me, normed, grad_mixed, weights, zs, plan, back_plan):
    tokens, width = normed.shape
    _, rows, n3 = weights[0].shape
    n = 2 * n3 // 3
    pieces = tuple(jax.ShapeDtypeStruct((len(p), rows, n3), BF16) for p in back_plan)
    return pl.pallas_call(
        functools.partial(mlp_in, plan, back_plan),
        out_shape=(jax.ShapeDtypeStruct((3, tokens, n), BF16),) + pieces,
        in_specs=[SCALARS, ANY, ANY] + [ANY] * len(plan),
        out_specs=(ANY,) * (1 + len(pieces)),
        scratch_shapes=[
            pltpu.VMEM((tokens, width), BF16),
            pltpu.VMEM((tokens, width), BF16),
            pltpu.VMEM((3, width, n), BF16),
            pltpu.VMEM((3, tokens, n), BF16),
            pltpu.VMEM((3, width, n), BF16),
            pltpu.SemaphoreType.DMA((2,)),
            copy_sems(zs, 3),
            pltpu.SemaphoreType.DMA((3,)),
            copy_sems(zs, 3),
        ],
        compiler_params=vmem(60),
        cost_estimate=work(20),
        name="mlp",
    )(me, normed, grad_mixed, *weights)


def contract_in(plans, used, me_ref, a0, a1, *refs):
    count = len(plans[0])
    weights = (refs[:count], refs[count : count + len(plans[1])])
    outs, (acts, w_scr, total, staged, act_sems, sems, out_sems) = (
        refs[count + len(plans[1]) : -7],
        refs[-7:],
    )
    n = w_scr.shape[3]
    steps = []
    for chunk, source in enumerate((a0, a1)):
        fetch = fetch_copies(
            me_ref, plans[chunk], weights[chunk], [(p * n // 2, n // 2) for p in used],
            by_part(w_scr.at[chunk]), sems.at[chunk],
        )
        for at, part in enumerate(used):
            load = pltpu.make_async_copy(
                source.at[part], acts.at[chunk, at], act_sems.at[chunk, at]
            )
            steps.append((chunk, at, [load] + fetch[at]))
    for _, _, copies in steps:
        start(copies)
    tokens = acts.shape[2]
    half = tokens // 2
    for index, (chunk, at, copies) in enumerate(steps):
        wait(copies)
        if index < len(steps) - 1:
            product = mm(acts[chunk, at], w_scr[chunk, at], NT)
            total[...] = product if index == 0 else total[...] + product
    emits = []
    chunk, at, _ = steps[-1]
    for side in range(2):
        rows = pl.ds(side * half, half)
        product = total[rows] + mm(acts[chunk, at, rows], w_scr[chunk, at], NT)
        staged[side] = product.astype(BF16)
        emits.append(pltpu.make_async_copy(staged.at[side], outs[side], out_sems.at[side]))
        emits[-1].start()
    wait(emits)


def contract(me, acts, weights, zs, plans, used, name, micros):
    _, tokens, n = acts[0].shape
    _, rows, n3 = weights[0][0].shape
    width = zs * 2 * rows
    count = len(plans[0]) + len(plans[1])
    shape = jax.ShapeDtypeStruct((tokens // 2, width), BF16)
    return pl.pallas_call(
        functools.partial(contract_in, plans, used),
        out_shape=(shape, shape),
        in_specs=[SCALARS, ANY, ANY] + [ANY] * count,
        out_specs=(ANY, ANY),
        scratch_shapes=[
            pltpu.VMEM((2, len(used), tokens, n), BF16),
            pltpu.VMEM((2, len(used), width, n), BF16),
            pltpu.VMEM((tokens, width), F32),
            pltpu.VMEM((2, tokens // 2, width), BF16),
            pltpu.SemaphoreType.DMA((2, len(used))),
            pltpu.SemaphoreType.DMA((2, len(used), 2, 2, zs)),
            pltpu.SemaphoreType.DMA((2,)),
        ],
        compiler_params=vmem(48),
        cost_estimate=work(micros),
        name=name,
    )(me, *acts, *weights[0], *weights[1])


def scatter_lanes(me, value, full, stay_ref, leave_ref):
    slab = stay_ref.shape[2]
    full[...] = value
    for py in range(2):
        for ref, pc in ((stay_ref, 0), (leave_ref, 1)):
            at = (me[2] ^ py) * 2 + (me[3] ^ pc)
            ref[py] = full[:, pl.ds(pl.multiple_of(at * slab, slab), slab)]


def finish_in(me_ref, len_ref, h_ref, own0, own1, recv_ref, stay_ref, leave_ref, full):
    own = jnp.where(me_ref[3] == 0, own0[...].astype(F32), own1[...].astype(F32))
    total = h_ref[...] + (own + recv_ref[...].astype(F32))
    tokens = total.shape[0]
    at = lax.broadcasted_iota(jnp.int32, total.shape, 0) + me_ref[3] * tokens
    total = jnp.where(at < len_ref[0], total, 0.0)
    scatter_lanes(me_ref, total.astype(BF16), full, stay_ref, leave_ref)


def finish(me, length, hidden, own, recv, slab):
    half, width = recv.shape
    part = pl.BlockSpec((2, half, slab), lambda i, m, n: (0, 0, 0))
    mine = pl.BlockSpec((half, width), lambda i, m, n: (m[3], 0))
    row = pl.BlockSpec((half, width), lambda i, m, n: (0, 0))
    shape = jax.ShapeDtypeStruct((2, half, slab), BF16)
    return pl.pallas_call(
        finish_in,
        out_shape=(shape, shape),
        grid_spec=pltpu.PrefetchScalarGridSpec(
            num_scalar_prefetch=2,
            grid=(1,),
            in_specs=[mine, row, row, row],
            out_specs=(part, part),
            scratch_shapes=[pltpu.VMEM((half, width), BF16)],
        ),
        compiler_params=params(40),
        cost_estimate=work(3),
        name="finish",
    )(me, length, hidden, *own, recv)


def norm_second_back_in(
    h_ref, own0, own1, recv0, recv1, gm_ref, gain_ref, gh_ref, gb_ref
):
    hidden = h_ref[...]
    width = hidden.shape[1]
    rstd = lax.rsqrt(jnp.mean(hidden * hidden, axis=1, keepdims=True) + EPSILON)
    grad = of_halves(own0, own1) + of_halves(recv0, recv1)
    weighted = grad * gain_ref[...].astype(F32)
    stat = jnp.sum(weighted * hidden, axis=1, keepdims=True)
    grad_h = (
        gm_ref[...].astype(F32)
        + rstd * weighted
        - hidden * (rstd * rstd * rstd * stat / width)
    )
    gh_ref[...] = grad_h
    gb_ref[...] = grad_h.astype(BF16)


def norm_second_back(hidden, own, recv, grad_mixed, gain):
    tokens, width = hidden.shape
    row = pl.BlockSpec((tokens // 4, width), lambda i: (i, 0))
    one = pl.BlockSpec((1, width), lambda i: (0, 0))
    pair = halves(tokens // 4, width)
    return pl.pallas_call(
        norm_second_back_in,
        out_shape=(
            jax.ShapeDtypeStruct((tokens, width), F32),
            jax.ShapeDtypeStruct((tokens, width), BF16),
        ),
        grid=(4,),
        in_specs=[row, *pair, *pair, row, one],
        out_specs=(row, row),
        compiler_params=params(40),
        cost_estimate=work(5),
        name="norm_second_back",
    )(hidden, *own, *recv, grad_mixed, gain)


def out_back_in(plan, back_plan, me_ref, gb_hbm, a_hbm, *refs):
    count = len(plan)
    weights, ga_hbm, outs = refs[:count], refs[count], refs[count + 1 : count + 3]
    gb_ref, a_ref, ga_ref, w_scr, staged, load_sems, sems, out_sems = refs[count + 3 :]
    n = w_scr.shape[2]
    first = weights[0].shape[2] - n
    (fetch,) = fetch_copies(me_ref, plan, weights, [(first, n)], by_half(w_scr), sems)
    (emit,) = emit_copies(me_ref, back_plan, outs, [(0, n)], by_half(staged), out_sems)
    load_gb = [pltpu.make_async_copy(gb_hbm, gb_ref, load_sems.at[0])]
    load_a = [pltpu.make_async_copy(a_hbm, a_ref, load_sems.at[1])]
    keep = [pltpu.make_async_copy(ga_ref, ga_hbm, load_sems.at[2])]
    for copies in (load_gb, fetch, load_a):
        start(copies)
    wait(load_gb + fetch)
    for half in range(2):
        ga_ref[:, half * n : (half + 1) * n] = mm(gb_ref[...], w_scr[half], NN).astype(BF16)
    start(keep)
    wait(load_a)
    for half in range(2):
        cut = slice(half * n, (half + 1) * n)
        staged[half] = mm(gb_ref[...], a_ref[:, cut], TN).astype(BF16)
    start(emit)
    wait(keep + emit)


def out_back(me, grad_branch, attended, weights):
    tokens, width = grad_branch.shape
    heads_wide = attended.shape[1]
    half_zs, rows, _ = weights[0].shape
    zs = 2 * half_zs
    n = heads_wide // 2
    piece = jax.ShapeDtypeStruct((2 * zs, rows, n), BF16)
    return pl.pallas_call(
        functools.partial(out_back_in, plan_planes(zs), plan_back_lines(zs)),
        out_shape=(jax.ShapeDtypeStruct((tokens, heads_wide), BF16),) + (piece,) * 2,
        in_specs=[SCALARS, ANY, ANY] + [ANY] * len(weights),
        out_specs=(ANY,) * 3,
        scratch_shapes=[
            pltpu.VMEM((tokens, width), BF16),
            pltpu.VMEM((tokens, heads_wide), BF16),
            pltpu.VMEM((tokens, heads_wide), BF16),
            pltpu.VMEM((2, width, n), BF16),
            pltpu.VMEM((2, width, n), BF16),
            pltpu.SemaphoreType.DMA((3,)),
            copy_sems(zs, 1),
            copy_sems(zs, 1),
        ],
        compiler_params=vmem(40),
        cost_estimate=work(5),
        name="out_back",
    )(me, grad_branch, attended, *weights)


def attend_back_in(len_ref, q_ref, k_ref, v_ref, g_ref, lse_ref, gq_ref, gk_ref, gv_ref, *scratch):
    gk_acc, gv_acc = scratch
    tokens = q_ref.shape[0]
    rows = tokens // 4
    scale = HEAD_DIM ** (-0.5)
    length = len_ref[0]
    keys_t = k_ref[...].T
    gk_acc[...] = jnp.zeros_like(gk_acc)
    gv_acc[...] = jnp.zeros_like(gv_acc)
    for at in range(4):
        first, last = at * rows, (at + 1) * rows
        queries = stack_heads(q_ref[first:last] * jnp.asarray(scale, BF16))
        grads = stack_heads(g_ref[first:last])
        scores = masked_scores(length, k_ref[:last], queries, first)
        probs = jnp.exp(scores - lse_ref[0, at : at + 1])
        grad_probs = mm(v_ref[:last], grads, NT)
        inner = jnp.sum(probs * grad_probs, axis=0, keepdims=True)
        grad_scores = (probs * (grad_probs - inner)).astype(BF16)
        both = mm(keys_t[:, :last], grad_scores, NN)
        joined = jnp.concatenate([both[:HEAD_DIM, :rows], both[HEAD_DIM:, rows:]], axis=0)
        gq_ref[first:last] = (joined.T * scale).astype(BF16)
        gk_acc[:last] += mm(grad_scores, queries, NN)
        gv_acc[:last] += mm(probs.astype(BF16), grads, NN)
    gk_ref[...] = gk_acc[...].astype(BF16)
    gv_ref[...] = gv_acc[...].astype(BF16)


def attend_back(length, qkv, grad_attended, lse, half):
    tokens = qkv.shape[0]
    per = lse.shape[0] // 2

    def spec(which):
        return pl.BlockSpec((tokens, PAIR), lambda i: (0, half * 3 * per + which * per + i))

    out = pl.BlockSpec((tokens, PAIR), lambda i: (0, i))
    shape = jax.ShapeDtypeStruct((tokens, per * PAIR), BF16)
    return pl.pallas_call(
        attend_back_in,
        out_shape=(shape, shape, shape),
        grid=(per,),
        in_specs=[
            SCALARS,
            spec(0),
            spec(1),
            spec(2),
            pl.BlockSpec((tokens, PAIR), lambda i: (0, half * per + i)),
            pl.BlockSpec((1, 4, tokens // 2), lambda i: (half * per + i, 0, 0)),
        ],
        out_specs=(out, out, out),
        scratch_shapes=[pltpu.VMEM((tokens, PAIR), F32), pltpu.VMEM((tokens, PAIR), F32)],
        compiler_params=params(56),
        cost_estimate=work(11),
        name="attend_back",
    )(length, qkv, qkv, qkv, grad_attended, lse)


def weight_back_in(back_plan, me_ref, gq, gk, gv, n_hbm, *refs):
    count = len(back_plan)
    outs, (grad, n_ref, staged, load_sems, out_sems) = refs[:count], refs[count:]
    columns = staged.shape[1]
    n = columns // 3
    loads = [
        pltpu.make_async_copy(ref, grad.at[:, pl.ds(at * n, n)], load_sems.at[at])
        for at, ref in enumerate((gq, gk, gv))
    ] + [pltpu.make_async_copy(n_hbm, n_ref, load_sems.at[3])]
    (emit,) = emit_copies(
        me_ref, back_plan, outs, [(0, columns)], lambda at, half, rows: staged.at[rows, :], out_sems
    )
    start(loads)
    wait(loads)
    staged[...] = mm(n_ref[...], grad[...], TN).astype(BF16)
    start(emit)
    wait(emit)


def weight_back(me, grads, normed, zs, half):
    tokens, width = normed.shape
    columns = 3 * grads[0].shape[1]
    back_plan = [p for p in plan_back_planes(zs) if p[0][0] == half]
    if half == 0:
        back_plan = back_plan[:1] + [back_plan[1][: zs // 2], back_plan[1][zs // 2 :]]
    pieces = tuple(
        jax.ShapeDtypeStruct((len(p), width // (2 * zs), columns), BF16) for p in back_plan
    )
    return pl.pallas_call(
        functools.partial(weight_back_in, back_plan),
        out_shape=pieces,
        in_specs=[SCALARS] + [ANY] * 4,
        out_specs=(ANY,) * len(pieces),
        scratch_shapes=[
            pltpu.VMEM((tokens, columns), BF16),
            pltpu.VMEM((tokens, width), BF16),
            pltpu.VMEM((width, columns), BF16),
            pltpu.SemaphoreType.DMA((4,)),
            copy_sems(zs, 1),
        ],
        compiler_params=vmem(40),
        cost_estimate=work(4),
        name="weight_back",
    )(me, *grads, normed)


def qkv_back_in(plan, me_ref, *refs):
    grads, weights, outs = refs[:6], refs[6 : 6 + len(plan)], refs[6 + len(plan) : 8 + len(plan)]
    grad, w_scr, staged, load_sems, sems, out_sems = refs[8 + len(plan) :]
    columns = w_scr.shape[2]
    n = columns // 3
    loads = [
        pltpu.make_async_copy(
            ref, grad.at[at // 3, :, pl.ds(at % 3 * n, n)], load_sems.at[at]
        )
        for at, ref in enumerate(grads)
    ]
    (fetch,) = fetch_copies(me_ref, plan, weights, [(0, columns)], by_half(w_scr), sems)
    copies = [fetch[: len(fetch) // 2] + loads[:3], fetch[len(fetch) // 2 :] + loads[3:]]
    start(copies[0])
    start(copies[1])
    half = staged.shape[1]
    wait(copies[0])
    first = mm(grad[0], w_scr[0], NT)
    wait(copies[1])
    staged[0] = (first[:half] + mm(grad[1, :half], w_scr[1], NT)).astype(BF16)
    staged[1] = (first[half:] + mm(grad[1, half:], w_scr[1], NT)).astype(BF16)
    emit = [
        pltpu.make_async_copy(staged.at[me_ref[3]], outs[0], out_sems.at[0]),
        pltpu.make_async_copy(staged.at[1 - me_ref[3]], outs[1], out_sems.at[1]),
    ]
    start(emit)
    wait(emit)


def qkv_back(me, grads, weights, columns):
    tokens, n = grads[0].shape
    half_zs, rows, _ = weights[0].shape
    zs = 2 * half_zs
    width = zs * 2 * rows
    plan = plan_planes(zs)
    shape = jax.ShapeDtypeStruct((tokens // 2, width), BF16)
    return pl.pallas_call(
        functools.partial(qkv_back_in, plan),
        out_shape=(shape, shape),
        in_specs=[SCALARS] + [ANY] * (6 + len(plan)),
        out_specs=(ANY, ANY),
        scratch_shapes=[
            pltpu.VMEM((2, tokens, columns), BF16),
            pltpu.VMEM((2, width, columns), BF16),
            pltpu.VMEM((2, tokens // 2, width), BF16),
            pltpu.SemaphoreType.DMA((6,)),
            copy_sems(zs, 1),
            pltpu.SemaphoreType.DMA((2,)),
        ],
        compiler_params=vmem(48),
        cost_estimate=work(6),
        name="qkv_back",
    )(me, *grads, *weights)


def norm_first_back_in(
    me_ref, x_ref, own_ref, recv_ref, gh_ref, gain_ref, stay_ref, leave_ref, full
):
    x = x_ref[...].astype(F32)
    width = x.shape[1]
    rstd = lax.rsqrt(jnp.mean(x * x, axis=1, keepdims=True) + EPSILON)
    grad = own_ref[...].astype(F32) + recv_ref[...].astype(F32)
    weighted = grad * gain_ref[...].astype(F32)
    stat = jnp.sum(weighted * x, axis=1, keepdims=True)
    gx = gh_ref[...] + rstd * weighted - x * (rstd * rstd * rstd * stat / width)
    scatter_lanes(me_ref, gx.astype(BF16), full, stay_ref, leave_ref)


def norm_first_back(me, x, own, recv, grad_h, gain, slab):
    half, width = own.shape
    part = pl.BlockSpec((2, half, slab), lambda i, m: (0, 0, 0))
    mine = pl.BlockSpec((half, width), lambda i, m: (m[3], 0))
    row = pl.BlockSpec((half, width), lambda i, m: (0, 0))
    one = pl.BlockSpec((1, width), lambda i, m: (0, 0))
    shape = jax.ShapeDtypeStruct((2, half, slab), BF16)
    return pl.pallas_call(
        norm_first_back_in,
        out_shape=(shape, shape),
        grid_spec=pltpu.PrefetchScalarGridSpec(
            num_scalar_prefetch=1,
            grid=(1,),
            in_specs=[mine, row, row, mine, one],
            out_specs=(part, part),
            scratch_shapes=[pltpu.VMEM((half, width), BF16)],
        ),
        compiler_params=params(40),
        cost_estimate=work(4),
        name="norm_first_back",
    )(me, x, own, recv, grad_h, gain)


def shards(
    patches,
    w_query,
    w_key,
    w_value,
    w_out,
    w_gate,
    w_up,
    w_down,
    gain_attn,
    gain_mlp,
    lengths,
    cotangent,
):
    slab = patches.shape[1]
    rows_axis, cols_axis = lax.axis_size("row"), lax.axis_size("col")
    width = slab * cols_axis
    micro = lengths.shape[0]
    seq = patches.shape[0] // micro
    zs = rows_axis // 2
    row, col = lax.axis_index("row"), lax.axis_index("col")
    z, x, y, c = row // 2, row % 2, col // 2, col % 2
    me = jnp.stack([z, x, y, c]).astype(jnp.int32)
    heads_here = w_query.shape[1]
    columns = 3 * heads_here

    def swap(value, axis, bit):
        size = lax.axis_size(axis)
        return lax.ppermute(value, axis, [(i, i ^ bit) for i in range(size)])

    sent = {"x": [], "y": [], "z": [], "c": []}
    depth = {"x": 2, "y": 2, "z": 2, "c": 2}
    bits = {"x": ("row", 1), "y": ("col", 2), "c": ("col", 1)}

    def send(value, link, bit=None):
        axis, one = bits.get(link, ("row", bit))
        queue = sent[link]
        if len(queue) >= depth[link]:
            value = lax.optimization_barrier((value, queue[-depth[link]]))[0]
        out = swap(value, axis, one)
        queue.append(out)
        return out

    def gather_z(shard, *done):
        near, bit = shard[None], zs // 2
        while bit > 1:
            near = jnp.concatenate([near, tie(send(near, "z", 2 * bit), *done)])
            bit //= 2
        return near, send(near, "z", 2)

    def tie(value, *done):
        return lax.optimization_barrier((value, *done))[0]

    def order_rows(both):
        owned = [0]
        for bit in [1] + [2 * (zs >> k) for k in range(1, zs.bit_length())]:
            owned += [at ^ bit for at in owned]
        ordered = [jnp.zeros_like(both[0])] * rows_axis
        for at, rel in enumerate(owned):
            ordered = [jnp.where((row ^ rel) == k, both[at], o) for k, o in enumerate(ordered)]
        return jnp.concatenate(ordered, axis=1)

    def add(*values):
        total = values[0].astype(F32)
        for value in values[1:]:
            total = total + value.astype(F32)
        return total

    def leave_z(pieces):
        return add(*(p[zs // 2 :] for p in pieces)).astype(BF16)

    def keep_z(pieces, come):
        return add(*(p[: zs // 2] for p in pieces), come)

    def next_z(total, bit=4):
        count = total.shape[0] // 2
        if not count:
            return total, None, bit
        return total[:count], send(total[count:].astype(BF16), "z", bit), bit

    def last_z(total, come, bit):
        while come is not None:
            total, come, bit = next_z(add(total, come), 2 * bit)
        return total[0]

    def out_x(total):
        count, bit = zs // 4, 8
        while count > 1:
            count //= 2
            come = swap(total[4 * count :].astype(BF16), "row", bit)
            total, bit = add(total[: 4 * count], come), bit * 2
        return total[:2], swap(total[2:].astype(BF16), "row", 1)

    def tie_all(values, *done):
        return lax.optimization_barrier((tuple(values), done))[0]

    def pick(flag, one, other):
        return jnp.where(flag == 0, one, other)

    def split_micro(value):
        both = value.reshape(micro, seq, slab)
        mine = lax.dynamic_index_in_dim(both, y, 0, keepdims=False)
        return mine, lax.dynamic_index_in_dim(both, 1 - y, 0, keepdims=False)

    def spread(mine, theirs):
        theirs = send(theirs, "y")
        pair = jnp.stack([mine, theirs])
        other = send(pair, "c")
        blocks = [
            pick(
                y ^ yy,
                pick(c ^ cc, pair[0], other[0]),
                pick(c ^ cc, pair[1], other[1]),
            )
            for yy in range(2)
            for cc in range(2)
        ]
        return jnp.concatenate(blocks, axis=1), theirs

    def unspread_start(stay, leave):
        come = swap(leave, "col", 1)
        return stay, come, swap(jnp.stack([stay[1], come[1]]), "col", 2)

    def unspread_finish(stay, come, got):
        return jnp.concatenate(
            [
                pick(
                    y ^ at,
                    pick(c ^ side, stay[0], come[0]),
                    pick(c ^ side, got[0], got[1]),
                )
                for at in range(2)
                for side in range(2)
            ],
            axis=0,
        )

    inner = w_gate.shape[1]
    padded = -(-inner // 256) * 256
    chunk = padded // 2
    pad = ((0, 0), (0, padded - inner))
    attn_shard = jnp.concatenate([w_query, w_key, w_value, w_out.T], axis=1)
    gate_up_down = [jnp.pad(w_gate, pad), jnp.pad(w_up, pad), jnp.pad(w_down.T, pad)]
    mlp_shards = [
        jnp.concatenate([w[:, at * chunk : (at + 1) * chunk] for w in gate_up_down], axis=1)
        for at in range(2)
    ]
    gain_parts = jnp.stack([gain_attn, gain_mlp])[None]
    gain_parts = jnp.concatenate([gain_parts, swap(gain_parts, "row", 1)])
    patches_mine, patches_other = split_micro(patches)
    near, bit = tie(attn_shard, patches_other)[None], zs // 2
    while bit > 1:
        come = send(near, "z", 2 * bit)
        gain_parts = jnp.concatenate([gain_parts, swap(gain_parts, "row", 2 * bit)])
        near = jnp.concatenate([near, tie(come, gain_parts)])
        bit //= 2
    gain_parts = jnp.concatenate([gain_parts, swap(gain_parts, "row", 2)])
    gains = order_rows(gain_parts)
    attn_gain, mlp_gain = gains[0:1], gains[1:2]
    x_all, x_half = spread(patches_mine, patches_other)
    cotangent_all, cotangent_half = spread(*split_micro(cotangent))
    a0, a1 = near, send(near, "z", 2)
    b0, c0 = send(a0, "x"), send(a0, "y")
    b1, c1 = send(tie(a1, b0), "x"), send(tie(a1, c0), "y")
    d0, d1 = send(tie(c0, b1), "x"), send(tie(b1, c1), "y")
    attn_w = (a0, a1, b0, b1, c0, c1, d0, d1)
    e0, e1 = gather_z(tie(mlp_shards[0], a1), b1, c1)
    one_near = jnp.concatenate([e0, e1])
    two_near = jnp.concatenate(gather_z(tie(mlp_shards[1], e1)))
    f, g = swap(tie(one_near, d0), "row", 1), swap(tie(one_near, d1), "col", 2)
    one_w = (one_near, f, g, swap(g[: zs // 2], "row", 1), swap(f[zs // 2 :], "col", 2))

    length = lax.dynamic_slice_in_dim(lengths, y, 1)
    grad_mixed = jnp.where(
        lax.iota(jnp.int32, seq)[:, None] < length, cotangent_all, jnp.zeros((), BF16)
    )

    back_plan = plan_back_planes(zs)
    plans = (plan_wholes(zs),) * 2
    normed_one = norm_first(x_all, attn_gain)
    qkv = project_qkv(me, tie(normed_one, one_near), attn_w, columns)
    attended, lse = attend(length, qkv, 2 * heads_here // HEAD_DIM)
    branch = project_out(me, tie(attended, g, f), attn_w)
    f, g = swap(tie(two_near, one_w[3]), "row", 1), swap(tie(two_near, one_w[4]), "col", 2)
    hidden, normed_two = norm_second(
        tie(x_all, grad_mixed), branch, [send(v, "c") for v in branch], mlp_gain
    )

    act_one, *grad_one = mlp(
        me, normed_two, grad_mixed, one_w, zs, plans[0], back_plan
    )
    g00, g01, g10, g11 = grad_one
    f, g = tie_all((f, g), act_one)
    two_w = (two_near, f, g, swap(g[: zs // 2], "row", 1), swap(f[zs // 2 :], "col", 2))
    far_one = send(g11, "x")
    act_two, *grad_two = mlp(
        me, tie(normed_two, act_one), grad_mixed, two_w, zs, plans[1], back_plan
    )
    h00, h01, h10, h11 = grad_two
    far_two = send(h11, "y")
    side_one = send(tie(g01, act_two), "x")
    weights = (one_w, two_w)
    acts = (act_one, act_two)
    back_two = contract(me, acts, weights, zs, plans, (0, 1), "mlp_back", 9)
    back_recv = [send(v, "c") for v in back_two]
    over_one = add(*tie_all((g10, far_one), back_two[0])).astype(BF16)
    acts = (act_one, tie(act_two, over_one))
    mixed = contract(me, acts, weights, zs, plans, (2,), "mlp_out", 6)
    over_one = send(over_one, "y")
    grad_h, grad_branch = norm_second_back(
        tie(hidden, mixed[0]), back_two, back_recv, grad_mixed, mlp_gain
    )
    mixed_recv = send(tie(pick(c, mixed[1], mixed[0]), grad_branch), "c")
    side_two = send(h10, "y")
    over_two = add(*tie_all((h01, far_two), grad_branch)).astype(BF16)

    grad_attended, o0, o1 = out_back(me, tie(grad_branch, over_two), attended, attn_w)
    over_two = send(over_two, "x")
    finished = finish(me, length, tie(hidden, grad_attended), mixed, mixed_recv, slab)
    leave_out = send(o1, "z", 2)
    grads = attend_back(length, qkv, tie(grad_attended, finished[0]), lse, 1)
    first_one = leave_z(tie_all((g00, side_one, over_one), grads[0]))
    finished = tie_all(finished, grads[0])
    output_sent = unspread_start(*finished)
    other_grads = grads
    p10, p11 = weight_back(
        me, (tie(grads[0], first_one, leave_out), *grads[1:]), normed_one, zs, 1
    )
    far_qkv = send(p11, "x")
    first_one = send(first_one, "z", 2)
    out_sum = add(*tie_all((o0, leave_out), p10))
    keep_out, leave_out = out_sum[:zs], out_sum[zs:].astype(BF16)
    pieces = tie_all((h00, side_two, over_two), p10)
    leave_two = leave_z(pieces)
    grads = attend_back(
        length, qkv, tie(grad_attended, p10, leave_out, leave_two), lse, 0
    )
    out_come = swap(leave_out, "row", 4)
    two_come = swap(leave_two, "row", 2)
    sum_one = next_z(keep_z((g00, side_one, over_one), tie(first_one, grads[0])))
    count = zs // 2
    p10, far_qkv = tie_all((p10, far_qkv), grads[0])
    over_hi = add(p10[count:], far_qkv[count:]).astype(BF16)
    over_lo = add(p10[:count], far_qkv[:count]).astype(BF16)
    out_sum = add(keep_out, tie(out_come, grads[0]))
    sum_two = keep_z(pieces, tie(two_come, grads[0]))
    out_sum, out_come = out_x(out_sum)
    p00, side_lo, side_hi = weight_back(
        me, (tie(grads[0], over_hi, over_lo, sum_two, output_sent[2]), *grads[1:]),
        normed_one, zs, 0
    )
    over_hi = swap(over_hi, "col", 2)
    over_lo = swap(over_lo, "col", 2)
    side_hi, side_lo = swap(side_hi, "row", 1), swap(side_lo, "row", 1)
    sum_two = next_z(sum_two)
    out_sum = add(out_sum, tie(out_come, p00))
    back_own, back_other = qkv_back(
        me, (tie(grads[0], p00, out_sum), *grads[1:], *other_grads), attn_w, columns
    )
    out_come = swap(out_sum[1].astype(BF16), "col", 2)
    grad_x = norm_first_back(
        me, tie(x_all, over_hi, side_hi), back_own, send(back_other, "c"), grad_h, attn_gain, slab
    )
    patches_sent = unspread_start(*grad_x)
    leave_qkv = add(p00[count:], over_hi, side_hi).astype(BF16)
    come_qkv = swap(leave_qkv, "row", 2)

    def late(come):
        return tie(come, leave_qkv) if come is not None else None

    out_grad = add(out_sum[0], tie(out_come, come_qkv))
    output = unspread_finish(*tie_all(output_sent, leave_qkv))
    sum_one = last_z(sum_one[0], late(sum_one[1]), sum_one[2])
    sum_two = last_z(sum_two[0], late(sum_two[1]), sum_two[2])
    qkv_sum, qkv_come, bit = next_z(add(p00[:count], over_lo, side_lo, come_qkv))
    qkv_grad = last_z(qkv_sum, tie(qkv_come, patches_sent[2]), bit)
    grad_patches = unspread_finish(*patches_sent).astype(F32)
    mlp_sums = [
        jnp.concatenate([v[:, at * chunk : (at + 1) * chunk] for v in (sum_one, sum_two)], axis=1)[
            :, :inner
        ]
        for at in range(3)
    ]

    def weighed(weights, grads):
        return sum(jnp.sum(w.astype(F32) * g, axis=1) for w, g in zip(weights, grads, strict=True))

    gain_grads = jnp.stack(
        [
            weighed(
                (w_query, w_key, w_value),
                [qkv_grad[:, at * heads_here : (at + 1) * heads_here] for at in range(3)],
            ),
            weighed((w_gate, w_up), mlp_sums[:2]),
        ]
    )
    for bit in (2, 1):
        gain_grads = gain_grads + swap(gain_grads, "col", bit)
    gain_grads = gain_grads / jnp.stack([gain_attn, gain_mlp]).astype(F32)

    return (
        output,
        grad_patches,
        qkv_grad[:, :heads_here],
        qkv_grad[:, heads_here : 2 * heads_here],
        qkv_grad[:, 2 * heads_here :],
        out_grad.T,
        mlp_sums[0],
        mlp_sums[1],
        mlp_sums[2].T,
        gain_grads[0],
        gain_grads[1],
    )


def solution(mesh):
    placed = (
        P("row", "col"),
        P("row", "col"),
        P("row", "col"),
        P("row", "col"),
        P("col", "row"),
        P("row", "col"),
        P("row", "col"),
        P("col", "row"),
        P("row"),
        P("row"),
        P("row"),
        P("row", "col"),
    )
    return jax.shard_map(
        shards,
        mesh=mesh,
        in_specs=placed,
        out_specs=(
            P("row", "col"),
            P("row", "col"),
            P("row", "col"),
            P("row", "col"),
            P("row", "col"),
            P("col", "row"),
            P("row", "col"),
            P("row", "col"),
            P("col", "row"),
            P("row"),
            P("row"),
        ),
        check_vma=False,
    )
```

```python
import functools

import jax
import jax.numpy as jnp
from jax import lax
from jax.experimental import pallas as pl
from jax.experimental.pallas import tpu as pltpu
from jax.sharding import PartitionSpec as P

HEAD_DIM = 64
PAIR = 2 * HEAD_DIM
EPSILON = 1e-06
MASKED = -1000000000.0
BF16 = jnp.bfloat16
F32 = jnp.float32
MIB = 1 << 20

NN = (((1,), (0,)), ((), ()))
NT = (((1,), (1,)), ((), ()))
TN = (((0,), (0,)), ((), ()))

ANY = pl.BlockSpec(memory_space=pltpu.HBM)
SCALARS = pl.BlockSpec(memory_space=pltpu.SMEM)


def mm(left, right, dims):
    return lax.dot_general(left, right, dims, preferred_element_type=F32)


def work(micros, values=0):
    return pl.CostEstimate(
        flops=int(micros * 1.15e9), transcendentals=0, bytes_accessed=int(micros * 1e6) + values
    )


def params(mib):
    return pltpu.CompilerParams(
        dimension_semantics=("arbitrary",), vmem_limit_bytes=mib * MIB
    )


def z_order(zs):
    order, bit = [0], zs // 2
    while bit:
        order += [at ^ bit for at in order]
        bit //= 2
    return order


def plan_planes(zs):
    order, half = z_order(zs), zs // 2
    return [
        [(py, px, pz) for pz in order[lo : lo + half]]
        for py in range(2)
        for px in range(2)
        for lo in (0, half)
    ]


def plan_wholes(zs):
    order, half = z_order(zs), zs // 2
    out = [[(py, px, pz) for pz in order] for py, px in ((0, 0), (0, 1), (1, 0))]
    return out + [[(1, 1, pz) for pz in order[lo : lo + half]] for lo in (0, half)]


def plan_back_planes(zs):
    return [[(py, px, pz) for pz in z_order(zs)] for py in range(2) for px in range(2)]


def plan_back_lines(zs):
    order, half = z_order(zs), zs // 2
    return [
        [(py, px, pz) for pz in order[lo : lo + half] for px in range(2) for py in range(2)]
        for lo in (0, half)
    ]


def block_copies(me, plan, buffers, parts, scratch_of, sems, out):
    rows = buffers[0].shape[1]
    copies = [[] for _ in parts]
    for blocks, buffer in zip(plan, buffers, strict=True):
        for at_block, (py, px, pz) in enumerate(blocks):
            owner = ((me[0] ^ pz) * 2) + (me[1] ^ px)
            for at, (first, n) in enumerate(parts):
                remote = buffer.at[at_block, :, pl.ds(first, n)]
                local = scratch_of(at, py, pl.ds(owner * rows, rows))
                ends = (local, remote) if out else (remote, local)
                copies[at].append(pltpu.make_async_copy(*ends, sems.at[at, py, px, pz]))
    return copies


def fetch_copies(me, plan, buffers, parts, scratch_of, sems):
    return block_copies(me, plan, buffers, parts, scratch_of, sems, False)


def emit_copies(me, plan, buffers, parts, scratch_of, sems):
    return block_copies(me, plan, buffers, parts, scratch_of, sems, True)


def copy_sems(zs, parts):
    return pltpu.SemaphoreType.DMA((parts, 2, 2, zs))


def start(copies):
    for copy in copies:
        copy.start()


def wait(copies):
    for copy in copies:
        copy.wait()


def run(parts):
    for copies in parts:
        start(copies)
    for copies in parts:
        wait(copies)


def vmem(mib):
    return pltpu.CompilerParams(vmem_limit_bytes=mib * MIB)


def norm_in(x_ref, gain_ref, n_ref):
    x = x_ref[...].astype(F32)
    rstd = lax.rsqrt(jnp.mean(x * x, axis=1, keepdims=True) + EPSILON)
    n_ref[...] = (x * rstd * gain_ref[...].astype(F32)).astype(BF16)


def norm_first(x, gain):
    tokens, width = x.shape
    block = tokens // 4
    row = pl.BlockSpec((block, width), lambda i: (i, 0))
    return pl.pallas_call(
        norm_in,
        out_shape=jax.ShapeDtypeStruct((tokens, width), BF16),
        grid=(4,),
        in_specs=[row, pl.BlockSpec((1, width), lambda i: (0, 0))],
        out_specs=row,
        compiler_params=params(32),
        cost_estimate=work(1),
        name="norm_first",
    )(x, gain)


def by_half(scratch):
    return lambda at, half, rows: scratch.at[half, rows, :]


def by_part(scratch):
    n = scratch.shape[2] // 2
    return lambda at, half, rows: scratch.at[at, rows, pl.ds(half * n, n)]


def project_in(plan, me_ref, n_ref, *refs):
    weights, (out_ref, w_scr, sems) = refs[:8], refs[8:]
    n = w_scr.shape[2]

    @pl.when(pl.program_id(0) == 0)
    def _():
        run(fetch_copies(me_ref, plan, weights, [(0, n)], by_half(w_scr), sems))

    for half in range(2):
        out_ref[:, half * n : (half + 1) * n] = mm(n_ref[...], w_scr[half], NN).astype(BF16)


def project_qkv(me, normed, weights, columns):
    tokens, width = normed.shape
    block = tokens // 4
    zs = 2 * weights[0].shape[0]
    return pl.pallas_call(
        functools.partial(project_in, plan_planes(zs)),
        out_shape=jax.ShapeDtypeStruct((tokens, 2 * columns), BF16),
        grid=(4,),
        in_specs=[SCALARS, pl.BlockSpec((block, width), lambda i: (i, 0))] + [ANY] * 8,
        out_specs=pl.BlockSpec((block, 2 * columns), lambda i: (i, 0)),
        scratch_shapes=[pltpu.VMEM((2, width, columns), BF16), copy_sems(zs, 1)],
        compiler_params=params(32),
        cost_estimate=work(6),
        name="project_qkv",
    )(me, normed, *weights)


def stack_heads(pair):
    lane = lax.broadcasted_iota(jnp.int32, pair.shape, 1)
    zero = jnp.zeros_like(pair)
    return jnp.concatenate(
        [jnp.where(lane < HEAD_DIM, pair, zero), jnp.where(lane < HEAD_DIM, zero, pair)], axis=0
    )


def masked_scores(length, key_rows, queries, first):
    raw = mm(key_rows, queries, NT)
    keys, columns = raw.shape
    rows = columns // 2
    query_at = lax.broadcasted_iota(jnp.int32, (1, columns), 1)
    query_at = first + jnp.where(query_at >= rows, query_at - rows, query_at)
    limit = jnp.minimum(query_at + 1, length)
    return jnp.where(lax.broadcasted_iota(jnp.int32, raw.shape, 0) < limit, raw, MASKED)


def attend_in(len_ref, q_ref, k_ref, v_ref, o_ref, lse_ref):
    tokens = q_ref.shape[0]
    rows = tokens // 4
    scale = HEAD_DIM ** (-0.5)
    length = len_ref[0]
    values_t = v_ref[...].T
    for at in range(4):
        first, last = at * rows, (at + 1) * rows
        queries = stack_heads(q_ref[first:last] * jnp.asarray(scale, BF16))
        scores = masked_scores(length, k_ref[:last], queries, first)
        peak = jnp.max(scores, axis=0, keepdims=True)
        expo = jnp.exp(scores - peak)
        denom = jnp.sum(expo, axis=0, keepdims=True)
        probs = (expo * (1.0 / denom)).astype(BF16)
        both = mm(values_t[:, :last], probs, NN)
        joined = jnp.concatenate([both[:HEAD_DIM, :rows], both[HEAD_DIM:, rows:]], axis=0)
        o_ref[first:last] = joined.T.astype(BF16)
        lse_ref[0, at : at + 1] = peak + jnp.log(denom)


def attend(length, qkv, heads):
    tokens = qkv.shape[0]
    pairs = heads // 2
    per = qkv.shape[1] // (6 * PAIR)

    def spec(which):
        return pl.BlockSpec(
            (tokens, PAIR), lambda i: (0, (i // per) * 3 * per + which * per + i % per)
        )

    return pl.pallas_call(
        attend_in,
        out_shape=(
            jax.ShapeDtypeStruct((tokens, pairs * PAIR), BF16),
            jax.ShapeDtypeStruct((pairs, 4, tokens // 2), F32),
        ),
        grid=(pairs,),
        in_specs=[SCALARS, spec(0), spec(1), spec(2)],
        out_specs=(
            pl.BlockSpec((tokens, PAIR), lambda i: (0, i)),
            pl.BlockSpec((1, 4, tokens // 2), lambda i: (i, 0, 0)),
        ),
        compiler_params=params(48),
        cost_estimate=work(13),
        name="attend",
    )(length, qkv, qkv, qkv)


def halves(block, width):
    return (
        pl.BlockSpec((block, width), lambda i: (jnp.minimum(i, 1), 0)),
        pl.BlockSpec((block, width), lambda i: (jnp.maximum(i - 2, 0), 0)),
    )


def to_halves(first, second, value):
    @pl.when(pl.program_id(0) < 2)
    def _():
        first[...] = value

    @pl.when(pl.program_id(0) >= 2)
    def _():
        second[...] = value


def of_halves(first, second):
    return jnp.where(pl.program_id(0) < 2, first[...].astype(F32), second[...].astype(F32))


def project_out_in(plan, me_ref, a_ref, *refs):
    weights, (out0, out1, w_scr, sems) = refs[:8], refs[8:]
    n = w_scr.shape[2]
    first = weights[0].shape[2] - n

    @pl.when(pl.program_id(0) == 0)
    def _():
        run(fetch_copies(me_ref, plan, weights, [(first, n)], by_half(w_scr), sems))

    total = mm(a_ref[:, :n], w_scr[0], NT) + mm(a_ref[:, n:], w_scr[1], NT)
    to_halves(out0, out1, total.astype(BF16))


def project_out(me, attended, weights):
    tokens, heads_wide = attended.shape
    half_zs, rows, _ = weights[0].shape
    zs = 2 * half_zs
    width = zs * 2 * rows
    n = heads_wide // 2
    block = tokens // 4
    return pl.pallas_call(
        functools.partial(project_out_in, plan_planes(zs)),
        out_shape=(jax.ShapeDtypeStruct((tokens // 2, width), BF16),) * 2,
        grid=(4,),
        in_specs=[SCALARS, pl.BlockSpec((block, 2 * n), lambda i: (i, 0))] + [ANY] * 8,
        out_specs=halves(block, width),
        scratch_shapes=[pltpu.VMEM((2, width, n), BF16), copy_sems(2 * half_zs, 1)],
        compiler_params=params(32),
        cost_estimate=work(5),
        name="project_out",
    )(me, attended, *weights)


def norm_second_in(x_ref, own0, own1, recv0, recv1, gain_ref, h_ref, n_ref):
    hidden = x_ref[...].astype(F32) + (of_halves(own0, own1) + of_halves(recv0, recv1))
    h_ref[...] = hidden
    rstd = lax.rsqrt(jnp.mean(hidden * hidden, axis=1, keepdims=True) + EPSILON)
    n_ref[...] = (hidden * rstd * gain_ref[...].astype(F32)).astype(BF16)


def norm_second(x, own, recv, gain):
    tokens, width = x.shape
    row = pl.BlockSpec((tokens // 4, width), lambda i: (i, 0))
    pair = halves(tokens // 4, width)
    return pl.pallas_call(
        norm_second_in,
        out_shape=(
            jax.ShapeDtypeStruct((tokens, width), F32),
            jax.ShapeDtypeStruct((tokens, width), BF16),
        ),
        grid=(4,),
        in_specs=[row, *pair, *pair, pl.BlockSpec((1, width), lambda i: (0, 0))],
        out_specs=(row, row),
        compiler_params=params(40),
        cost_estimate=work(4),
        name="norm_second",
    )(x, *own, *recv, gain)


def mlp_in(plan, back_plan, me_ref, n_hbm, m_hbm, *refs):
    count, back_count = len(plan), len(back_plan)
    weights, act_hbm = refs[:count], refs[count]
    outs = refs[count + 1 : count + 1 + back_count]
    n_ref, m_ref, w_scr, acts, staged, load_sems, sems, act_sems, out_sems = refs[
        count + 1 + back_count :
    ]
    n = w_scr.shape[2]
    parts = [(at * n // 2, n // 2) for at in range(3)]
    load_n = [pltpu.make_async_copy(n_hbm, n_ref, load_sems.at[0])]
    load_m = [pltpu.make_async_copy(m_hbm, m_ref, load_sems.at[1])]
    fetch = fetch_copies(me_ref, plan, weights, parts, by_part(w_scr), sems)
    emit = emit_copies(me_ref, back_plan, outs, parts, by_part(staged), out_sems)
    keep = [
        [pltpu.make_async_copy(acts.at[at], act_hbm.at[at], act_sems.at[at])] for at in range(3)
    ]
    for copies in (load_n, fetch[0], fetch[1], load_m, fetch[2]):
        start(copies)
    for lo in range(0, n, 256):
        cut = slice(lo, lo + 256)
        if lo == 0:
            wait(load_n + fetch[0])
        gate = mm(n_ref[...], w_scr[0, :, cut], NN)
        if lo == 0:
            wait(fetch[1])
        up = mm(n_ref[...], w_scr[1, :, cut], NN)
        if lo == 0:
            wait(load_m + fetch[2])
        grad_hidden = mm(m_ref[...], w_scr[2, :, cut], NN)
        sig = 0.5 * jnp.tanh(0.5 * gate) + 0.5
        act = gate * sig
        acts[2, :, cut] = (act * up).astype(BF16)
        acts[0, :, cut] = (grad_hidden * up * (sig * (1.0 + gate * (1.0 - sig)))).astype(BF16)
        acts[1, :, cut] = (grad_hidden * act).astype(BF16)
    for at in range(3):
        start(keep[at])
        staged[at] = mm((n_ref if at < 2 else m_ref)[...], acts[at], TN).astype(BF16)
        start(emit[at])
    for at in range(3):
        wait(keep[at] + emit[at])


def mlp(me, normed, grad_mixed, weights, zs, plan, back_plan):
    tokens, width = normed.shape
    _, rows, n3 = weights[0].shape
    n = 2 * n3 // 3
    pieces = tuple(jax.ShapeDtypeStruct((len(p), rows, n3), BF16) for p in back_plan)
    return pl.pallas_call(
        functools.partial(mlp_in, plan, back_plan),
        out_shape=(jax.ShapeDtypeStruct((3, tokens, n), BF16),) + pieces,
        in_specs=[SCALARS, ANY, ANY] + [ANY] * len(plan),
        out_specs=(ANY,) * (1 + len(pieces)),
        scratch_shapes=[
            pltpu.VMEM((tokens, width), BF16),
            pltpu.VMEM((tokens, width), BF16),
            pltpu.VMEM((3, width, n), BF16),
            pltpu.VMEM((3, tokens, n), BF16),
            pltpu.VMEM((3, width, n), BF16),
            pltpu.SemaphoreType.DMA((2,)),
            copy_sems(zs, 3),
            pltpu.SemaphoreType.DMA((3,)),
            copy_sems(zs, 3),
        ],
        compiler_params=vmem(60),
        cost_estimate=work(20),
        name="mlp",
    )(me, normed, grad_mixed, *weights)


def contract_in(plans, used, me_ref, a0, a1, *refs):
    count = len(plans[0])
    weights = (refs[:count], refs[count : count + len(plans[1])])
    outs, (acts, w_scr, total, staged, act_sems, sems, out_sems) = (
        refs[count + len(plans[1]) : -7],
        refs[-7:],
    )
    n = w_scr.shape[3]
    steps = []
    for chunk, source in enumerate((a0, a1)):
        fetch = fetch_copies(
            me_ref, plans[chunk], weights[chunk], [(p * n // 2, n // 2) for p in used],
            by_part(w_scr.at[chunk]), sems.at[chunk],
        )
        for at, part in enumerate(used):
            load = pltpu.make_async_copy(
                source.at[part], acts.at[chunk, at], act_sems.at[chunk, at]
            )
            steps.append((chunk, at, [load] + fetch[at]))
    for _, _, copies in steps:
        start(copies)
    tokens = acts.shape[2]
    half = tokens // 2
    for index, (chunk, at, copies) in enumerate(steps):
        wait(copies)
        if index < len(steps) - 1:
            product = mm(acts[chunk, at], w_scr[chunk, at], NT)
            total[...] = product if index == 0 else total[...] + product
    emits = []
    chunk, at, _ = steps[-1]
    for side in range(2):
        rows = pl.ds(side * half, half)
        product = total[rows] + mm(acts[chunk, at, rows], w_scr[chunk, at], NT)
        staged[side] = product.astype(BF16)
        emits.append(pltpu.make_async_copy(staged.at[side], outs[side], out_sems.at[side]))
        emits[-1].start()
    wait(emits)


def contract(me, acts, weights, zs, plans, used, name, micros):
    _, tokens, n = acts[0].shape
    _, rows, n3 = weights[0][0].shape
    width = zs * 2 * rows
    count = len(plans[0]) + len(plans[1])
    shape = jax.ShapeDtypeStruct((tokens // 2, width), BF16)
    return pl.pallas_call(
        functools.partial(contract_in, plans, used),
        out_shape=(shape, shape),
        in_specs=[SCALARS, ANY, ANY] + [ANY] * count,
        out_specs=(ANY, ANY),
        scratch_shapes=[
            pltpu.VMEM((2, len(used), tokens, n), BF16),
            pltpu.VMEM((2, len(used), width, n), BF16),
            pltpu.VMEM((tokens, width), F32),
            pltpu.VMEM((2, tokens // 2, width), BF16),
            pltpu.SemaphoreType.DMA((2, len(used))),
            pltpu.SemaphoreType.DMA((2, len(used), 2, 2, zs)),
            pltpu.SemaphoreType.DMA((2,)),
        ],
        compiler_params=vmem(48),
        cost_estimate=work(micros),
        name=name,
    )(me, *acts, *weights[0], *weights[1])


def scatter_lanes(me, value, full, stay_ref, leave_ref):
    slab = stay_ref.shape[2]
    full[...] = value
    for py in range(2):
        for ref, pc in ((stay_ref, 0), (leave_ref, 1)):
            at = (me[2] ^ py) * 2 + (me[3] ^ pc)
            ref[py] = full[:, pl.ds(pl.multiple_of(at * slab, slab), slab)]


def finish_in(me_ref, len_ref, h_ref, own0, own1, recv_ref, stay_ref, leave_ref, full):
    own = jnp.where(me_ref[3] == 0, own0[...].astype(F32), own1[...].astype(F32))
    total = h_ref[...] + (own + recv_ref[...].astype(F32))
    tokens = total.shape[0]
    at = lax.broadcasted_iota(jnp.int32, total.shape, 0) + me_ref[3] * tokens
    total = jnp.where(at < len_ref[0], total, 0.0)
    scatter_lanes(me_ref, total.astype(BF16), full, stay_ref, leave_ref)


def finish(me, length, hidden, own, recv, slab):
    half, width = recv.shape
    part = pl.BlockSpec((2, half, slab), lambda i, m, n: (0, 0, 0))
    mine = pl.BlockSpec((half, width), lambda i, m, n: (m[3], 0))
    row = pl.BlockSpec((half, width), lambda i, m, n: (0, 0))
    shape = jax.ShapeDtypeStruct((2, half, slab), BF16)
    return pl.pallas_call(
        finish_in,
        out_shape=(shape, shape),
        grid_spec=pltpu.PrefetchScalarGridSpec(
            num_scalar_prefetch=2,
            grid=(1,),
            in_specs=[mine, row, row, row],
            out_specs=(part, part),
            scratch_shapes=[pltpu.VMEM((half, width), BF16)],
        ),
        compiler_params=params(40),
        cost_estimate=work(3),
        name="finish",
    )(me, length, hidden, *own, recv)


def norm_second_back_in(
    h_ref, own0, own1, recv0, recv1, gm_ref, gain_ref, gh_ref, gb_ref
):
    hidden = h_ref[...]
    width = hidden.shape[1]
    rstd = lax.rsqrt(jnp.mean(hidden * hidden, axis=1, keepdims=True) + EPSILON)
    grad = of_halves(own0, own1) + of_halves(recv0, recv1)
    weighted = grad * gain_ref[...].astype(F32)
    stat = jnp.sum(weighted * hidden, axis=1, keepdims=True)
    grad_h = (
        gm_ref[...].astype(F32)
        + rstd * weighted
        - hidden * (rstd * rstd * rstd * stat / width)
    )
    gh_ref[...] = grad_h
    gb_ref[...] = grad_h.astype(BF16)


def norm_second_back(hidden, own, recv, grad_mixed, gain):
    tokens, width = hidden.shape
    row = pl.BlockSpec((tokens // 4, width), lambda i: (i, 0))
    one = pl.BlockSpec((1, width), lambda i: (0, 0))
    pair = halves(tokens // 4, width)
    return pl.pallas_call(
        norm_second_back_in,
        out_shape=(
            jax.ShapeDtypeStruct((tokens, width), F32),
            jax.ShapeDtypeStruct((tokens, width), BF16),
        ),
        grid=(4,),
        in_specs=[row, *pair, *pair, row, one],
        out_specs=(row, row),
        compiler_params=params(40),
        cost_estimate=work(5),
        name="norm_second_back",
    )(hidden, *own, *recv, grad_mixed, gain)


def out_back_in(plan, back_plan, me_ref, gb_hbm, a_hbm, *refs):
    count = len(plan)
    weights, ga_hbm, outs = refs[:count], refs[count], refs[count + 1 : count + 3]
    gb_ref, a_ref, ga_ref, w_scr, staged, load_sems, sems, out_sems = refs[count + 3 :]
    n = w_scr.shape[2]
    first = weights[0].shape[2] - n
    (fetch,) = fetch_copies(me_ref, plan, weights, [(first, n)], by_half(w_scr), sems)
    (emit,) = emit_copies(me_ref, back_plan, outs, [(0, n)], by_half(staged), out_sems)
    load_gb = [pltpu.make_async_copy(gb_hbm, gb_ref, load_sems.at[0])]
    load_a = [pltpu.make_async_copy(a_hbm, a_ref, load_sems.at[1])]
    keep = [pltpu.make_async_copy(ga_ref, ga_hbm, load_sems.at[2])]
    for copies in (load_gb, fetch, load_a):
        start(copies)
    wait(load_gb + fetch)
    for half in range(2):
        ga_ref[:, half * n : (half + 1) * n] = mm(gb_ref[...], w_scr[half], NN).astype(BF16)
    start(keep)
    wait(load_a)
    for half in range(2):
        cut = slice(half * n, (half + 1) * n)
        staged[half] = mm(gb_ref[...], a_ref[:, cut], TN).astype(BF16)
    start(emit)
    wait(keep + emit)


def out_back(me, grad_branch, attended, weights):
    tokens, width = grad_branch.shape
    heads_wide = attended.shape[1]
    half_zs, rows, _ = weights[0].shape
    zs = 2 * half_zs
    n = heads_wide // 2
    piece = jax.ShapeDtypeStruct((2 * zs, rows, n), BF16)
    return pl.pallas_call(
        functools.partial(out_back_in, plan_planes(zs), plan_back_lines(zs)),
        out_shape=(jax.ShapeDtypeStruct((tokens, heads_wide), BF16),) + (piece,) * 2,
        in_specs=[SCALARS, ANY, ANY] + [ANY] * len(weights),
        out_specs=(ANY,) * 3,
        scratch_shapes=[
            pltpu.VMEM((tokens, width), BF16),
            pltpu.VMEM((tokens, heads_wide), BF16),
            pltpu.VMEM((tokens, heads_wide), BF16),
            pltpu.VMEM((2, width, n), BF16),
            pltpu.VMEM((2, width, n), BF16),
            pltpu.SemaphoreType.DMA((3,)),
            copy_sems(zs, 1),
            copy_sems(zs, 1),
        ],
        compiler_params=vmem(40),
        cost_estimate=work(5),
        name="out_back",
    )(me, grad_branch, attended, *weights)


def attend_back_in(len_ref, q_ref, k_ref, v_ref, g_ref, lse_ref, gq_ref, gk_ref, gv_ref, *scratch):
    gk_acc, gv_acc = scratch
    tokens = q_ref.shape[0]
    rows = tokens // 4
    scale = HEAD_DIM ** (-0.5)
    length = len_ref[0]
    keys_t = k_ref[...].T
    gk_acc[...] = jnp.zeros_like(gk_acc)
    gv_acc[...] = jnp.zeros_like(gv_acc)
    for at in range(4):
        first, last = at * rows, (at + 1) * rows
        queries = stack_heads(q_ref[first:last] * jnp.asarray(scale, BF16))
        grads = stack_heads(g_ref[first:last])
        scores = masked_scores(length, k_ref[:last], queries, first)
        probs = jnp.exp(scores - lse_ref[0, at : at + 1])
        grad_probs = mm(v_ref[:last], grads, NT)
        inner = jnp.sum(probs * grad_probs, axis=0, keepdims=True)
        grad_scores = (probs * (grad_probs - inner)).astype(BF16)
        both = mm(keys_t[:, :last], grad_scores, NN)
        joined = jnp.concatenate([both[:HEAD_DIM, :rows], both[HEAD_DIM:, rows:]], axis=0)
        gq_ref[first:last] = (joined.T * scale).astype(BF16)
        gk_acc[:last] += mm(grad_scores, queries, NN)
        gv_acc[:last] += mm(probs.astype(BF16), grads, NN)
    gk_ref[...] = gk_acc[...].astype(BF16)
    gv_ref[...] = gv_acc[...].astype(BF16)


def attend_back(length, qkv, grad_attended, lse, half):
    tokens = qkv.shape[0]
    per = lse.shape[0] // 2

    def spec(which):
        return pl.BlockSpec((tokens, PAIR), lambda i: (0, half * 3 * per + which * per + i))

    out = pl.BlockSpec((tokens, PAIR), lambda i: (0, i))
    shape = jax.ShapeDtypeStruct((tokens, per * PAIR), BF16)
    return pl.pallas_call(
        attend_back_in,
        out_shape=(shape, shape, shape),
        grid=(per,),
        in_specs=[
            SCALARS,
            spec(0),
            spec(1),
            spec(2),
            pl.BlockSpec((tokens, PAIR), lambda i: (0, half * per + i)),
            pl.BlockSpec((1, 4, tokens // 2), lambda i: (half * per + i, 0, 0)),
        ],
        out_specs=(out, out, out),
        scratch_shapes=[pltpu.VMEM((tokens, PAIR), F32), pltpu.VMEM((tokens, PAIR), F32)],
        compiler_params=params(56),
        cost_estimate=work(11),
        name="attend_back",
    )(length, qkv, qkv, qkv, grad_attended, lse)


def weight_back_in(back_plan, me_ref, gq, gk, gv, n_hbm, *refs):
    count = len(back_plan)
    outs, (grad, n_ref, staged, load_sems, out_sems) = refs[:count], refs[count:]
    columns = staged.shape[1]
    n = columns // 3
    loads = [
        pltpu.make_async_copy(ref, grad.at[:, pl.ds(at * n, n)], load_sems.at[at])
        for at, ref in enumerate((gq, gk, gv))
    ] + [pltpu.make_async_copy(n_hbm, n_ref, load_sems.at[3])]
    (emit,) = emit_copies(
        me_ref, back_plan, outs, [(0, columns)], lambda at, half, rows: staged.at[rows, :], out_sems
    )
    start(loads)
    wait(loads)
    staged[...] = mm(n_ref[...], grad[...], TN).astype(BF16)
    start(emit)
    wait(emit)


def weight_back(me, grads, normed, zs, half):
    tokens, width = normed.shape
    columns = 3 * grads[0].shape[1]
    back_plan = [p for p in plan_back_planes(zs) if p[0][0] == half]
    if half == 0:
        back_plan = back_plan[:1] + [back_plan[1][: zs // 2], back_plan[1][zs // 2 :]]
    pieces = tuple(
        jax.ShapeDtypeStruct((len(p), width // (2 * zs), columns), BF16) for p in back_plan
    )
    return pl.pallas_call(
        functools.partial(weight_back_in, back_plan),
        out_shape=pieces,
        in_specs=[SCALARS] + [ANY] * 4,
        out_specs=(ANY,) * len(pieces),
        scratch_shapes=[
            pltpu.VMEM((tokens, columns), BF16),
            pltpu.VMEM((tokens, width), BF16),
            pltpu.VMEM((width, columns), BF16),
            pltpu.SemaphoreType.DMA((4,)),
            copy_sems(zs, 1),
        ],
        compiler_params=vmem(40),
        cost_estimate=work(4),
        name="weight_back",
    )(me, *grads, normed)


def qkv_back_in(plan, me_ref, *refs):
    grads, weights, outs = refs[:6], refs[6 : 6 + len(plan)], refs[6 + len(plan) : 8 + len(plan)]
    grad, w_scr, staged, load_sems, sems, out_sems = refs[8 + len(plan) :]
    columns = w_scr.shape[2]
    n = columns // 3
    loads = [
        pltpu.make_async_copy(
            ref, grad.at[at // 3, :, pl.ds(at % 3 * n, n)], load_sems.at[at]
        )
        for at, ref in enumerate(grads)
    ]
    (fetch,) = fetch_copies(me_ref, plan, weights, [(0, columns)], by_half(w_scr), sems)
    copies = [fetch[: len(fetch) // 2] + loads[:3], fetch[len(fetch) // 2 :] + loads[3:]]
    start(copies[0])
    start(copies[1])
    half = staged.shape[1]
    wait(copies[0])
    first = mm(grad[0], w_scr[0], NT)
    wait(copies[1])
    staged[0] = (first[:half] + mm(grad[1, :half], w_scr[1], NT)).astype(BF16)
    staged[1] = (first[half:] + mm(grad[1, half:], w_scr[1], NT)).astype(BF16)
    emit = [
        pltpu.make_async_copy(staged.at[me_ref[3]], outs[0], out_sems.at[0]),
        pltpu.make_async_copy(staged.at[1 - me_ref[3]], outs[1], out_sems.at[1]),
    ]
    start(emit)
    wait(emit)


def qkv_back(me, grads, weights, columns):
    tokens, n = grads[0].shape
    half_zs, rows, _ = weights[0].shape
    zs = 2 * half_zs
    width = zs * 2 * rows
    plan = plan_planes(zs)
    shape = jax.ShapeDtypeStruct((tokens // 2, width), BF16)
    return pl.pallas_call(
        functools.partial(qkv_back_in, plan),
        out_shape=(shape, shape),
        in_specs=[SCALARS] + [ANY] * (6 + len(plan)),
        out_specs=(ANY, ANY),
        scratch_shapes=[
            pltpu.VMEM((2, tokens, columns), BF16),
            pltpu.VMEM((2, width, columns), BF16),
            pltpu.VMEM((2, tokens // 2, width), BF16),
            pltpu.SemaphoreType.DMA((6,)),
            copy_sems(zs, 1),
            pltpu.SemaphoreType.DMA((2,)),
        ],
        compiler_params=vmem(48),
        cost_estimate=work(6),
        name="qkv_back",
    )(me, *grads, *weights)


def norm_first_back_in(
    me_ref, x_ref, own_ref, recv_ref, gh_ref, gain_ref, stay_ref, leave_ref, full
):
    x = x_ref[...].astype(F32)
    width = x.shape[1]
    rstd = lax.rsqrt(jnp.mean(x * x, axis=1, keepdims=True) + EPSILON)
    grad = own_ref[...].astype(F32) + recv_ref[...].astype(F32)
    weighted = grad * gain_ref[...].astype(F32)
    stat = jnp.sum(weighted * x, axis=1, keepdims=True)
    gx = gh_ref[...] + rstd * weighted - x * (rstd * rstd * rstd * stat / width)
    scatter_lanes(me_ref, gx.astype(BF16), full, stay_ref, leave_ref)


def norm_first_back(me, x, own, recv, grad_h, gain, slab):
    half, width = own.shape
    part = pl.BlockSpec((2, half, slab), lambda i, m: (0, 0, 0))
    mine = pl.BlockSpec((half, width), lambda i, m: (m[3], 0))
    row = pl.BlockSpec((half, width), lambda i, m: (0, 0))
    one = pl.BlockSpec((1, width), lambda i, m: (0, 0))
    shape = jax.ShapeDtypeStruct((2, half, slab), BF16)
    return pl.pallas_call(
        norm_first_back_in,
        out_shape=(shape, shape),
        grid_spec=pltpu.PrefetchScalarGridSpec(
            num_scalar_prefetch=1,
            grid=(1,),
            in_specs=[mine, row, row, mine, one],
            out_specs=(part, part),
            scratch_shapes=[pltpu.VMEM((half, width), BF16)],
        ),
        compiler_params=params(40),
        cost_estimate=work(4),
        name="norm_first_back",
    )(me, x, own, recv, grad_h, gain)


def shards(
    patches,
    w_query,
    w_key,
    w_value,
    w_out,
    w_gate,
    w_up,
    w_down,
    gain_attn,
    gain_mlp,
    lengths,
    cotangent,
):
    slab = patches.shape[1]
    rows_axis, cols_axis = lax.axis_size("row"), lax.axis_size("col")
    width = slab * cols_axis
    micro = lengths.shape[0]
    seq = patches.shape[0] // micro
    zs = rows_axis // 2
    row, col = lax.axis_index("row"), lax.axis_index("col")
    z, x, y, c = row // 2, row % 2, col // 2, col % 2
    me = jnp.stack([z, x, y, c]).astype(jnp.int32)
    heads_here = w_query.shape[1]
    columns = 3 * heads_here

    def swap(value, axis, bit):
        size = lax.axis_size(axis)
        return lax.ppermute(value, axis, [(i, i ^ bit) for i in range(size)])

    sent = {"x": [], "y": [], "z": [], "c": []}
    depth = {"x": 2, "y": 2, "z": 2, "c": 2}
    bits = {"x": ("row", 1), "y": ("col", 2), "c": ("col", 1)}

    def send(value, link, bit=None):
        axis, one = bits.get(link, ("row", bit))
        queue = sent[link]
        if len(queue) >= depth[link]:
            value = lax.optimization_barrier((value, queue[-depth[link]]))[0]
        out = swap(value, axis, one)
        queue.append(out)
        return out

    def gather_z(shard, *done):
        near, bit = shard[None], zs // 2
        while bit > 1:
            near = jnp.concatenate([near, tie(send(near, "z", 2 * bit), *done)])
            bit //= 2
        return near, send(near, "z", 2)

    def tie(value, *done):
        return lax.optimization_barrier((value, *done))[0]

    def order_rows(both):
        owned = [0]
        for bit in [1] + [2 * (zs >> k) for k in range(1, zs.bit_length())]:
            owned += [at ^ bit for at in owned]
        ordered = [jnp.zeros_like(both[0])] * rows_axis
        for at, rel in enumerate(owned):
            ordered = [jnp.where((row ^ rel) == k, both[at], o) for k, o in enumerate(ordered)]
        return jnp.concatenate(ordered, axis=1)

    def add(*values):
        total = values[0].astype(F32)
        for value in values[1:]:
            total = total + value.astype(F32)
        return total

    def leave_z(pieces):
        return add(*(p[zs // 2 :] for p in pieces)).astype(BF16)

    def keep_z(pieces, come):
        return add(*(p[: zs // 2] for p in pieces), come)

    def next_z(total, bit=4):
        count = total.shape[0] // 2
        if not count:
            return total, None, bit
        return total[:count], send(total[count:].astype(BF16), "z", bit), bit

    def last_z(total, come, bit):
        while come is not None:
            total, come, bit = next_z(add(total, come), 2 * bit)
        return total[0]

    def out_x(total):
        count, bit = zs // 4, 8
        while count > 1:
            count //= 2
            come = swap(total[4 * count :].astype(BF16), "row", bit)
            total, bit = add(total[: 4 * count], come), bit * 2
        return total[:2], swap(total[2:].astype(BF16), "row", 1)

    def tie_all(values, *done):
        return lax.optimization_barrier((tuple(values), done))[0]

    def pick(flag, one, other):
        return jnp.where(flag == 0, one, other)

    def split_micro(value):
        both = value.reshape(micro, seq, slab)
        mine = lax.dynamic_index_in_dim(both, y, 0, keepdims=False)
        return mine, lax.dynamic_index_in_dim(both, 1 - y, 0, keepdims=False)

    def spread(mine, theirs):
        theirs = send(theirs, "y")
        pair = jnp.stack([mine, theirs])
        other = send(pair, "c")
        blocks = [
            pick(
                y ^ yy,
                pick(c ^ cc, pair[0], other[0]),
                pick(c ^ cc, pair[1], other[1]),
            )
            for yy in range(2)
            for cc in range(2)
        ]
        return jnp.concatenate(blocks, axis=1), theirs

    def unspread_start(stay, leave):
        come = swap(leave, "col", 1)
        return stay, come, swap(jnp.stack([stay[1], come[1]]), "col", 2)

    def unspread_finish(stay, come, got):
        return jnp.concatenate(
            [
                pick(
                    y ^ at,
                    pick(c ^ side, stay[0], come[0]),
                    pick(c ^ side, got[0], got[1]),
                )
                for at in range(2)
                for side in range(2)
            ],
            axis=0,
        )

    inner = w_gate.shape[1]
    padded = -(-inner // 256) * 256
    chunk = padded // 2
    pad = ((0, 0), (0, padded - inner))
    attn_shard = jnp.concatenate([w_query, w_key, w_value, w_out.T], axis=1)
    gate_up_down = [jnp.pad(w_gate, pad), jnp.pad(w_up, pad), jnp.pad(w_down.T, pad)]
    mlp_shards = [
        jnp.concatenate([w[:, at * chunk : (at + 1) * chunk] for w in gate_up_down], axis=1)
        for at in range(2)
    ]
    gain_parts = jnp.stack([gain_attn, gain_mlp])[None]
    gain_parts = jnp.concatenate([gain_parts, swap(gain_parts, "row", 1)])
    patches_mine, patches_other = split_micro(patches)
    bit = zs // 2
    while bit:
        gain_parts = jnp.concatenate([gain_parts, swap(gain_parts, "row", 2 * bit)])
        bit //= 2
    near, bit = tie(attn_shard, patches_other, gain_parts)[None], zs // 2
    while bit > 1:
        near = jnp.concatenate([near, send(near, "z", 2 * bit)])
        bit //= 2
    a0, a1 = near, send(near, "z", 2)
    gains = order_rows(gain_parts)
    attn_gain, mlp_gain = gains[0:1], gains[1:2]
    x_all, x_half = spread(patches_mine, patches_other)
    cotangent_all, cotangent_half = spread(*split_micro(cotangent))
    b0, c0 = send(a0, "x"), send(a0, "y")
    b1, c1 = send(tie(a1, b0), "x"), send(tie(a1, c0), "y")
    d0, d1 = send(tie(c0, b1), "x"), send(b1, "y")
    attn_w = (a0, a1, b0, b1, c0, c1, d0, d1)
    e0, e1 = gather_z(tie(mlp_shards[0], a1), b1)
    one_near = jnp.concatenate([e0, e1])
    two_near = jnp.concatenate(gather_z(tie(mlp_shards[1], e1)))
    f, g = swap(tie(one_near, d0), "row", 1), swap(tie(one_near, d1), "col", 2)

    length = lax.dynamic_slice_in_dim(lengths, y, 1)
    grad_mixed = jnp.where(
        lax.iota(jnp.int32, seq)[:, None] < length, cotangent_all, jnp.zeros((), BF16)
    )

    back_plan = plan_back_planes(zs)
    plans = (plan_wholes(zs),) * 2
    normed_one = norm_first(x_all, attn_gain)
    qkv = project_qkv(me, tie(normed_one, one_near), attn_w, columns)
    attended, lse = attend(length, qkv, 2 * heads_here // HEAD_DIM)
    g_lo, f_hi = tie_all((g[: zs // 2], f[zs // 2 :]), attended)
    one_w = (one_near, f, g, swap(g_lo, "row", 1), swap(f_hi, "col", 2))
    branch = project_out(me, tie(attended, g_lo, f_hi), attn_w)
    f, g = swap(tie(two_near, one_w[3]), "row", 1), swap(tie(two_near, one_w[4]), "col", 2)
    hidden, normed_two = norm_second(
        x_all, branch, [send(tie(v, *one_w[3:], two_near, grad_mixed), "c") for v in branch], mlp_gain
    )

    act_one, *grad_one = mlp(
        me, normed_two, grad_mixed, one_w, zs, plans[0], back_plan
    )
    g00, g01, g10, g11 = grad_one
    f, g = tie_all((f, g), act_one)
    two_w = (two_near, f, g, swap(g[: zs // 2], "row", 1), swap(f[zs // 2 :], "col", 2))
    far_one = send(g11, "x")
    act_two, *grad_two = mlp(
        me, tie(normed_two, act_one), grad_mixed, two_w, zs, plans[1], back_plan
    )
    h00, h01, h10, h11 = grad_two
    far_two = send(h11, "y")
    side_one = send(tie(g01, act_two), "x")
    weights = (one_w, two_w)
    acts = (act_one, act_two)
    back_two = contract(me, acts, weights, zs, plans, (0, 1), "mlp_back", 9)
    back_recv = [send(v, "c") for v in back_two]
    over_one = add(*tie_all((g10, far_one), back_two[0])).astype(BF16)
    acts = (act_one, tie(act_two, over_one))
    mixed = contract(me, acts, weights, zs, plans, (2,), "mlp_out", 6)
    over_one = send(over_one, "y")
    grad_h, grad_branch = norm_second_back(
        tie(hidden, mixed[0]), back_two, back_recv, grad_mixed, mlp_gain
    )
    mixed_recv = send(tie(pick(c, mixed[1], mixed[0]), grad_branch), "c")
    side_two = send(h10, "y")
    over_two = add(*tie_all((h01, far_two), grad_branch)).astype(BF16)

    grad_attended, o0, o1 = out_back(me, tie(grad_branch, over_two), attended, attn_w)
    over_two = send(over_two, "x")
    finished = finish(me, length, tie(hidden, grad_attended), mixed, mixed_recv, slab)
    leave_out = send(o1, "z", 2)
    grads = attend_back(length, qkv, tie(grad_attended, finished[0]), lse, 1)
    first_one = leave_z(tie_all((g00, side_one, over_one), grads[0]))
    finished = tie_all(finished, grads[0])
    output_sent = unspread_start(*finished)
    other_grads = grads
    p10, p11 = weight_back(
        me, (tie(grads[0], first_one, leave_out), *grads[1:]), normed_one, zs, 1
    )
    far_qkv = send(p11, "x")
    first_one = send(first_one, "z", 2)
    out_sum = add(*tie_all((o0, leave_out), p10))
    keep_out, leave_out = out_sum[:zs], out_sum[zs:].astype(BF16)
    pieces = tie_all((h00, side_two, over_two), p10)
    leave_two = leave_z(pieces)
    grads = attend_back(
        length, qkv, tie(grad_attended, p10, leave_out, leave_two), lse, 0
    )
    out_come = swap(leave_out, "row", 4)
    two_come = swap(leave_two, "row", 2)
    sum_one = next_z(keep_z((g00, side_one, over_one), tie(first_one, grads[0])))
    count = zs // 2
    p10, far_qkv = tie_all((p10, far_qkv), grads[0])
    over_hi = add(p10[count:], far_qkv[count:]).astype(BF16)
    over_lo = add(p10[:count], far_qkv[:count]).astype(BF16)
    out_sum = add(keep_out, tie(out_come, grads[0]))
    sum_two = keep_z(pieces, tie(two_come, grads[0]))
    out_sum, out_come = out_x(out_sum)
    p00, side_lo, side_hi = weight_back(
        me, (tie(grads[0], over_hi, over_lo, sum_two, output_sent[2]), *grads[1:]),
        normed_one, zs, 0
    )
    over_hi = swap(over_hi, "col", 2)
    over_lo = swap(over_lo, "col", 2)
    side_hi, side_lo = swap(side_hi, "row", 1), swap(side_lo, "row", 1)
    sum_two = next_z(sum_two)
    out_sum = add(out_sum, tie(out_come, p00))
    back_own, back_other = qkv_back(
        me, (tie(grads[0], p00, out_sum), *grads[1:], *other_grads), attn_w, columns
    )
    out_come = swap(out_sum[1].astype(BF16), "col", 2)
    grad_x = norm_first_back(
        me, tie(x_all, over_hi, side_hi), back_own, send(back_other, "c"), grad_h, attn_gain, slab
    )
    patches_sent = unspread_start(*grad_x)
    leave_qkv = add(p00[count:], over_hi, side_hi).astype(BF16)
    come_qkv = swap(leave_qkv, "row", 2)

    out_grad = add(out_sum[0], tie(out_come, come_qkv))
    output = unspread_finish(*tie_all(output_sent, leave_qkv))
    sum_one = last_z(sum_one[0], tie(sum_one[1], leave_qkv), sum_one[2])
    sum_two = last_z(sum_two[0], tie(sum_two[1], leave_qkv), sum_two[2])
    qkv_sum, qkv_come, bit = next_z(add(p00[:count], over_lo, side_lo, tie(come_qkv, grad_x[0])))
    qkv_grad = last_z(qkv_sum, tie(qkv_come, patches_sent[2]), bit)
    sum_one, sum_two = tie_all((sum_one, sum_two), qkv_sum)
    grad_patches = unspread_finish(*patches_sent).astype(F32)
    mlp_sums = [
        jnp.concatenate([v[:, at * chunk : (at + 1) * chunk] for v in (sum_one, sum_two)], axis=1)[
            :, :inner
        ]
        for at in range(3)
    ]

    def weighed(weights, grads):
        return sum(jnp.sum(w.astype(F32) * g, axis=1) for w, g in zip(weights, grads, strict=True))

    gain_grads = jnp.stack(
        [
            weighed(
                (w_query, w_key, w_value),
                [qkv_grad[:, at * heads_here : (at + 1) * heads_here] for at in range(3)],
            ),
            weighed((w_gate, w_up), mlp_sums[:2]),
        ]
    )
    for bit in (2, 1):
        gain_grads = gain_grads + swap(gain_grads, "col", bit)
    gain_grads = gain_grads / jnp.stack([gain_attn, gain_mlp]).astype(F32)

    return (
        output,
        grad_patches,
        qkv_grad[:, :heads_here],
        qkv_grad[:, heads_here : 2 * heads_here],
        qkv_grad[:, 2 * heads_here :],
        out_grad.T,
        mlp_sums[0],
        mlp_sums[1],
        mlp_sums[2].T,
        gain_grads[0],
        gain_grads[1],
    )


def solution(mesh):
    placed = (
        P("row", "col"),
        P("row", "col"),
        P("row", "col"),
        P("row", "col"),
        P("col", "row"),
        P("row", "col"),
        P("row", "col"),
        P("col", "row"),
        P("row"),
        P("row"),
        P("row"),
        P("row", "col"),
    )
    return jax.shard_map(
        shards,
        mesh=mesh,
        in_specs=placed,
        out_specs=(
            P("row", "col"),
            P("row", "col"),
            P("row", "col"),
            P("row", "col"),
            P("row", "col"),
            P("col", "row"),
            P("row", "col"),
            P("row", "col"),
            P("col", "row"),
            P("row"),
            P("row"),
        ),
        check_vma=False,
    )
```

```python
import functools

import jax
import jax.numpy as jnp
from jax import lax
from jax.experimental import pallas as pl
from jax.experimental.pallas import tpu as pltpu
from jax.sharding import PartitionSpec as P

HEAD_DIM = 64
PAIR = 2 * HEAD_DIM
EPSILON = 1e-06
MASKED = -1000000000.0
BF16 = jnp.bfloat16
F32 = jnp.float32
MIB = 1 << 20

NN = (((1,), (0,)), ((), ()))
NT = (((1,), (1,)), ((), ()))
TN = (((0,), (0,)), ((), ()))

ANY = pl.BlockSpec(memory_space=pltpu.HBM)
SCALARS = pl.BlockSpec(memory_space=pltpu.SMEM)


def mm(left, right, dims):
    return lax.dot_general(left, right, dims, preferred_element_type=F32)


def work(micros, values=0):
    return pl.CostEstimate(
        flops=int(micros * 1.15e9), transcendentals=0, bytes_accessed=int(micros * 1e6) + values
    )


def params(mib):
    return pltpu.CompilerParams(
        dimension_semantics=("arbitrary",), vmem_limit_bytes=mib * MIB
    )


def z_order(zs):
    order, bit = [0], zs // 2
    while bit:
        order += [at ^ bit for at in order]
        bit //= 2
    return order


def plan_planes(zs):
    order, half = z_order(zs), zs // 2
    return [
        [(py, px, pz) for pz in order[lo : lo + half]]
        for py in range(2)
        for px in range(2)
        for lo in (0, half)
    ]


def plan_wholes(zs):
    order, half = z_order(zs), zs // 2
    out = [[(py, px, pz) for pz in order] for py, px in ((0, 0), (0, 1), (1, 0))]
    return out + [[(1, 1, pz) for pz in order[lo : lo + half]] for lo in (0, half)]


def plan_back_planes(zs):
    return [[(py, px, pz) for pz in z_order(zs)] for py in range(2) for px in range(2)]


def plan_back_lines(zs):
    order, half = z_order(zs), zs // 2
    return [
        [(py, px, pz) for pz in order[lo : lo + half] for px in range(2) for py in range(2)]
        for lo in (0, half)
    ]


def block_copies(me, plan, buffers, parts, scratch_of, sems, out):
    rows = buffers[0].shape[1]
    copies = [[] for _ in parts]
    for blocks, buffer in zip(plan, buffers, strict=True):
        for at_block, (py, px, pz) in enumerate(blocks):
            owner = ((me[0] ^ pz) * 2) + (me[1] ^ px)
            for at, (first, n) in enumerate(parts):
                remote = buffer.at[at_block, :, pl.ds(first, n)]
                local = scratch_of(at, py, pl.ds(owner * rows, rows))
                ends = (local, remote) if out else (remote, local)
                copies[at].append(pltpu.make_async_copy(*ends, sems.at[at, py, px, pz]))
    return copies


def fetch_copies(me, plan, buffers, parts, scratch_of, sems):
    return block_copies(me, plan, buffers, parts, scratch_of, sems, False)


def emit_copies(me, plan, buffers, parts, scratch_of, sems):
    return block_copies(me, plan, buffers, parts, scratch_of, sems, True)


def copy_sems(zs, parts):
    return pltpu.SemaphoreType.DMA((parts, 2, 2, zs))


def start(copies):
    for copy in copies:
        copy.start()


def wait(copies):
    for copy in copies:
        copy.wait()


def run(parts):
    for copies in parts:
        start(copies)
    for copies in parts:
        wait(copies)


def vmem(mib):
    return pltpu.CompilerParams(vmem_limit_bytes=mib * MIB)


def norm_in(x_ref, gain_ref, n_ref):
    x = x_ref[...].astype(F32)
    rstd = lax.rsqrt(jnp.mean(x * x, axis=1, keepdims=True) + EPSILON)
    n_ref[...] = (x * rstd * gain_ref[...].astype(F32)).astype(BF16)


def norm_first(x, gain):
    tokens, width = x.shape
    block = tokens // 4
    row = pl.BlockSpec((block, width), lambda i: (i, 0))
    return pl.pallas_call(
        norm_in,
        out_shape=jax.ShapeDtypeStruct((tokens, width), BF16),
        grid=(4,),
        in_specs=[row, pl.BlockSpec((1, width), lambda i: (0, 0))],
        out_specs=row,
        compiler_params=params(32),
        cost_estimate=work(1),
        name="norm_first",
    )(x, gain)


def by_half(scratch):
    return lambda at, half, rows: scratch.at[half, rows, :]


def by_part(scratch):
    n = scratch.shape[2] // 2
    return lambda at, half, rows: scratch.at[at, rows, pl.ds(half * n, n)]


def project_in(plan, me_ref, n_ref, *refs):
    weights, (out_ref, w_scr, sems) = refs[:8], refs[8:]
    n = w_scr.shape[2]

    @pl.when(pl.program_id(0) == 0)
    def _():
        run(fetch_copies(me_ref, plan, weights, [(0, n)], by_half(w_scr), sems))

    for half in range(2):
        out_ref[:, half * n : (half + 1) * n] = mm(n_ref[...], w_scr[half], NN).astype(BF16)


def project_qkv(me, normed, weights, columns):
    tokens, width = normed.shape
    block = tokens // 4
    zs = 2 * weights[0].shape[0]
    return pl.pallas_call(
        functools.partial(project_in, plan_planes(zs)),
        out_shape=jax.ShapeDtypeStruct((tokens, 2 * columns), BF16),
        grid=(4,),
        in_specs=[SCALARS, pl.BlockSpec((block, width), lambda i: (i, 0))] + [ANY] * 8,
        out_specs=pl.BlockSpec((block, 2 * columns), lambda i: (i, 0)),
        scratch_shapes=[pltpu.VMEM((2, width, columns), BF16), copy_sems(zs, 1)],
        compiler_params=params(32),
        cost_estimate=work(6),
        name="project_qkv",
    )(me, normed, *weights)


def stack_heads(pair):
    lane = lax.broadcasted_iota(jnp.int32, pair.shape, 1)
    zero = jnp.zeros_like(pair)
    return jnp.concatenate(
        [jnp.where(lane < HEAD_DIM, pair, zero), jnp.where(lane < HEAD_DIM, zero, pair)], axis=0
    )


def masked_scores(length, key_rows, queries, first):
    raw = mm(key_rows, queries, NT)
    keys, columns = raw.shape
    rows = columns // 2
    query_at = lax.broadcasted_iota(jnp.int32, (1, columns), 1)
    query_at = first + jnp.where(query_at >= rows, query_at - rows, query_at)
    limit = jnp.minimum(query_at + 1, length)
    return jnp.where(lax.broadcasted_iota(jnp.int32, raw.shape, 0) < limit, raw, MASKED)


def attend_in(len_ref, q_ref, k_ref, v_ref, o_ref, lse_ref):
    tokens = q_ref.shape[0]
    rows = tokens // 4
    scale = HEAD_DIM ** (-0.5)
    length = len_ref[0]
    values_t = v_ref[...].T
    for at in range(4):
        first, last = at * rows, (at + 1) * rows
        queries = stack_heads(q_ref[first:last] * jnp.asarray(scale, BF16))
        scores = masked_scores(length, k_ref[:last], queries, first)
        peak = jnp.max(scores, axis=0, keepdims=True)
        expo = jnp.exp(scores - peak)
        denom = jnp.sum(expo, axis=0, keepdims=True)
        probs = (expo * (1.0 / denom)).astype(BF16)
        both = mm(values_t[:, :last], probs, NN)
        joined = jnp.concatenate([both[:HEAD_DIM, :rows], both[HEAD_DIM:, rows:]], axis=0)
        o_ref[first:last] = joined.T.astype(BF16)
        lse_ref[0, at : at + 1] = peak + jnp.log(denom)


def attend(length, qkv, heads):
    tokens = qkv.shape[0]
    pairs = heads // 2
    per = qkv.shape[1] // (6 * PAIR)

    def spec(which):
        return pl.BlockSpec(
            (tokens, PAIR), lambda i: (0, (i // per) * 3 * per + which * per + i % per)
        )

    return pl.pallas_call(
        attend_in,
        out_shape=(
            jax.ShapeDtypeStruct((tokens, pairs * PAIR), BF16),
            jax.ShapeDtypeStruct((pairs, 4, tokens // 2), F32),
        ),
        grid=(pairs,),
        in_specs=[SCALARS, spec(0), spec(1), spec(2)],
        out_specs=(
            pl.BlockSpec((tokens, PAIR), lambda i: (0, i)),
            pl.BlockSpec((1, 4, tokens // 2), lambda i: (i, 0, 0)),
        ),
        compiler_params=params(48),
        cost_estimate=work(13),
        name="attend",
    )(length, qkv, qkv, qkv)


def halves(block, width):
    return (
        pl.BlockSpec((block, width), lambda i: (jnp.minimum(i, 1), 0)),
        pl.BlockSpec((block, width), lambda i: (jnp.maximum(i - 2, 0), 0)),
    )


def to_halves(first, second, value):
    @pl.when(pl.program_id(0) < 2)
    def _():
        first[...] = value

    @pl.when(pl.program_id(0) >= 2)
    def _():
        second[...] = value


def of_halves(first, second):
    return jnp.where(pl.program_id(0) < 2, first[...].astype(F32), second[...].astype(F32))


def project_out_in(plan, me_ref, a_ref, *refs):
    weights, (out0, out1, w_scr, sems) = refs[:8], refs[8:]
    n = w_scr.shape[2]
    first = weights[0].shape[2] - n

    @pl.when(pl.program_id(0) == 0)
    def _():
        run(fetch_copies(me_ref, plan, weights, [(first, n)], by_half(w_scr), sems))

    total = mm(a_ref[:, :n], w_scr[0], NT) + mm(a_ref[:, n:], w_scr[1], NT)
    to_halves(out0, out1, total.astype(BF16))


def project_out(me, attended, weights):
    tokens, heads_wide = attended.shape
    half_zs, rows, _ = weights[0].shape
    zs = 2 * half_zs
    width = zs * 2 * rows
    n = heads_wide // 2
    block = tokens // 4
    return pl.pallas_call(
        functools.partial(project_out_in, plan_planes(zs)),
        out_shape=(jax.ShapeDtypeStruct((tokens // 2, width), BF16),) * 2,
        grid=(4,),
        in_specs=[SCALARS, pl.BlockSpec((block, 2 * n), lambda i: (i, 0))] + [ANY] * 8,
        out_specs=halves(block, width),
        scratch_shapes=[pltpu.VMEM((2, width, n), BF16), copy_sems(2 * half_zs, 1)],
        compiler_params=params(32),
        cost_estimate=work(5),
        name="project_out",
    )(me, attended, *weights)


def norm_second_in(x_ref, own0, own1, recv0, recv1, gain_ref, h_ref, n_ref):
    hidden = x_ref[...].astype(F32) + (of_halves(own0, own1) + of_halves(recv0, recv1))
    h_ref[...] = hidden
    rstd = lax.rsqrt(jnp.mean(hidden * hidden, axis=1, keepdims=True) + EPSILON)
    n_ref[...] = (hidden * rstd * gain_ref[...].astype(F32)).astype(BF16)


def norm_second(x, own, recv, gain):
    tokens, width = x.shape
    row = pl.BlockSpec((tokens // 4, width), lambda i: (i, 0))
    pair = halves(tokens // 4, width)
    return pl.pallas_call(
        norm_second_in,
        out_shape=(
            jax.ShapeDtypeStruct((tokens, width), F32),
            jax.ShapeDtypeStruct((tokens, width), BF16),
        ),
        grid=(4,),
        in_specs=[row, *pair, *pair, pl.BlockSpec((1, width), lambda i: (0, 0))],
        out_specs=(row, row),
        compiler_params=params(40),
        cost_estimate=work(4),
        name="norm_second",
    )(x, *own, *recv, gain)


def mlp_in(plan, back_plan, me_ref, n_hbm, m_hbm, *refs):
    count, back_count = len(plan), len(back_plan)
    weights, act_hbm = refs[:count], refs[count]
    outs = refs[count + 1 : count + 1 + back_count]
    n_ref, m_ref, w_scr, acts, staged, load_sems, sems, act_sems, out_sems = refs[
        count + 1 + back_count :
    ]
    n = w_scr.shape[2]
    parts = [(at * n // 2, n // 2) for at in range(3)]
    load_n = [pltpu.make_async_copy(n_hbm, n_ref, load_sems.at[0])]
    load_m = [pltpu.make_async_copy(m_hbm, m_ref, load_sems.at[1])]
    fetch = fetch_copies(me_ref, plan, weights, parts, by_part(w_scr), sems)
    emit = emit_copies(me_ref, back_plan, outs, parts, by_part(staged), out_sems)
    keep = [
        [pltpu.make_async_copy(acts.at[at], act_hbm.at[at], act_sems.at[at])] for at in range(3)
    ]
    for copies in (load_n, fetch[0], fetch[1], load_m, fetch[2]):
        start(copies)
    for lo in range(0, n, 256):
        cut = slice(lo, lo + 256)
        if lo == 0:
            wait(load_n + fetch[0])
        gate = mm(n_ref[...], w_scr[0, :, cut], NN)
        if lo == 0:
            wait(fetch[1])
        up = mm(n_ref[...], w_scr[1, :, cut], NN)
        if lo == 0:
            wait(load_m + fetch[2])
        grad_hidden = mm(m_ref[...], w_scr[2, :, cut], NN)
        sig = 0.5 * jnp.tanh(0.5 * gate) + 0.5
        act = gate * sig
        acts[2, :, cut] = (act * up).astype(BF16)
        acts[0, :, cut] = (grad_hidden * up * (sig * (1.0 + gate * (1.0 - sig)))).astype(BF16)
        acts[1, :, cut] = (grad_hidden * act).astype(BF16)
    for at in range(3):
        start(keep[at])
        staged[at] = mm((n_ref if at < 2 else m_ref)[...], acts[at], TN).astype(BF16)
        start(emit[at])
    for at in range(3):
        wait(keep[at] + emit[at])


def mlp(me, normed, grad_mixed, weights, zs, plan, back_plan):
    tokens, width = normed.shape
    _, rows, n3 = weights[0].shape
    n = 2 * n3 // 3
    pieces = tuple(jax.ShapeDtypeStruct((len(p), rows, n3), BF16) for p in back_plan)
    return pl.pallas_call(
        functools.partial(mlp_in, plan, back_plan),
        out_shape=(jax.ShapeDtypeStruct((3, tokens, n), BF16),) + pieces,
        in_specs=[SCALARS, ANY, ANY] + [ANY] * len(plan),
        out_specs=(ANY,) * (1 + len(pieces)),
        scratch_shapes=[
            pltpu.VMEM((tokens, width), BF16),
            pltpu.VMEM((tokens, width), BF16),
            pltpu.VMEM((3, width, n), BF16),
            pltpu.VMEM((3, tokens, n), BF16),
            pltpu.VMEM((3, width, n), BF16),
            pltpu.SemaphoreType.DMA((2,)),
            copy_sems(zs, 3),
            pltpu.SemaphoreType.DMA((3,)),
            copy_sems(zs, 3),
        ],
        compiler_params=vmem(60),
        cost_estimate=work(20),
        name="mlp",
    )(me, normed, grad_mixed, *weights)


def contract_in(plans, used, me_ref, a0, a1, *refs):
    count = len(plans[0])
    weights = (refs[:count], refs[count : count + len(plans[1])])
    outs, (acts, w_scr, total, staged, act_sems, sems, out_sems) = (
        refs[count + len(plans[1]) : -7],
        refs[-7:],
    )
    n = w_scr.shape[3]
    steps = []
    for chunk, source in enumerate((a0, a1)):
        fetch = fetch_copies(
            me_ref, plans[chunk], weights[chunk], [(p * n // 2, n // 2) for p in used],
            by_part(w_scr.at[chunk]), sems.at[chunk],
        )
        for at, part in enumerate(used):
            load = pltpu.make_async_copy(
                source.at[part], acts.at[chunk, at], act_sems.at[chunk, at]
            )
            steps.append((chunk, at, [load] + fetch[at]))
    for _, _, copies in steps:
        start(copies)
    tokens = acts.shape[2]
    half = tokens // 2
    for index, (chunk, at, copies) in enumerate(steps):
        wait(copies)
        if index < len(steps) - 1:
            product = mm(acts[chunk, at], w_scr[chunk, at], NT)
            total[...] = product if index == 0 else total[...] + product
    emits = []
    chunk, at, _ = steps[-1]
    for side in range(2):
        rows = pl.ds(side * half, half)
        product = total[rows] + mm(acts[chunk, at, rows], w_scr[chunk, at], NT)
        staged[side] = product.astype(BF16)
        emits.append(pltpu.make_async_copy(staged.at[side], outs[side], out_sems.at[side]))
        emits[-1].start()
    wait(emits)


def contract(me, acts, weights, zs, plans, used, name, micros):
    _, tokens, n = acts[0].shape
    _, rows, n3 = weights[0][0].shape
    width = zs * 2 * rows
    count = len(plans[0]) + len(plans[1])
    shape = jax.ShapeDtypeStruct((tokens // 2, width), BF16)
    return pl.pallas_call(
        functools.partial(contract_in, plans, used),
        out_shape=(shape, shape),
        in_specs=[SCALARS, ANY, ANY] + [ANY] * count,
        out_specs=(ANY, ANY),
        scratch_shapes=[
            pltpu.VMEM((2, len(used), tokens, n), BF16),
            pltpu.VMEM((2, len(used), width, n), BF16),
            pltpu.VMEM((tokens, width), F32),
            pltpu.VMEM((2, tokens // 2, width), BF16),
            pltpu.SemaphoreType.DMA((2, len(used))),
            pltpu.SemaphoreType.DMA((2, len(used), 2, 2, zs)),
            pltpu.SemaphoreType.DMA((2,)),
        ],
        compiler_params=vmem(48),
        cost_estimate=work(micros),
        name=name,
    )(me, *acts, *weights[0], *weights[1])


def scatter_lanes(me, value, full, stay_ref, leave_ref):
    slab = stay_ref.shape[2]
    full[...] = value
    for py in range(2):
        for ref, pc in ((stay_ref, 0), (leave_ref, 1)):
            at = (me[2] ^ py) * 2 + (me[3] ^ pc)
            ref[py] = full[:, pl.ds(pl.multiple_of(at * slab, slab), slab)]


def finish_in(me_ref, len_ref, h_ref, own0, own1, recv_ref, stay_ref, leave_ref, full):
    own = jnp.where(me_ref[3] == 0, own0[...].astype(F32), own1[...].astype(F32))
    total = h_ref[...] + (own + recv_ref[...].astype(F32))
    tokens = total.shape[0]
    at = lax.broadcasted_iota(jnp.int32, total.shape, 0) + me_ref[3] * tokens
    total = jnp.where(at < len_ref[0], total, 0.0)
    scatter_lanes(me_ref, total.astype(BF16), full, stay_ref, leave_ref)


def finish(me, length, hidden, own, recv, slab):
    half, width = recv.shape
    part = pl.BlockSpec((2, half, slab), lambda i, m, n: (0, 0, 0))
    mine = pl.BlockSpec((half, width), lambda i, m, n: (m[3], 0))
    row = pl.BlockSpec((half, width), lambda i, m, n: (0, 0))
    shape = jax.ShapeDtypeStruct((2, half, slab), BF16)
    return pl.pallas_call(
        finish_in,
        out_shape=(shape, shape),
        grid_spec=pltpu.PrefetchScalarGridSpec(
            num_scalar_prefetch=2,
            grid=(1,),
            in_specs=[mine, row, row, row],
            out_specs=(part, part),
            scratch_shapes=[pltpu.VMEM((half, width), BF16)],
        ),
        compiler_params=params(40),
        cost_estimate=work(3),
        name="finish",
    )(me, length, hidden, *own, recv)


def norm_second_back_in(
    h_ref, own0, own1, recv0, recv1, gm_ref, gain_ref, gh_ref, gb_ref
):
    hidden = h_ref[...]
    width = hidden.shape[1]
    rstd = lax.rsqrt(jnp.mean(hidden * hidden, axis=1, keepdims=True) + EPSILON)
    grad = of_halves(own0, own1) + of_halves(recv0, recv1)
    weighted = grad * gain_ref[...].astype(F32)
    stat = jnp.sum(weighted * hidden, axis=1, keepdims=True)
    grad_h = (
        gm_ref[...].astype(F32)
        + rstd * weighted
        - hidden * (rstd * rstd * rstd * stat / width)
    )
    gh_ref[...] = grad_h
    gb_ref[...] = grad_h.astype(BF16)


def norm_second_back(hidden, own, recv, grad_mixed, gain):
    tokens, width = hidden.shape
    row = pl.BlockSpec((tokens // 4, width), lambda i: (i, 0))
    one = pl.BlockSpec((1, width), lambda i: (0, 0))
    pair = halves(tokens // 4, width)
    return pl.pallas_call(
        norm_second_back_in,
        out_shape=(
            jax.ShapeDtypeStruct((tokens, width), F32),
            jax.ShapeDtypeStruct((tokens, width), BF16),
        ),
        grid=(4,),
        in_specs=[row, *pair, *pair, row, one],
        out_specs=(row, row),
        compiler_params=params(40),
        cost_estimate=work(5),
        name="norm_second_back",
    )(hidden, *own, *recv, grad_mixed, gain)


def out_back_in(plan, back_plan, me_ref, gb_hbm, a_hbm, *refs):
    count = len(plan)
    weights, ga_hbm, outs = refs[:count], refs[count], refs[count + 1 : count + 3]
    gb_ref, a_ref, ga_ref, w_scr, staged, load_sems, sems, out_sems = refs[count + 3 :]
    n = w_scr.shape[2]
    first = weights[0].shape[2] - n
    (fetch,) = fetch_copies(me_ref, plan, weights, [(first, n)], by_half(w_scr), sems)
    (emit,) = emit_copies(me_ref, back_plan, outs, [(0, n)], by_half(staged), out_sems)
    load_gb = [pltpu.make_async_copy(gb_hbm, gb_ref, load_sems.at[0])]
    load_a = [pltpu.make_async_copy(a_hbm, a_ref, load_sems.at[1])]
    keep = [pltpu.make_async_copy(ga_ref, ga_hbm, load_sems.at[2])]
    for copies in (load_gb, fetch, load_a):
        start(copies)
    wait(load_gb + fetch)
    for half in range(2):
        ga_ref[:, half * n : (half + 1) * n] = mm(gb_ref[...], w_scr[half], NN).astype(BF16)
    start(keep)
    wait(load_a)
    for half in range(2):
        cut = slice(half * n, (half + 1) * n)
        staged[half] = mm(gb_ref[...], a_ref[:, cut], TN).astype(BF16)
    start(emit)
    wait(keep + emit)


def out_back(me, grad_branch, attended, weights):
    tokens, width = grad_branch.shape
    heads_wide = attended.shape[1]
    half_zs, rows, _ = weights[0].shape
    zs = 2 * half_zs
    n = heads_wide // 2
    piece = jax.ShapeDtypeStruct((2 * zs, rows, n), BF16)
    return pl.pallas_call(
        functools.partial(out_back_in, plan_planes(zs), plan_back_lines(zs)),
        out_shape=(jax.ShapeDtypeStruct((tokens, heads_wide), BF16),) + (piece,) * 2,
        in_specs=[SCALARS, ANY, ANY] + [ANY] * len(weights),
        out_specs=(ANY,) * 3,
        scratch_shapes=[
            pltpu.VMEM((tokens, width), BF16),
            pltpu.VMEM((tokens, heads_wide), BF16),
            pltpu.VMEM((tokens, heads_wide), BF16),
            pltpu.VMEM((2, width, n), BF16),
            pltpu.VMEM((2, width, n), BF16),
            pltpu.SemaphoreType.DMA((3,)),
            copy_sems(zs, 1),
            copy_sems(zs, 1),
        ],
        compiler_params=vmem(40),
        cost_estimate=work(5),
        name="out_back",
    )(me, grad_branch, attended, *weights)


def attend_back_in(len_ref, q_ref, k_ref, v_ref, g_ref, lse_ref, gq_ref, gk_ref, gv_ref, *scratch):
    gk_acc, gv_acc = scratch
    tokens = q_ref.shape[0]
    rows = tokens // 4
    scale = HEAD_DIM ** (-0.5)
    length = len_ref[0]
    keys_t = k_ref[...].T
    gk_acc[...] = jnp.zeros_like(gk_acc)
    gv_acc[...] = jnp.zeros_like(gv_acc)
    for at in range(4):
        first, last = at * rows, (at + 1) * rows
        queries = stack_heads(q_ref[first:last] * jnp.asarray(scale, BF16))
        grads = stack_heads(g_ref[first:last])
        scores = masked_scores(length, k_ref[:last], queries, first)
        probs = jnp.exp(scores - lse_ref[0, at : at + 1])
        grad_probs = mm(v_ref[:last], grads, NT)
        inner = jnp.sum(probs * grad_probs, axis=0, keepdims=True)
        grad_scores = (probs * (grad_probs - inner)).astype(BF16)
        both = mm(keys_t[:, :last], grad_scores, NN)
        joined = jnp.concatenate([both[:HEAD_DIM, :rows], both[HEAD_DIM:, rows:]], axis=0)
        gq_ref[first:last] = (joined.T * scale).astype(BF16)
        gk_acc[:last] += mm(grad_scores, queries, NN)
        gv_acc[:last] += mm(probs.astype(BF16), grads, NN)
    gk_ref[...] = gk_acc[...].astype(BF16)
    gv_ref[...] = gv_acc[...].astype(BF16)


def attend_back(length, qkv, grad_attended, lse, half):
    tokens = qkv.shape[0]
    per = lse.shape[0] // 2

    def spec(which):
        return pl.BlockSpec((tokens, PAIR), lambda i: (0, half * 3 * per + which * per + i))

    out = pl.BlockSpec((tokens, PAIR), lambda i: (0, i))
    shape = jax.ShapeDtypeStruct((tokens, per * PAIR), BF16)
    return pl.pallas_call(
        attend_back_in,
        out_shape=(shape, shape, shape),
        grid=(per,),
        in_specs=[
            SCALARS,
            spec(0),
            spec(1),
            spec(2),
            pl.BlockSpec((tokens, PAIR), lambda i: (0, half * per + i)),
            pl.BlockSpec((1, 4, tokens // 2), lambda i: (half * per + i, 0, 0)),
        ],
        out_specs=(out, out, out),
        scratch_shapes=[pltpu.VMEM((tokens, PAIR), F32), pltpu.VMEM((tokens, PAIR), F32)],
        compiler_params=params(56),
        cost_estimate=work(11),
        name="attend_back",
    )(length, qkv, qkv, qkv, grad_attended, lse)


def weight_back_in(back_plan, me_ref, gq, gk, gv, n_hbm, *refs):
    count = len(back_plan)
    outs, (grad, n_ref, staged, load_sems, out_sems) = refs[:count], refs[count:]
    columns = staged.shape[1]
    n = columns // 3
    loads = [
        pltpu.make_async_copy(ref, grad.at[:, pl.ds(at * n, n)], load_sems.at[at])
        for at, ref in enumerate((gq, gk, gv))
    ] + [pltpu.make_async_copy(n_hbm, n_ref, load_sems.at[3])]
    (emit,) = emit_copies(
        me_ref, back_plan, outs, [(0, columns)], lambda at, half, rows: staged.at[rows, :], out_sems
    )
    start(loads)
    wait(loads)
    staged[...] = mm(n_ref[...], grad[...], TN).astype(BF16)
    start(emit)
    wait(emit)


def weight_back(me, grads, normed, zs, half):
    tokens, width = normed.shape
    columns = 3 * grads[0].shape[1]
    back_plan = [p for p in plan_back_planes(zs) if p[0][0] == half]
    if half == 0:
        back_plan = back_plan[:1] + [back_plan[1][: zs // 2], back_plan[1][zs // 2 :]]
    pieces = tuple(
        jax.ShapeDtypeStruct((len(p), width // (2 * zs), columns), BF16) for p in back_plan
    )
    return pl.pallas_call(
        functools.partial(weight_back_in, back_plan),
        out_shape=pieces,
        in_specs=[SCALARS] + [ANY] * 4,
        out_specs=(ANY,) * len(pieces),
        scratch_shapes=[
            pltpu.VMEM((tokens, columns), BF16),
            pltpu.VMEM((tokens, width), BF16),
            pltpu.VMEM((width, columns), BF16),
            pltpu.SemaphoreType.DMA((4,)),
            copy_sems(zs, 1),
        ],
        compiler_params=vmem(40),
        cost_estimate=work(4),
        name="weight_back",
    )(me, *grads, normed)


def qkv_back_in(plan, me_ref, *refs):
    grads, weights, outs = refs[:6], refs[6 : 6 + len(plan)], refs[6 + len(plan) : 8 + len(plan)]
    grad, w_scr, staged, load_sems, sems, out_sems = refs[8 + len(plan) :]
    columns = w_scr.shape[2]
    n = columns // 3
    loads = [
        pltpu.make_async_copy(
            ref, grad.at[at // 3, :, pl.ds(at % 3 * n, n)], load_sems.at[at]
        )
        for at, ref in enumerate(grads)
    ]
    (fetch,) = fetch_copies(me_ref, plan, weights, [(0, columns)], by_half(w_scr), sems)
    copies = [fetch[: len(fetch) // 2] + loads[:3], fetch[len(fetch) // 2 :] + loads[3:]]
    start(copies[0])
    start(copies[1])
    half = staged.shape[1]
    wait(copies[0])
    first = mm(grad[0], w_scr[0], NT)
    wait(copies[1])
    staged[0] = (first[:half] + mm(grad[1, :half], w_scr[1], NT)).astype(BF16)
    staged[1] = (first[half:] + mm(grad[1, half:], w_scr[1], NT)).astype(BF16)
    emit = [
        pltpu.make_async_copy(staged.at[me_ref[3]], outs[0], out_sems.at[0]),
        pltpu.make_async_copy(staged.at[1 - me_ref[3]], outs[1], out_sems.at[1]),
    ]
    start(emit)
    wait(emit)


def qkv_back(me, grads, weights, columns):
    tokens, n = grads[0].shape
    half_zs, rows, _ = weights[0].shape
    zs = 2 * half_zs
    width = zs * 2 * rows
    plan = plan_planes(zs)
    shape = jax.ShapeDtypeStruct((tokens // 2, width), BF16)
    return pl.pallas_call(
        functools.partial(qkv_back_in, plan),
        out_shape=(shape, shape),
        in_specs=[SCALARS] + [ANY] * (6 + len(plan)),
        out_specs=(ANY, ANY),
        scratch_shapes=[
            pltpu.VMEM((2, tokens, columns), BF16),
            pltpu.VMEM((2, width, columns), BF16),
            pltpu.VMEM((2, tokens // 2, width), BF16),
            pltpu.SemaphoreType.DMA((6,)),
            copy_sems(zs, 1),
            pltpu.SemaphoreType.DMA((2,)),
        ],
        compiler_params=vmem(48),
        cost_estimate=work(6),
        name="qkv_back",
    )(me, *grads, *weights)


def norm_first_back_in(
    me_ref, x_ref, own_ref, recv_ref, gh_ref, gain_ref, stay_ref, leave_ref, full
):
    x = x_ref[...].astype(F32)
    width = x.shape[1]
    rstd = lax.rsqrt(jnp.mean(x * x, axis=1, keepdims=True) + EPSILON)
    grad = own_ref[...].astype(F32) + recv_ref[...].astype(F32)
    weighted = grad * gain_ref[...].astype(F32)
    stat = jnp.sum(weighted * x, axis=1, keepdims=True)
    gx = gh_ref[...] + rstd * weighted - x * (rstd * rstd * rstd * stat / width)
    scatter_lanes(me_ref, gx.astype(BF16), full, stay_ref, leave_ref)


def norm_first_back(me, x, own, recv, grad_h, gain, slab):
    half, width = own.shape
    part = pl.BlockSpec((2, half, slab), lambda i, m: (0, 0, 0))
    mine = pl.BlockSpec((half, width), lambda i, m: (m[3], 0))
    row = pl.BlockSpec((half, width), lambda i, m: (0, 0))
    one = pl.BlockSpec((1, width), lambda i, m: (0, 0))
    shape = jax.ShapeDtypeStruct((2, half, slab), BF16)
    return pl.pallas_call(
        norm_first_back_in,
        out_shape=(shape, shape),
        grid_spec=pltpu.PrefetchScalarGridSpec(
            num_scalar_prefetch=1,
            grid=(1,),
            in_specs=[mine, row, row, mine, one],
            out_specs=(part, part),
            scratch_shapes=[pltpu.VMEM((half, width), BF16)],
        ),
        compiler_params=params(40),
        cost_estimate=work(4),
        name="norm_first_back",
    )(me, x, own, recv, grad_h, gain)


def shards(
    patches,
    w_query,
    w_key,
    w_value,
    w_out,
    w_gate,
    w_up,
    w_down,
    gain_attn,
    gain_mlp,
    lengths,
    cotangent,
):
    slab = patches.shape[1]
    rows_axis, cols_axis = lax.axis_size("row"), lax.axis_size("col")
    width = slab * cols_axis
    micro = lengths.shape[0]
    seq = patches.shape[0] // micro
    zs = rows_axis // 2
    row, col = lax.axis_index("row"), lax.axis_index("col")
    z, x, y, c = row // 2, row % 2, col // 2, col % 2
    me = jnp.stack([z, x, y, c]).astype(jnp.int32)
    heads_here = w_query.shape[1]
    columns = 3 * heads_here

    def swap(value, axis, bit):
        size = lax.axis_size(axis)
        return lax.ppermute(value, axis, [(i, i ^ bit) for i in range(size)])

    sent = {"x": [], "y": [], "z": [], "c": []}
    depth = {"x": 2, "y": 2, "z": 2, "c": 2}
    bits = {"x": ("row", 1), "y": ("col", 2), "c": ("col", 1)}

    def send(value, link, bit=None):
        axis, one = bits.get(link, ("row", bit))
        queue = sent[link]
        if len(queue) >= depth[link]:
            value = lax.optimization_barrier((value, queue[-depth[link]]))[0]
        out = swap(value, axis, one)
        queue.append(out)
        return out

    def gather_z(shard, *done):
        near, bit = shard[None], zs // 2
        while bit > 1:
            near = jnp.concatenate([near, tie(send(near, "z", 2 * bit), *done)])
            bit //= 2
        return near, send(near, "z", 2)

    def tie(value, *done):
        return lax.optimization_barrier((value, *done))[0]

    def order_rows(both):
        owned = [0]
        for bit in [1] + [2 * (zs >> k) for k in range(1, zs.bit_length())]:
            owned += [at ^ bit for at in owned]
        ordered = [jnp.zeros_like(both[0])] * rows_axis
        for at, rel in enumerate(owned):
            ordered = [jnp.where((row ^ rel) == k, both[at], o) for k, o in enumerate(ordered)]
        return jnp.concatenate(ordered, axis=1)

    def add(*values):
        total = values[0].astype(F32)
        for value in values[1:]:
            total = total + value.astype(F32)
        return total

    def leave_z(pieces):
        return add(*(p[zs // 2 :] for p in pieces)).astype(BF16)

    def keep_z(pieces, come):
        return add(*(p[: zs // 2] for p in pieces), come)

    def next_z(total, bit=4):
        count = total.shape[0] // 2
        if not count:
            return total, None, bit
        return total[:count], send(total[count:].astype(BF16), "z", bit), bit

    def last_z(total, come, bit):
        while come is not None:
            total, come, bit = next_z(add(total, come), 2 * bit)
        return total[0]

    def out_x(total):
        count, bit = zs // 4, 8
        while count > 1:
            count //= 2
            come = swap(total[4 * count :].astype(BF16), "row", bit)
            total, bit = add(total[: 4 * count], come), bit * 2
        return total[:2], swap(total[2:].astype(BF16), "row", 1)

    def tie_all(values, *done):
        return lax.optimization_barrier((tuple(values), done))[0]

    def pick(flag, one, other):
        return jnp.where(flag == 0, one, other)

    def split_micro(value):
        both = value.reshape(micro, seq, slab)
        mine = lax.dynamic_index_in_dim(both, y, 0, keepdims=False)
        return mine, lax.dynamic_index_in_dim(both, 1 - y, 0, keepdims=False)

    def spread(mine, theirs):
        theirs = send(theirs, "y")
        pair = jnp.stack([mine, theirs])
        other = send(pair, "c")
        blocks = [
            pick(
                y ^ yy,
                pick(c ^ cc, pair[0], other[0]),
                pick(c ^ cc, pair[1], other[1]),
            )
            for yy in range(2)
            for cc in range(2)
        ]
        return jnp.concatenate(blocks, axis=1), theirs

    def unspread_start(stay, leave):
        come = swap(leave, "col", 1)
        return stay, come, jnp.stack([stay[1], come[1]])

    def unspread_finish(stay, come, got):
        return jnp.concatenate(
            [
                pick(
                    y ^ at,
                    pick(c ^ side, stay[0], come[0]),
                    pick(c ^ side, got[0], got[1]),
                )
                for at in range(2)
                for side in range(2)
            ],
            axis=0,
        )

    inner = w_gate.shape[1]
    padded = -(-inner // 256) * 256
    chunk = padded // 2
    pad = ((0, 0), (0, padded - inner))
    attn_shard = jnp.concatenate([w_query, w_key, w_value, w_out.T], axis=1)
    gate_up_down = [jnp.pad(w_gate, pad), jnp.pad(w_up, pad), jnp.pad(w_down.T, pad)]
    mlp_shards = [
        jnp.concatenate([w[:, at * chunk : (at + 1) * chunk] for w in gate_up_down], axis=1)
        for at in range(2)
    ]
    gain_parts = jnp.stack([gain_attn, gain_mlp])[None]
    gain_parts = jnp.concatenate([gain_parts, swap(gain_parts, "row", 1)])
    patches_mine, patches_other = split_micro(patches)
    bit = zs // 2
    while bit:
        gain_parts = jnp.concatenate([gain_parts, swap(gain_parts, "row", 2 * bit)])
        bit //= 2
    near, bit = tie(attn_shard, patches_other, gain_parts)[None], zs // 2
    while bit > 1:
        near = jnp.concatenate([near, send(near, "z", 2 * bit)])
        bit //= 2
    a0, a1 = near, send(near, "z", 2)
    gains = order_rows(gain_parts)
    attn_gain, mlp_gain = gains[0:1], gains[1:2]
    x_all, x_half = spread(patches_mine, patches_other)
    cotangent_all, cotangent_half = spread(*split_micro(cotangent))
    b0, c0 = send(a0, "x"), send(a0, "y")
    b1, c1 = send(tie(a1, b0), "x"), send(tie(a1, c0), "y")
    d0, d1 = send(tie(c0, b1), "x"), send(b1, "y")
    attn_w = (a0, a1, b0, b1, c0, c1, d0, d1)
    e0, e1 = gather_z(tie(mlp_shards[0], a1), b1)
    one_near = jnp.concatenate([e0, e1])
    two_near = jnp.concatenate(gather_z(tie(mlp_shards[1], e1)))
    f, g = swap(tie(one_near, d0), "row", 1), swap(tie(one_near, d1), "col", 2)

    length = lax.dynamic_slice_in_dim(lengths, y, 1)
    grad_mixed = jnp.where(
        lax.iota(jnp.int32, seq)[:, None] < length, cotangent_all, jnp.zeros((), BF16)
    )

    back_plan = plan_back_planes(zs)
    plans = (plan_wholes(zs),) * 2
    normed_one = norm_first(x_all, attn_gain)
    qkv = project_qkv(me, tie(normed_one, one_near), attn_w, columns)
    attended, lse = attend(length, qkv, 2 * heads_here // HEAD_DIM)
    g_lo, f_hi = tie_all((g[: zs // 2], f[zs // 2 :]), attended)
    one_w = (one_near, f, g, swap(g_lo, "row", 1), swap(f_hi, "col", 2))
    branch = project_out(me, tie(attended, g_lo, f_hi), attn_w)
    f, g = swap(tie(two_near, one_w[3]), "row", 1), swap(tie(two_near, one_w[4]), "col", 2)
    hidden, normed_two = norm_second(
        x_all, branch, [send(tie(v, *one_w[3:], two_near, grad_mixed), "c") for v in branch], mlp_gain
    )

    act_one, *grad_one = mlp(
        me, normed_two, grad_mixed, one_w, zs, plans[0], back_plan
    )
    g00, g01, g10, g11 = grad_one
    f, g = tie_all((f, g), act_one)
    two_w = (two_near, f, g, swap(g[: zs // 2], "row", 1), swap(f[zs // 2 :], "col", 2))
    far_one = send(g11, "x")
    act_two, *grad_two = mlp(
        me, tie(normed_two, act_one), grad_mixed, two_w, zs, plans[1], back_plan
    )
    h00, h01, h10, h11 = grad_two
    far_two = send(h11, "y")
    side_one = send(tie(g01, act_two), "x")
    weights = (one_w, two_w)
    acts = (act_one, act_two)
    back_two = contract(me, acts, weights, zs, plans, (0, 1), "mlp_back", 9)
    back_recv = [send(v, "c") for v in back_two]
    over_one = add(*tie_all((g10, far_one), back_two[0])).astype(BF16)
    acts = (act_one, tie(act_two, over_one))
    mixed = contract(me, acts, weights, zs, plans, (2,), "mlp_out", 6)
    over_one = send(over_one, "y")
    grad_h, grad_branch = norm_second_back(
        tie(hidden, mixed[0]), back_two, back_recv, grad_mixed, mlp_gain
    )
    mixed_recv = send(tie(pick(c, mixed[1], mixed[0]), grad_branch), "c")
    side_two = send(h10, "y")
    over_two = add(*tie_all((h01, far_two), grad_branch)).astype(BF16)

    grad_attended, o0, o1 = out_back(me, tie(grad_branch, over_two), attended, attn_w)
    over_two = send(over_two, "x")
    finished = finish(me, length, tie(hidden, grad_attended), mixed, mixed_recv, slab)
    leave_out = send(o1, "z", 2)
    grads = attend_back(length, qkv, tie(grad_attended, finished[0]), lse, 1)
    first_one = leave_z(tie_all((g00, side_one, over_one), grads[0]))
    finished = tie_all(finished, grads[0])
    output_sent = unspread_start(*finished)
    other_grads = grads
    p10, p11 = weight_back(
        me, (tie(grads[0], first_one, leave_out), *grads[1:]), normed_one, zs, 1
    )
    far_qkv = send(p11, "x")
    first_one = send(first_one, "z", 2)
    out_sum = add(*tie_all((o0, leave_out), p10))
    keep_out, leave_out = out_sum[:zs], out_sum[zs:].astype(BF16)
    pieces = tie_all((h00, side_two, over_two), p10)
    leave_two = leave_z(pieces)
    grads = attend_back(
        length, qkv, tie(grad_attended, p10, leave_out, leave_two, output_sent[2]), lse, 0
    )
    output_sent = (*output_sent[:2], swap(output_sent[2], "col", 2))
    out_come = swap(leave_out, "row", 4)
    two_come = swap(leave_two, "row", 2)
    sum_one = next_z(keep_z((g00, side_one, over_one), tie(first_one, grads[0])))
    count = zs // 2
    p10, far_qkv = tie_all((p10, far_qkv), grads[0], output_sent[2])
    over_hi = add(p10[count:], far_qkv[count:]).astype(BF16)
    over_lo = add(p10[:count], far_qkv[:count]).astype(BF16)
    out_sum = add(keep_out, tie(out_come, grads[0], output_sent[2]))
    sum_two = keep_z(pieces, tie(two_come, grads[0]))
    out_sum, out_come = out_x(out_sum)
    p00, side_lo, side_hi = weight_back(
        me, (tie(grads[0], over_hi, over_lo, sum_two), *grads[1:]),
        normed_one, zs, 0
    )
    over_hi = swap(over_hi, "col", 2)
    over_lo = swap(tie(over_lo, p00), "col", 2)
    side_hi, side_lo = swap(side_hi, "row", 1), swap(side_lo, "row", 1)
    sum_two = next_z(sum_two)
    out_sum = add(out_sum, tie(out_come, p00))
    back_own, back_other = qkv_back(
        me, (tie(grads[0], p00, out_sum), *grads[1:], *other_grads), attn_w, columns
    )
    out_come = swap(out_sum[1].astype(BF16), "col", 2)
    grad_x = norm_first_back(
        me, tie(x_all, over_hi, side_hi), back_own, send(back_other, "c"), grad_h, attn_gain, slab
    )
    patches_sent = unspread_start(*grad_x)
    patches_sent = (*patches_sent[:2], swap(patches_sent[2], "col", 2))
    leave_qkv = add(p00[count:], over_hi, side_hi).astype(BF16)
    come_qkv = swap(leave_qkv, "row", 2)

    out_grad = add(out_sum[0], tie(out_come, come_qkv))
    output = unspread_finish(*tie_all(output_sent, leave_qkv))
    sum_one = last_z(sum_one[0], tie(sum_one[1], leave_qkv), sum_one[2])
    sum_two = last_z(sum_two[0], tie(sum_two[1], leave_qkv), sum_two[2])
    qkv_sum, qkv_come, bit = next_z(add(p00[:count], over_lo, side_lo, tie(come_qkv, grad_x[0])))
    qkv_grad = last_z(qkv_sum, tie(qkv_come, patches_sent[2]), bit)
    sum_one, sum_two = tie_all((sum_one, sum_two), qkv_sum)
    grad_patches = unspread_finish(*patches_sent).astype(F32)
    mlp_sums = [
        jnp.concatenate([v[:, at * chunk : (at + 1) * chunk] for v in (sum_one, sum_two)], axis=1)[
            :, :inner
        ]
        for at in range(3)
    ]

    def weighed(weights, grads):
        return sum(jnp.sum(w.astype(F32) * g, axis=1) for w, g in zip(weights, grads, strict=True))

    gain_grads = jnp.stack(
        [
            weighed(
                (w_query, w_key, w_value),
                [qkv_grad[:, at * heads_here : (at + 1) * heads_here] for at in range(3)],
            ),
            weighed((w_gate, w_up), mlp_sums[:2]),
        ]
    )
    others = [swap(gain_grads, "col", bit) for bit in (2, 1, 3)]
    gain_grads = (gain_grads + others[0]) + (others[1] + others[2])
    gain_grads = gain_grads / jnp.stack([gain_attn, gain_mlp]).astype(F32)

    return (
        output,
        grad_patches,
        qkv_grad[:, :heads_here],
        qkv_grad[:, heads_here : 2 * heads_here],
        qkv_grad[:, 2 * heads_here :],
        out_grad.T,
        mlp_sums[0],
        mlp_sums[1],
        mlp_sums[2].T,
        gain_grads[0],
        gain_grads[1],
    )


def solution(mesh):
    placed = (
        P("row", "col"),
        P("row", "col"),
        P("row", "col"),
        P("row", "col"),
        P("col", "row"),
        P("row", "col"),
        P("row", "col"),
        P("col", "row"),
        P("row"),
        P("row"),
        P("row"),
        P("row", "col"),
    )
    return jax.shard_map(
        shards,
        mesh=mesh,
        in_specs=placed,
        out_specs=(
            P("row", "col"),
            P("row", "col"),
            P("row", "col"),
            P("row", "col"),
            P("row", "col"),
            P("col", "row"),
            P("row", "col"),
            P("row", "col"),
            P("col", "row"),
            P("row"),
            P("row"),
        ),
        check_vma=False,
    )
```
